32 devices in a mesh: fsdp: 4 (over z), ctx: 2 (over y), tp: 4 (over x, core).
Axes of the slice: x: 2, y: 2, z: 4, core: 2. Of those that a mesh axis runs over, the one named last changes fastest.
Arguments:
- tokens: bfloat16 [4, 768, 1024], P('fsdp', 'ctx'), may hold values from -16 to 16
- cotangent: bfloat16 [4, 768, 1024], P('fsdp', 'ctx'), may hold values from -6 to 6
- positions: int32 [4, 768], P('fsdp', 'ctx'), may hold values from 0 to 767, as said below
- routes: int32 [4, 768, 8], P('fsdp', 'ctx'), may hold values from 0 to 31, all different within a row; in each aligned block of 384 rows (0 to 383, 384 to 767, ..., all dimensions but the last counted through in order) at most 192 rows name the same one
- attn_gain: bfloat16 [1024], P('fsdp'), may hold values from 0.5 to 1.5
- w_query: bfloat16 [1024, 1024], P('fsdp', 'tp'), may hold values from -0.1875 to 0.1875
- key_value_projection: bfloat16 [1024, 8, 2, 64], P('fsdp', 'tp'), may hold values from -0.1875 to 0.1875
- output_projection_weight: bfloat16 [1024, 1024], P('tp', 'fsdp'), may hold values from -0.75 to 0.75
- ffn_gain: bfloat16 [1024], P('fsdp'), may hold values from 0.5 to 1.5
- w_router: bfloat16 [1024, 32], P('fsdp'), may hold values from -0.1875 to 0.1875
- w_gate: bfloat16 [32, 1024, 512], P('tp', 'fsdp'), may hold values from -0.1875 to 0.1875
- w_up: bfloat16 [32, 1024, 512], P('tp', 'fsdp'), may hold values from -0.1875 to 0.1875
- w_down: bfloat16 [32, 1024, 512], P('tp', 'fsdp'), may hold values from -0.75 to 0.75
Outputs:
- out: bfloat16 [4, 768, 1024], P('fsdp', 'ctx')
- d_tokens: float32 [4, 768, 1024], P('fsdp', 'ctx')
- d_attn_gain: float32 [1024], P('fsdp')
- d_query: float32 [1024, 1024], P('fsdp', 'tp')
- d_keyval: float32 [1024, 8, 2, 64], P('fsdp', 'tp')
- d_out: float32 [1024, 1024], P('tp', 'fsdp')
- d_ffn_gain: float32 [1024], P('fsdp')
- d_router: float32 [1024, 32], P('fsdp')
- d_gate: float32 [32, 1024, 512], P('tp', 'fsdp')
- d_up: float32 [32, 1024, 512], P('tp', 'fsdp')
- d_down: float32 [32, 1024, 512], P('tp', 'fsdp')
The draws below stay inside these ranges and needn't reach their ends.
Inputs may be any that keep to these rules, and one draw needn't show every extreme that they name: positions[s, i] is 0 at the first token of a document and one more than positions[s, i - 1] otherwise; every sequence begins a document at its first token; the first sequence is one whole document. `routes`: each row names 8 different experts; in the rows of one device (aligned blocks of 384 rows) no expert is named by more than 192 rows, a bound that some block reaches.
All inputs are finite; a program needn't handle non-finite values.
Results may differ from the reference program's by a relative error of at most 0.02.
Values may be sent and summed in bfloat16 or wider, within the bound.
No kernel may reach another device: no remote copies, remote signals or barrier semaphores. Data moves between devices by JAX's collectives and lax.ppermute only.
A program may use at most 192 MiB of HBM per device.

```python
import math
import jax
import jax.numpy as jnp
import numpy as np
from jax import lax

MODEL_DIM = 1024
QUERY_HEADS = 16
KEY_VALUE_HEADS = 8
HEAD_SIZE = 64
EXPERTS = 32
FF = 512
TOPK = 8
SEQ_LEN = 768
SEQS = 4
TOK_DEV = 384
CAP = 192
N_CTX = 2


def draw_tokens(key, part):
    row_key = jax.random.fold_in(key, 11)
    column_key = jax.random.fold_in(key, 12)
    value_key = jax.random.fold_in(key, 13)
    row_scale = jnp.exp(jax.random.uniform(row_key, (SEQS, SEQ_LEN, 1), jnp.float32, math.log(0.3), math.log(3.0)))
    column_scale = jnp.exp(jax.random.uniform(column_key, (1, 1, MODEL_DIM), jnp.float32, math.log(0.5), math.log(2.0)))
    base_values = jax.random.normal(value_key, (SEQS, SEQ_LEN, MODEL_DIM), jnp.float32)
    return jnp.clip(base_values * row_scale * column_scale, -16.0, 16.0).astype(jnp.bfloat16)


def draw_positions(key, part):
    doc_marks = jax.random.randint(jax.random.fold_in(key, 21), (SEQS, SEQ_LEN), 0, SEQ_LEN // 2) == 0
    doc_marks = doc_marks.at[0, :].set(False)
    doc_marks = doc_marks.at[:, 0].set(True)
    place_ids = jnp.arange(SEQ_LEN, dtype=jnp.int32)
    latest = lax.cummax(jnp.where(doc_marks, place_ids[None, :], 0), axis=1)
    return (place_ids[None, :] - latest).astype(jnp.int32)


def block_scale(rng, shape, pieces, smallest, top_value):
    factor_of = 1.0
    for dim, blocks in pieces:
        draws = jax.random.uniform(jax.random.fold_in(jax.random.fold_in(rng, 6), dim), (blocks,), jnp.float32, smallest / len(pieces), top_value / len(pieces))
        factor_of = factor_of * jnp.repeat(jnp.exp(draws), shape[dim] // blocks).reshape((-1,) + (1,) * (len(shape) - 1 - dim))
    return factor_of


def deal_out(own_key, own, number, rows, number_of, top, most, slope):
    order = jax.random.permutation(own_key, number_of)
    crowded, ordinary = portions_of(number_of, rows * top, most, slope, True), portions_of(number_of, rows * top, most, slope, False)
    places = jnp.arange(number_of)

    def named(lengths, turn):
        used = int((lengths > 0).sum())
        fixed = max(1, used // 4)
        moved = fixed + (places - fixed + turn * (used - fixed)) % max(1, number_of - fixed)
        return jnp.zeros((number_of,), jnp.int32).at[order[jnp.where(places < fixed, places, moved)]].set(jnp.asarray(lengths, jnp.int32))

    lengths = jnp.where(number % 4 == 0, named(crowded, number // 4), named(ordinary, number - number // 4 - 1))
    mixed = jax.random.permutation(jax.random.fold_in(own, 3), number_of)
    giver, sink = mixed[0:number_of // 2 * 2:2], mixed[1:number_of // 2 * 2:2]
    slack = jnp.minimum(lengths[giver] - 1, most - lengths[sink]) // 2
    slack = jnp.where((giver == order[0]) | (sink == order[0]) | (lengths[sink] == 0), 0, jnp.maximum(slack, 0))
    moved = jax.random.randint(jax.random.fold_in(own, 4), (number_of // 2,), 0, 1 << 20) % (slack + 1)
    lengths = lengths.at[giver].add(-moved).at[sink].add(moved)
    labels = jnp.searchsorted(jnp.cumsum(lengths), jnp.arange(rows * top), side="right").astype(jnp.int32)
    table = labels.reshape(top, rows).T
    table = table[jax.random.permutation(jax.random.fold_in(own, 1), rows)]
    turn = jax.random.randint(jax.random.fold_in(own, 2), (rows, 1), 0, top)
    return jnp.take_along_axis(table, (jnp.arange(top)[None, :] + turn) % top, axis=1)


def portions_of(amount, total, most, lean, full):
    portions = [(1 << 20) // math.isqrt(rank ** lean) + 1 for rank in range(1, amount + 1)]
    largest = most if full else min(most, max(-(-total // amount), total * portions[0] // sum(portions)))
    least = 1 if total - largest >= amount - 1 else 0
    counts, spare = [largest] + [least] * (amount - 1), total - largest - least * (amount - 1)
    while spare > 0:
        candidates = [i for i in range(1, amount) if counts[i] < largest] or [i for i in range(1, amount) if counts[i] < most]
        whole, budget = sum([portions[i] for i in candidates]), spare
        for i in candidates:
            extra = min(most - counts[i], max(1, budget * portions[i] // whole), spare)
            counts[i] = counts[i] + extra
            spare = spare - extra
    return np.array(counts)


def gaussian(key, extent, width, limit, split=(), kind=jnp.bfloat16):
    array = jax.random.normal(key, extent, jnp.float32) * width
    if len(split) > 0:
        array = block_scale(key, extent, split, -0.22, 0.18) * array
    return jnp.clip(array, min=-limit, max=limit).astype(kind)


def setup_inputs(seed: int = 0) -> dict:
    arg_keys = jax.random.split(jax.random.key(seed), 14)
    tokens = draw_tokens(jax.random.fold_in(arg_keys[13], 71), 0)
    cotangent = gaussian(arg_keys[1], (SEQS, SEQ_LEN, MODEL_DIM), 1.0, 6.0, ((0, 4), (1, 2)))
    positions = draw_positions(jax.random.fold_in(arg_keys[13], 71), 0)
    routes_keys = jax.random.split(jax.random.fold_in(arg_keys[3], 1), SEQS * SEQ_LEN // TOK_DEV)
    routes_turns = jax.random.permutation(jax.random.fold_in(arg_keys[3], 3), SEQS * SEQ_LEN // TOK_DEV)
    routes = jax.vmap(lambda own, number: deal_out(jax.random.fold_in(arg_keys[3], 2), own, number, TOK_DEV, EXPERTS, TOPK, CAP, 1))(routes_keys, routes_turns).reshape((SEQS, SEQ_LEN, TOPK))
    attn_gain = jnp.clip(1.0 + 0.1 * jax.random.normal(arg_keys[4], (MODEL_DIM,), jnp.float32), 0.5, 1.5).astype(jnp.bfloat16)
    w_query = gaussian(arg_keys[5], (MODEL_DIM, QUERY_HEADS * HEAD_SIZE), MODEL_DIM ** -0.5, 0.1875, ((0, 4), (1, 4)))
    key_value_projection = gaussian(arg_keys[6], (MODEL_DIM, KEY_VALUE_HEADS, 2, HEAD_SIZE), MODEL_DIM ** -0.5, 0.1875, ((0, 4), (1, 4)))
    output_projection_weight = gaussian(arg_keys[7], (QUERY_HEADS * HEAD_SIZE, MODEL_DIM), (QUERY_HEADS * HEAD_SIZE // 16) ** -0.5, 0.75, ((0, 4), (1, 4)))
    ffn_gain = jnp.clip(1.0 + 0.1 * jax.random.normal(arg_keys[8], (MODEL_DIM,), jnp.float32), 0.5, 1.5).astype(jnp.bfloat16)
    w_router = gaussian(arg_keys[9], (MODEL_DIM, EXPERTS), MODEL_DIM ** -0.5, 0.1875, ((0, 4),))
    w_gate = gaussian(arg_keys[10], (EXPERTS, MODEL_DIM, FF), MODEL_DIM ** -0.5, 0.1875, ((0, 4), (1, 4)))
    w_up = gaussian(arg_keys[11], (EXPERTS, MODEL_DIM, FF), MODEL_DIM ** -0.5, 0.1875, ((0, 4), (1, 4)))
    w_down = gaussian(arg_keys[12], (EXPERTS, MODEL_DIM, FF), (FF // 8) ** -0.5, 0.75, ((0, 4), (1, 4)))
    return {"tokens": tokens, "cotangent": cotangent, "positions": positions, "routes": routes, "attn_gain": attn_gain, "w_query": w_query, "key_value_projection": key_value_projection, "output_projection_weight": output_projection_weight, "ffn_gain": ffn_gain, "w_router": w_router, "w_gate": w_gate, "w_up": w_up, "w_down": w_down}


EPS = 1e-06
THETA = 10000.0

def narrow_width_rows(values):
    return lax.optimization_barrier(values.astype(jnp.bfloat16))

def rope_tables(place_rows, head_width):
    half_width = head_width // 2
    inverse = THETA ** (-2.0 * jnp.arange(half_width, dtype=jnp.float32) / head_width)
    angle = place_rows.astype(jnp.float32)[:, None] * inverse[None, :]
    return (jnp.cos(angle)[:, None, :], jnp.sin(angle)[:, None, :])

def apply_rotary(vector, cosine_lookup, sine_lookup, direction):
    half_width = vector.shape[-1] // 2
    first_half = vector[..., :half_width]
    second_half = vector[..., half_width:]
    return jnp.concatenate([first_half * cosine_lookup - direction * second_half * sine_lookup, direction * first_half * sine_lookup + second_half * cosine_lookup], axis=-1)

def rms_forward(wide_rows, gain_vector):
    factor = lax.rsqrt(lax.optimization_barrier(jnp.mean(wide_rows * wide_rows, axis=-1, keepdims=True)) + EPS)
    normed = wide_rows * factor
    return (normed, factor, narrow_width_rows(normed * gain_vector.astype(jnp.float32)))

def rms_backward(gradient, normed, factor, gain_vector):
    gain_grad = lax.optimization_barrier(jnp.sum(gradient * normed, axis=0))
    inner_term = gradient * gain_vector.astype(jnp.float32)
    back_term = factor * (inner_term - normed * lax.optimization_barrier(jnp.mean(inner_term * normed, axis=-1, keepdims=True)))
    return (back_term, gain_grad)

def attend_mask(query_ids, query_starts, key_ids):
    return (key_ids[None, :] <= query_ids[:, None]) & (key_ids[None, :] >= query_starts[:, None])

def router_gates(logits, picks):
    selected = lax.optimization_barrier(jnp.sum(jnp.where(picks, logits[:, None, :], 0.0), axis=-1))
    exp_sel = jnp.exp(selected)
    return exp_sel / lax.optimization_barrier(jnp.sum(exp_sel, axis=-1, keepdims=True))

def slot_tables(route_rows, gate_weights, first_expert, expert_count, capacity):
    token_count = route_rows.shape[0]
    owners = first_expert + jnp.arange(expert_count, dtype=jnp.int32)
    hit_mask = route_rows[:, :, None] == owners[None, None, :]
    member = lax.optimization_barrier(jnp.sum(hit_mask.astype(jnp.int32), axis=1)).astype(jnp.int32)
    weight_rows = lax.optimization_barrier(jnp.sum(jnp.where(hit_mask, gate_weights[:, :, None], 0.0), axis=1))
    places = (jnp.cumsum(member, axis=0) - 1).astype(jnp.int32)
    expert_ids = jnp.arange(expert_count, dtype=jnp.int32)
    slot_ids = jnp.where(member > 0, expert_ids[None, :] * capacity + places, expert_count * capacity).astype(jnp.int32)
    flat_slots = slot_ids.reshape(-1)
    token_ids = jnp.broadcast_to(jnp.arange(token_count, dtype=jnp.int32)[:, None], (token_count, expert_count)).reshape(-1)
    source = jnp.zeros((expert_count * capacity + 1,), jnp.int32).at[flat_slots].set(token_ids)[:-1]
    scaled = jnp.zeros((expert_count * capacity + 1,), gate_weights.dtype).at[flat_slots].set(weight_rows.reshape(-1))[:-1]
    return (hit_mask, slot_ids, source, scaled)

def expert_forward(hidden, source, w_gate, w_up, w_down, expert_count, capacity):
    picked = hidden[source].reshape(expert_count, capacity, hidden.shape[1]).astype(jnp.float32)
    gate_pre = jnp.einsum('ecd,edf->ecf', picked, w_gate.astype(jnp.float32))
    up_pre = jnp.einsum('ecd,edf->ecf', picked, w_up.astype(jnp.float32))
    activation = narrow_width_rows(jax.nn.silu(gate_pre) * up_pre)
    result = jnp.einsum('ecf,edf->ecd', activation.astype(jnp.float32), w_down.astype(jnp.float32))
    return (picked, gate_pre, up_pre, activation, result)

def combine(result, source, scaled, token_count):
    model_width = result.shape[-1]
    flat_result = result.reshape(-1, model_width)
    return jnp.zeros((token_count, model_width), jnp.float32).at[source].add(flat_result * scaled[:, None])

def expert_backward(grad_rows, hit_mask, slot_ids, source, scaled, saved, w_gate, w_up, w_down, expert_count, capacity, token_count):
    picked, gate_pre, up_pre, activation, result = saved
    model_width = grad_rows.shape[1]
    slot_grad = lax.optimization_barrier(jnp.sum(grad_rows * result.reshape(expert_count * capacity, model_width), axis=1))
    padded = jnp.concatenate([slot_grad, jnp.zeros((1,), jnp.float32)])
    per_expert = padded[slot_ids]
    gate_grad = lax.optimization_barrier(jnp.sum(jnp.where(hit_mask, per_expert[:, None, :], 0.0), axis=2))
    out_grad = narrow_width_rows(grad_rows * scaled[:, None]).reshape(expert_count, capacity, model_width).astype(jnp.float32)
    grad_down = jnp.einsum('ecd,ecf->edf', out_grad, activation.astype(jnp.float32))
    act_grad = jnp.einsum('ecd,edf->ecf', out_grad, w_down.astype(jnp.float32))
    sigmoid_gate = jax.nn.sigmoid(gate_pre)
    gate_pre_grad = narrow_width_rows(act_grad * up_pre * sigmoid_gate * (1.0 + gate_pre * (1.0 - sigmoid_gate))).astype(jnp.float32)
    up_pre_grad = narrow_width_rows(act_grad * gate_pre * sigmoid_gate).astype(jnp.float32)
    grad_gate = jnp.einsum('ecd,ecf->edf', picked, gate_pre_grad)
    grad_up = jnp.einsum('ecd,ecf->edf', picked, up_pre_grad)
    picked_grad = jnp.einsum('ecf,edf->ecd', gate_pre_grad, w_gate.astype(jnp.float32)) + jnp.einsum('ecf,edf->ecd', up_pre_grad, w_up.astype(jnp.float32))
    hidden_grad = jnp.zeros((token_count, model_width), jnp.float32).at[source].add(picked_grad.reshape(-1, model_width))
    return (gate_grad, hidden_grad, grad_gate, grad_up, grad_down)

def one_sequence(inputs, grad_output, place_rows, chosen, attn_gain, w_query, key_value_projection, output_projection_weight, ffn_gain, w_router, w_gate, w_up, w_down):
    context_length = inputs.shape[0]
    query_group_count = QUERY_HEADS // KEY_VALUE_HEADS
    factor = 1.0 / math.sqrt(HEAD_SIZE)
    wide_input = inputs.astype(jnp.float32)
    normed_one, factor_one, first_hidden_state = rms_forward(wide_input, attn_gain)
    key_value_weight = key_value_projection.reshape(MODEL_DIM, KEY_VALUE_HEADS * 2 * HEAD_SIZE)
    query_matrix = jnp.dot(first_hidden_state, w_query, preferred_element_type=jnp.float32).reshape(context_length, QUERY_HEADS, HEAD_SIZE)
    key_value_rows = jnp.dot(first_hidden_state, key_value_weight, preferred_element_type=jnp.float32).reshape(context_length, KEY_VALUE_HEADS, 2, HEAD_SIZE)
    cosine_lookup, sine_lookup = rope_tables(place_rows, HEAD_SIZE)
    rotated_query = narrow_width_rows(apply_rotary(query_matrix, cosine_lookup, sine_lookup, 1.0)).reshape(context_length, KEY_VALUE_HEADS, query_group_count, HEAD_SIZE)
    k_rot = narrow_width_rows(apply_rotary(key_value_rows[:, :, 0], cosine_lookup, sine_lookup, 1.0))
    v_rows = narrow_width_rows(key_value_rows[:, :, 1])
    token_ids = jnp.arange(context_length, dtype=jnp.int32)
    allowed = attend_mask(token_ids, (token_ids - place_rows).astype(jnp.int32), token_ids)
    scores = jnp.einsum('tkgd,skd->kgts', rotated_query.astype(jnp.float32), k_rot.astype(jnp.float32)) * factor
    exp_scores = jnp.where(allowed[None, None], jnp.exp(scores), 0.0)
    row_total = lax.optimization_barrier(jnp.sum(exp_scores, axis=-1))
    weighted = jnp.einsum('kgts,skd->kgtd', narrow_width_rows(exp_scores).astype(jnp.float32), v_rows.astype(jnp.float32))
    head_out = narrow_width_rows(weighted / row_total[..., None])
    flat_heads = head_out.transpose(2, 0, 1, 3).reshape(context_length, QUERY_HEADS * HEAD_SIZE)
    residual = wide_input + jnp.dot(flat_heads, output_projection_weight, preferred_element_type=jnp.float32)
    normed_two, factor_two, hidden_two = rms_forward(residual, ffn_gain)
    logits = jnp.dot(hidden_two, w_router, preferred_element_type=jnp.float32)
    picks = chosen[:, :, None] == jnp.arange(EXPERTS, dtype=jnp.int32)[None, None, :]
    gate_weights = router_gates(logits, picks)
    kept_blocks = []
    mixture_rows = []
    for block_index in range(N_CTX):
        low_row = block_index * TOK_DEV
        tables = slot_tables(chosen[low_row:low_row + TOK_DEV], gate_weights[low_row:low_row + TOK_DEV], 0, EXPERTS, CAP)
        saved = expert_forward(hidden_two[low_row:low_row + TOK_DEV], tables[2], w_gate, w_up, w_down, EXPERTS, CAP)
        mixture_rows.append(combine(saved[4], tables[2], tables[3], TOK_DEV))
        kept_blocks.append((tables, saved))
    output = (residual + jnp.concatenate(mixture_rows, axis=0)).astype(jnp.bfloat16)
    grad_wide = grad_output.astype(jnp.float32)
    grad_gate = jnp.zeros(w_gate.shape, jnp.float32)
    grad_up = jnp.zeros(w_up.shape, jnp.float32)
    grad_down = jnp.zeros(w_down.shape, jnp.float32)
    gate_grads = []
    hidden_grads = []
    for block_index in range(N_CTX):
        low_row = block_index * TOK_DEV
        tables, saved = kept_blocks[block_index]
        hit_mask, slot_ids, source, scaled = tables
        grad_rows = grad_wide[low_row:low_row + TOK_DEV][source]
        block_back = expert_backward(grad_rows, hit_mask, slot_ids, source, scaled, saved, w_gate, w_up, w_down, EXPERTS, CAP, TOK_DEV)
        gate_grads.append(block_back[0])
        hidden_grads.append(block_back[1])
        grad_gate = grad_gate + block_back[2]
        grad_up = grad_up + block_back[3]
        grad_down = grad_down + block_back[4]
    gate_grad = jnp.concatenate(gate_grads, axis=0)
    sel_grad = gate_weights * (gate_grad - lax.optimization_barrier(jnp.sum(gate_weights * gate_grad, axis=-1, keepdims=True)))
    logit_grad = narrow_width_rows(lax.optimization_barrier(jnp.sum(jnp.where(picks, sel_grad[:, :, None], 0.0), axis=1)))
    grad_router = jnp.dot(hidden_two.T, logit_grad, preferred_element_type=jnp.float32)
    hidden_grad = jnp.concatenate(hidden_grads, axis=0) + jnp.dot(logit_grad, w_router.T, preferred_element_type=jnp.float32)
    back_two, grad_ffn_gain = rms_backward(hidden_grad, normed_two, factor_two, ffn_gain)
    residual_grad = grad_wide + back_two
    residual_gradient_second = narrow_width_rows(residual_grad)
    grad_out_proj = jnp.dot(flat_heads.T, residual_gradient_second, preferred_element_type=jnp.float32)
    per_head_gradient = narrow_width_rows(jnp.dot(residual_gradient_second, output_projection_weight.T, preferred_element_type=jnp.float32)).reshape(context_length, KEY_VALUE_HEADS, query_group_count, HEAD_SIZE).transpose(1, 2, 0, 3)
    head_grad_wide = per_head_gradient.astype(jnp.float32)
    row_delta = lax.optimization_barrier(jnp.sum(head_grad_wide * head_out.astype(jnp.float32), axis=-1))
    probability = jnp.where(allowed[None, None], jnp.exp(scores - jnp.log(row_total)[..., None]), 0.0)
    prob_grad = jnp.einsum('kgtd,skd->kgts', head_grad_wide, v_rows.astype(jnp.float32))
    score_grad = narrow_width_rows(probability * (prob_grad - row_delta[..., None]) * factor).astype(jnp.float32)
    query_grad = jnp.einsum('kgts,skd->tkgd', score_grad, k_rot.astype(jnp.float32)).reshape(context_length, QUERY_HEADS, HEAD_SIZE)
    key_grad = jnp.einsum('kgts,tkgd->skd', score_grad, rotated_query.astype(jnp.float32))
    value_gradient = jnp.einsum('kgts,kgtd->skd', narrow_width_rows(probability).astype(jnp.float32), head_grad_wide)
    query_back = narrow_width_rows(apply_rotary(query_grad, cosine_lookup, sine_lookup, -1.0)).reshape(context_length, QUERY_HEADS * HEAD_SIZE)
    key_backward_rows = apply_rotary(key_grad, cosine_lookup, sine_lookup, -1.0)
    key_value_backward = narrow_width_rows(jnp.stack([key_backward_rows, value_gradient], axis=2)).reshape(context_length, KEY_VALUE_HEADS * 2 * HEAD_SIZE)
    grad_query = jnp.dot(first_hidden_state.T, query_back, preferred_element_type=jnp.float32)
    key_value_gradient = jnp.dot(first_hidden_state.T, key_value_backward, preferred_element_type=jnp.float32).reshape(MODEL_DIM, KEY_VALUE_HEADS, 2, HEAD_SIZE)
    hidden_one_grad = jnp.dot(query_back, w_query.T, preferred_element_type=jnp.float32) + jnp.dot(key_value_backward, key_value_weight.T, preferred_element_type=jnp.float32)
    back_one, grad_attn_gain = rms_backward(hidden_one_grad, normed_one, factor_one, attn_gain)
    input_grad = residual_grad + back_one
    return (output, input_grad, (grad_attn_gain, grad_query, key_value_gradient, grad_out_proj, grad_ffn_gain, grad_router, grad_gate, grad_up, grad_down))

def reference(tokens, cotangent, positions, routes, attn_gain, w_query, key_value_projection, output_projection_weight, ffn_gain, w_router, w_gate, w_up, w_down):
    weights = (attn_gain, w_query, key_value_projection, output_projection_weight, ffn_gain, w_router, w_gate, w_up, w_down)
    start_grads = tuple((jnp.zeros(weight.shape, jnp.float32) for weight in weights))

    def advance(carried, item):
        output, input_grad, grads = one_sequence(item[0], item[1], item[2], item[3], attn_gain, w_query, key_value_projection, output_projection_weight, ffn_gain, w_router, w_gate, w_up, w_down)
        return (tuple((old + new for old, new in zip(carried, grads))), (output, input_grad))
    grads, outputs = lax.scan(advance, start_grads, (tokens, cotangent, positions, routes))
    return (outputs[0], outputs[1], grads[0], grads[1], grads[2], grads[3], grads[4], grads[5], grads[6], grads[7], grads[8])
```

```python
import math

import jax
import jax.numpy as jnp
from jax import lax
from jax.sharding import PartitionSpec as P

QUERY_HEADS = 16
KEY_VALUE_HEADS = 8
HEAD_SIZE = 64


EPS = 1e-06
THETA = 10000.0


def shifted(block, axis, distance):
    devices = range(lax.axis_size(axis))
    route = [(i - distance, i) for i in devices if i - distance in devices]
    return lax.ppermute(block, axis, route)


def rope_tables(place_rows, head_width):
    half_width = head_width // 2
    inverse = THETA ** (-2.0 * jnp.arange(half_width, dtype=jnp.float32) / head_width)
    angle = place_rows.astype(jnp.float32)[:, None] * inverse[None, :]
    return (jnp.cos(angle)[:, None, :], jnp.sin(angle)[:, None, :])


def apply_rotary(vector, cosine_lookup, sine_lookup, direction):
    half_width = vector.shape[-1] // 2
    first_half = vector[..., :half_width]
    second_half = vector[..., half_width:]
    return jnp.concatenate(
        [
            first_half * cosine_lookup - direction * second_half * sine_lookup,
            direction * first_half * sine_lookup + second_half * cosine_lookup,
        ],
        axis=-1,
    )


def rms_forward(wide_rows, gain_vector):
    factor = lax.rsqrt(jnp.mean(wide_rows * wide_rows, axis=-1, keepdims=True) + EPS)
    normed = wide_rows * factor
    return (normed, factor, (normed * gain_vector.astype(jnp.float32)).astype(jnp.bfloat16))


def rms_backward(gradient, normed, factor, gain_vector):
    gain_grad = jnp.sum(gradient * normed, axis=0)
    inner_term = gradient * gain_vector.astype(jnp.float32)
    back_term = factor * (
        inner_term - normed * jnp.mean(inner_term * normed, axis=-1, keepdims=True)
    )
    return (back_term, gain_grad)


def attend_mask(query_ids, query_starts, key_ids):
    return (key_ids[None, :] <= query_ids[:, None]) & (key_ids[None, :] >= query_starts[:, None])


def router_gates(logits, picks):
    selected = jnp.sum(jnp.where(picks, logits[:, None, :], 0.0), axis=-1)
    exp_sel = jnp.exp(selected)
    return exp_sel / jnp.sum(exp_sel, axis=-1, keepdims=True)


def slot_tables(route_rows, gate_weights, first_expert, expert_count, capacity):
    token_count = route_rows.shape[0]
    owners = first_expert + jnp.arange(expert_count, dtype=jnp.int32)
    hit_mask = route_rows[:, :, None] == owners[None, None, :]
    member = jnp.sum(hit_mask.astype(jnp.int32), axis=1)
    weight_rows = jnp.sum(jnp.where(hit_mask, gate_weights[:, :, None], 0.0), axis=1)
    places = jnp.cumsum(member, axis=0) - 1
    expert_ids = jnp.arange(expert_count, dtype=jnp.int32)
    slot_ids = jnp.where(
        member > 0, expert_ids[None, :] * capacity + places, expert_count * capacity
    )
    flat_slots = slot_ids.reshape(-1)
    token_ids = jnp.broadcast_to(
        jnp.arange(token_count, dtype=jnp.int32)[:, None], (token_count, expert_count)
    ).reshape(-1)
    source = jnp.zeros((expert_count * capacity + 1,), jnp.int32).at[flat_slots].set(token_ids)[:-1]
    scaled = (
        jnp.zeros((expert_count * capacity + 1,), jnp.float32)
        .at[flat_slots]
        .set(weight_rows.reshape(-1))[:-1]
    )
    return (hit_mask, slot_ids, source, scaled)


def expert_forward(hidden, source, w_gate, w_up, w_down, expert_count, capacity):
    picked = hidden[source].reshape(expert_count, capacity, hidden.shape[1])
    gate_pre = jnp.einsum("ecd,edf->ecf", picked, w_gate, preferred_element_type=jnp.float32)
    up_pre = jnp.einsum("ecd,edf->ecf", picked, w_up, preferred_element_type=jnp.float32)
    activation = (jax.nn.silu(gate_pre) * up_pre).astype(jnp.bfloat16)
    result = jnp.einsum("ecf,edf->ecd", activation, w_down, preferred_element_type=jnp.float32)
    return (picked, gate_pre, up_pre, activation, result)


def combine(result, source, scaled, token_count):
    model_width = result.shape[-1]
    flat_result = result.reshape(-1, model_width)
    return (
        jnp.zeros((token_count, model_width), jnp.float32)
        .at[source]
        .add(flat_result * scaled[:, None])
    )


def expert_backward(
    grad_rows,
    hit_mask,
    slot_ids,
    source,
    scaled,
    saved,
    w_gate,
    w_up,
    w_down,
    expert_count,
    capacity,
    token_count,
):
    picked, gate_pre, up_pre, activation, result = saved
    model_width = grad_rows.shape[1]
    slot_grad = jnp.sum(grad_rows * result.reshape(expert_count * capacity, model_width), axis=1)
    padded = jnp.concatenate([slot_grad, jnp.zeros((1,), jnp.float32)])
    per_expert = padded[slot_ids]
    gate_grad = jnp.sum(jnp.where(hit_mask, per_expert[:, None, :], 0.0), axis=2)
    out_grad = (
        (grad_rows * scaled[:, None])
        .astype(jnp.bfloat16)
        .reshape(expert_count, capacity, model_width)
    )
    grad_down = jnp.einsum("ecd,ecf->edf", out_grad, activation, preferred_element_type=jnp.float32)
    act_grad = jnp.einsum("ecd,edf->ecf", out_grad, w_down, preferred_element_type=jnp.float32)
    sigmoid_gate = jax.nn.sigmoid(gate_pre)
    gate_pre_grad = (
        act_grad * up_pre * sigmoid_gate * (1.0 + gate_pre * (1.0 - sigmoid_gate))
    ).astype(jnp.bfloat16)
    up_pre_grad = (act_grad * gate_pre * sigmoid_gate).astype(jnp.bfloat16)
    grad_gate = jnp.einsum(
        "ecd,ecf->edf", picked, gate_pre_grad, preferred_element_type=jnp.float32
    )
    grad_up = jnp.einsum("ecd,ecf->edf", picked, up_pre_grad, preferred_element_type=jnp.float32)
    picked_grad = jnp.einsum(
        "ecf,edf->ecd", gate_pre_grad, w_gate, preferred_element_type=jnp.float32
    ) + jnp.einsum("ecf,edf->ecd", up_pre_grad, w_up, preferred_element_type=jnp.float32)
    hidden_grad = (
        jnp.zeros((token_count, model_width), jnp.float32)
        .at[source]
        .add(picked_grad.reshape(-1, model_width))
    )
    return (gate_grad, hidden_grad, grad_gate, grad_up, grad_down)


def local(
    tokens,
    cotangent,
    positions,
    routes,
    attn_gain,
    w_query,
    key_value_projection,
    output_projection_weight,
    ffn_gain,
    w_router,
    w_gate,
    w_up,
    w_down,
):
    gain_one, gain_two, query_full, keyval_full, out_full, router_full = (
        lax.all_gather(attn_gain, "fsdp", axis=0, tiled=True),
        lax.all_gather(ffn_gain, "fsdp", axis=0, tiled=True),
        lax.all_gather(w_query, "fsdp", axis=0, tiled=True),
        lax.all_gather(key_value_projection, "fsdp", axis=0, tiled=True),
        lax.all_gather(output_projection_weight, "fsdp", axis=1, tiled=True),
        lax.all_gather(w_router, "fsdp", axis=0, tiled=True),
    )
    expert_full = (
        lax.all_gather(w_gate, "fsdp", axis=1, tiled=True),
        lax.all_gather(w_up, "fsdp", axis=1, tiled=True),
        lax.all_gather(w_down, "fsdp", axis=1, tiled=True),
    )
    input_rows = tokens[0]
    local_len = input_rows.shape[0]
    model_width = input_rows.shape[1]
    query_group_count = QUERY_HEADS // KEY_VALUE_HEADS
    local_heads = w_query.shape[1] // HEAD_SIZE
    local_kv = local_heads // query_group_count
    expert_count = w_gate.shape[0]
    capacity = local_len // 2
    ctx_count = lax.axis_size("ctx")
    ctx_rank = lax.axis_index("ctx")
    factor = 1.0 / math.sqrt(HEAD_SIZE)
    key_value_weight = keyval_full.reshape(model_width, local_kv * 2 * HEAD_SIZE)
    wide_input = input_rows.astype(jnp.float32)
    normed_one, factor_one, first_hidden_state = rms_forward(wide_input, gain_one)
    query_matrix = jnp.dot(
        first_hidden_state, query_full, preferred_element_type=jnp.float32
    ).reshape(local_len, local_heads, HEAD_SIZE)
    key_value_rows = jnp.dot(
        first_hidden_state, key_value_weight, preferred_element_type=jnp.float32
    ).reshape(local_len, local_kv, 2, HEAD_SIZE)
    place_rows = positions[0]
    cosine_lookup, sine_lookup = rope_tables(place_rows, HEAD_SIZE)
    rotated_query = (
        apply_rotary(query_matrix, cosine_lookup, sine_lookup, 1.0)
        .astype(jnp.bfloat16)
        .reshape(local_len, local_kv, query_group_count, HEAD_SIZE)
    )
    k_rot = apply_rotary(key_value_rows[:, :, 0], cosine_lookup, sine_lookup, 1.0).astype(
        jnp.bfloat16
    )
    v_rows = key_value_rows[:, :, 1].astype(jnp.bfloat16)
    local_ids = jnp.arange(local_len, dtype=jnp.int32)
    query_ids = ctx_rank * local_len + local_ids
    query_starts = query_ids - place_rows
    kv_pack = jnp.concatenate([k_rot, v_rows], axis=-1)
    kv_blocks = [kv_pack]
    key_ids = [query_ids]
    travelling = kv_pack
    cycle_step = 1
    travelling = shifted(travelling, "ctx", 1)
    kv_blocks.append(travelling)
    key_ids.append((ctx_rank - cycle_step) * local_len + local_ids)
    row_total = jnp.zeros((local_kv, query_group_count, local_len), jnp.float32)
    weighted = jnp.zeros((local_kv, query_group_count, local_len, HEAD_SIZE), jnp.float32)
    masks = []
    for block_index in range(ctx_count):
        allowed = attend_mask(query_ids, query_starts, key_ids[block_index])
        masks.append(allowed)
        key_rows = kv_blocks[block_index][..., :HEAD_SIZE]
        value_rows = kv_blocks[block_index][..., HEAD_SIZE:]
        scores = (
            jnp.einsum(
                "tkgd,skd->kgts", rotated_query, key_rows, preferred_element_type=jnp.float32
            )
            * factor
        )
        exp_scores = jnp.where(allowed[None, None], jnp.exp(scores), 0.0)
        row_total = row_total + jnp.sum(exp_scores, axis=-1)
        weighted = weighted + jnp.einsum(
            "kgts,skd->kgtd",
            exp_scores.astype(jnp.bfloat16),
            value_rows,
            preferred_element_type=jnp.float32,
        )
    head_out = (weighted / row_total[..., None]).astype(jnp.bfloat16)
    flat_heads = head_out.transpose(2, 0, 1, 3).reshape(local_len, local_heads * HEAD_SIZE)
    attn_part = jnp.dot(flat_heads, out_full, preferred_element_type=jnp.float32)
    residual = wide_input + lax.psum(attn_part, "tp")
    normed_two, factor_two, hidden_two = rms_forward(residual, gain_two)
    logits = jnp.dot(hidden_two, router_full, preferred_element_type=jnp.float32)
    route_rows = routes[0]
    picks = (
        route_rows[:, :, None] == jnp.arange(router_full.shape[1], dtype=jnp.int32)[None, None, :]
    )
    gate_weights = router_gates(logits, picks)
    first_expert = lax.axis_index("tp") * expert_count
    hit_mask, slot_ids, source, scaled = slot_tables(
        route_rows, gate_weights, first_expert, expert_count, capacity
    )
    saved = expert_forward(
        hidden_two, source, expert_full[0], expert_full[1], expert_full[2], expert_count, capacity
    )
    mixture_part = combine(saved[4], source, scaled, local_len)
    mixture = lax.psum(mixture_part.astype(jnp.bfloat16), "tp").astype(jnp.float32)
    out_rows = (residual + mixture).astype(jnp.bfloat16)
    grad_wide = cotangent[0].astype(jnp.float32)
    back_weights = (
        lax.all_gather(w_gate, "fsdp", axis=1, tiled=True),
        lax.all_gather(w_up, "fsdp", axis=1, tiled=True),
        lax.all_gather(w_down, "fsdp", axis=1, tiled=True),
    )
    grad_rows = grad_wide[source]
    gate_grad_part, hidden_grad_part, grad_gate, grad_up, grad_down = expert_backward(
        grad_rows,
        hit_mask,
        slot_ids,
        source,
        scaled,
        saved,
        back_weights[0],
        back_weights[1],
        back_weights[2],
        expert_count,
        capacity,
        local_len,
    )
    hidden_grad_sum, gate_grad = lax.psum((hidden_grad_part, gate_grad_part), "tp")
    sel_grad = gate_weights * (
        gate_grad - jnp.sum(gate_weights * gate_grad, axis=-1, keepdims=True)
    )
    logit_grad = jnp.sum(jnp.where(picks, sel_grad[:, :, None], 0.0), axis=1).astype(jnp.bfloat16)
    grad_router = jnp.einsum(
        "td,te->de", hidden_two, logit_grad, preferred_element_type=jnp.float32
    )
    hidden_grad = hidden_grad_sum + jnp.einsum(
        "te,de->td", logit_grad, router_full, preferred_element_type=jnp.float32
    )
    back_two, grad_ffn_gain = rms_backward(hidden_grad, normed_two, factor_two, gain_two)
    residual_grad = grad_wide + back_two
    residual_gradient_second = residual_grad.astype(jnp.bfloat16)
    grad_out_proj = jnp.einsum(
        "ti,td->id", flat_heads, residual_gradient_second, preferred_element_type=jnp.float32
    )
    per_head_gradient = jnp.einsum(
        "td,id->ti", residual_gradient_second, out_full, preferred_element_type=jnp.float32
    ).astype(jnp.bfloat16)
    per_head_gradient = per_head_gradient.reshape(
        local_len, local_kv, query_group_count, HEAD_SIZE
    ).transpose(1, 2, 0, 3)
    row_delta = jnp.sum(
        per_head_gradient.astype(jnp.float32) * head_out.astype(jnp.float32), axis=-1
    )
    log_total = jnp.log(row_total)
    query_grad = jnp.zeros((local_len, local_kv, query_group_count, HEAD_SIZE), jnp.float32)
    kv_grads = []
    for block_index in range(ctx_count):
        key_rows = kv_blocks[block_index][..., :HEAD_SIZE]
        value_rows = kv_blocks[block_index][..., HEAD_SIZE:]
        scores = (
            jnp.einsum(
                "tkgd,skd->kgts", rotated_query, key_rows, preferred_element_type=jnp.float32
            )
            * factor
        )
        probability = jnp.where(
            masks[block_index][None, None], jnp.exp(scores - log_total[..., None]), 0.0
        )
        prob_grad = jnp.einsum(
            "kgtd,skd->kgts", per_head_gradient, value_rows, preferred_element_type=jnp.float32
        )
        score_grad = (probability * (prob_grad - row_delta[..., None]) * factor).astype(
            jnp.bfloat16
        )
        query_grad = query_grad + jnp.einsum(
            "kgts,skd->tkgd", score_grad, key_rows, preferred_element_type=jnp.float32
        )
        key_grad = jnp.einsum(
            "kgts,tkgd->skd", score_grad, rotated_query, preferred_element_type=jnp.float32
        )
        value_gradient = jnp.einsum(
            "kgts,kgtd->skd",
            probability.astype(jnp.bfloat16),
            per_head_gradient,
            preferred_element_type=jnp.float32,
        )
        kv_grads.append(jnp.concatenate([key_grad, value_gradient], axis=-1))
    cycle_step = 1
    returning = shifted(kv_grads[cycle_step].astype(jnp.bfloat16), "ctx", -1).astype(jnp.float32)
    kv_grad_total = kv_grads[0] + returning
    key_backward_rows = apply_rotary(
        kv_grad_total[..., :HEAD_SIZE], cosine_lookup, sine_lookup, -1.0
    )
    key_value_backward = (
        jnp.stack([key_backward_rows, kv_grad_total[..., HEAD_SIZE:]], axis=2)
        .astype(jnp.bfloat16)
        .reshape(local_len, local_kv * 2 * HEAD_SIZE)
    )
    query_back = (
        apply_rotary(
            query_grad.reshape(local_len, local_heads, HEAD_SIZE), cosine_lookup, sine_lookup, -1.0
        )
        .astype(jnp.bfloat16)
        .reshape(local_len, local_heads * HEAD_SIZE)
    )
    grad_query = jnp.einsum(
        "td,tf->df", first_hidden_state, query_back, preferred_element_type=jnp.float32
    )
    key_value_gradient = jnp.einsum(
        "td,tf->df", first_hidden_state, key_value_backward, preferred_element_type=jnp.float32
    ).reshape(model_width, local_kv, 2, HEAD_SIZE)
    hidden_one_part = jnp.einsum(
        "tf,df->td", query_back, query_full, preferred_element_type=jnp.float32
    ) + jnp.einsum(
        "tf,df->td", key_value_backward, key_value_weight, preferred_element_type=jnp.float32
    )
    hidden_one_grad = lax.psum(hidden_one_part.astype(jnp.bfloat16), "tp").astype(jnp.float32)
    back_one, grad_attn_gain = rms_backward(hidden_one_grad, normed_one, factor_one, gain_one)
    input_grad = residual_grad + back_one
    shards = (
        lax.psum_scatter(
            grad_attn_gain.astype(jnp.bfloat16), "fsdp", scatter_dimension=0, tiled=True
        ).astype(jnp.float32),
        lax.psum_scatter(
            grad_ffn_gain.astype(jnp.bfloat16), "fsdp", scatter_dimension=0, tiled=True
        ).astype(jnp.float32),
        lax.psum_scatter(
            grad_query.astype(jnp.bfloat16), "fsdp", scatter_dimension=0, tiled=True
        ).astype(jnp.float32),
        lax.psum_scatter(
            key_value_gradient.astype(jnp.bfloat16), "fsdp", scatter_dimension=0, tiled=True
        ).astype(jnp.float32),
        lax.psum_scatter(
            grad_out_proj.astype(jnp.bfloat16), "fsdp", scatter_dimension=1, tiled=True
        ).astype(jnp.float32),
        lax.psum_scatter(
            grad_router.astype(jnp.bfloat16), "fsdp", scatter_dimension=0, tiled=True
        ).astype(jnp.float32),
    )
    piece_gate, piece_up, piece_down = (
        lax.psum_scatter(
            grad_gate.astype(jnp.bfloat16), ("fsdp", "ctx"), scatter_dimension=1, tiled=True
        ).astype(jnp.float32),
        lax.psum_scatter(
            grad_up.astype(jnp.bfloat16), ("fsdp", "ctx"), scatter_dimension=1, tiled=True
        ).astype(jnp.float32),
        lax.psum_scatter(
            grad_down.astype(jnp.bfloat16), ("fsdp", "ctx"), scatter_dimension=1, tiled=True
        ).astype(jnp.float32),
    )
    expert_totals = (
        lax.all_gather(piece_gate.astype(jnp.bfloat16), "ctx", axis=1, tiled=True).astype(
            piece_gate.dtype
        ),
        lax.all_gather(piece_up.astype(jnp.bfloat16), "ctx", axis=1, tiled=True).astype(
            piece_up.dtype
        ),
        lax.all_gather(piece_down.astype(jnp.bfloat16), "ctx", axis=1, tiled=True).astype(
            piece_down.dtype
        ),
    )
    small_totals = (
        lax.psum(shards[0].astype(jnp.bfloat16), "ctx").astype(jnp.float32),
        lax.psum(shards[1].astype(jnp.bfloat16), "ctx").astype(jnp.float32),
        lax.psum(shards[2].astype(jnp.bfloat16), "ctx").astype(jnp.float32),
        lax.psum(shards[3].astype(jnp.bfloat16), "ctx").astype(jnp.float32),
        lax.psum(shards[4].astype(jnp.bfloat16), "ctx").astype(jnp.float32),
        lax.psum(shards[5].astype(jnp.bfloat16), "ctx").astype(jnp.float32),
    )
    return (
        out_rows[None],
        input_grad[None],
        small_totals[0],
        small_totals[2],
        small_totals[3],
        small_totals[4],
        small_totals[1],
        small_totals[5],
        expert_totals[0],
        expert_totals[1],
        expert_totals[2],
    )


def rotated(block, axis, distance):
    count = lax.axis_size(axis)
    return lax.ppermute(block, axis, [(i, (i + distance) % count) for i in range(count)])


def pick_block(stacked, index):
    return lax.dynamic_index_in_dim(stacked, index, 0, keepdims=False)


def sum_over_tp(part):
    count = lax.axis_size("tp")
    pieces = part.astype(jnp.bfloat16).reshape(count, part.shape[0] // count, part.shape[1])
    pieces = lax.all_to_all(pieces, "tp", 0, 0, tiled=True)
    return jnp.sum(pieces.astype(jnp.float32), axis=0)


def scatter_over_fsdp(stacked):
    count = lax.axis_size("fsdp")
    rank = lax.axis_index("fsdp")
    total = pick_block(stacked, rank).astype(jnp.float32)
    for step in range(1, count):
        leaving = pick_block(stacked, (rank + step) % count)
        total = total + rotated(leaving, "fsdp", step).astype(jnp.float32)
    return total


def sum_over_ctx(total):
    sent = total.astype(jnp.bfloat16)
    result = total
    for step in range(1, lax.axis_size("ctx")):
        result = result + rotated(sent, "ctx", step).astype(jnp.float32)
    return result


def local_spread(
    tokens,
    cotangent,
    positions,
    routes,
    attn_gain,
    w_query,
    key_value_projection,
    output_projection_weight,
    ffn_gain,
    w_router,
    w_gate,
    w_up,
    w_down,
):
    everywhere = ("fsdp", "ctx", "tp")
    fsdp_count, ctx_count, tp_count = (lax.axis_size(name) for name in everywhere)
    fsdp_rank, ctx_rank, tp_rank = (lax.axis_index(name) for name in everywhere)
    input_rows = tokens[0]
    local_len, model_width = input_rows.shape
    slice_width = w_query.shape[0]
    own_len = local_len // tp_count
    block_count = fsdp_count * ctx_count
    expert_total = w_router.shape[1]
    ff_width = w_gate.shape[2]
    query_group_count = QUERY_HEADS // KEY_VALUE_HEADS
    head_width = w_query.shape[1]
    local_heads = head_width // HEAD_SIZE
    local_kv = local_heads // query_group_count
    capacity = local_len // 2
    factor = 1.0 / math.sqrt(HEAD_SIZE)
    own_start = tp_rank * own_len

    def own_rows(rows):
        return lax.dynamic_slice_in_dim(rows, own_start, own_len, 0)

    kv_width = key_value_projection.shape[1] * 2 * HEAD_SIZE
    side = jnp.concatenate([w_router, attn_gain[:, None], ffn_gain[:, None]], axis=1)
    side = jnp.pad(side, ((0, 0), (0, -side.shape[1] % 128)))
    packed = jnp.concatenate(
        [w_query, key_value_projection.reshape(slice_width, kv_width), side], axis=1
    )
    packed = lax.all_gather(packed, "fsdp", axis=0, tiled=True)
    out_full = lax.all_gather(output_projection_weight, "fsdp", axis=1, tiled=True)
    query_full = packed[:, :head_width]
    key_value_weight = packed[:, head_width : head_width + kv_width]
    side_full = packed[:, head_width + kv_width :]
    router_full = side_full[:, :expert_total]
    gain_one = side_full[:, expert_total]
    gain_two = side_full[:, expert_total + 1]

    def leaving_weights(step):
        index = ((fsdp_rank + step) % fsdp_count) * ctx_count + ctx_rank
        return jnp.stack([pick_block(w, index) for w in (w_gate, w_up, w_down)])

    weight_parts = [leaving_weights(0)]
    for step in range(1, fsdp_count):
        weight_parts.append(rotated(leaving_weights(step), "fsdp", step))
    expert_weights = []
    for kind in range(3):
        whole = jnp.zeros((fsdp_count, slice_width, ff_width), jnp.bfloat16)
        for step in range(fsdp_count):
            whole = lax.dynamic_update_index_in_dim(
                whole, weight_parts[step][kind], (fsdp_rank - step) % fsdp_count, 0
            )
        expert_weights.append(whole.reshape(fsdp_count * slice_width, ff_width))
    gate_weight, up_weight, down_weight = expert_weights

    route_rows = own_rows(routes[0])
    route_tail = jnp.pad(
        route_rows.astype(jnp.bfloat16), ((0, 0), (0, -route_rows.shape[1] % 128))
    )
    carried = jnp.concatenate([own_rows(cotangent[0]), route_tail], axis=1)
    carried = lax.all_gather(carried, everywhere, axis=0, tiled=True)
    grad_all = carried[:, :model_width].reshape(block_count, local_len, model_width)
    routes_all = carried[:, model_width : model_width + route_rows.shape[1]].astype(jnp.int32)
    expert_ids = jnp.arange(expert_total, dtype=jnp.int32)
    chosen_all = jnp.any(routes_all[:, :, None] == expert_ids[None, None, :], axis=1)
    own_expert = tp_rank * block_count + fsdp_rank * ctx_count + ctx_rank
    member = jnp.any(routes_all == own_expert, axis=1).reshape(block_count, local_len)
    places = jnp.cumsum(member.astype(jnp.int32), axis=1) - 1
    slots = jnp.where(member, places, capacity)
    slot_ids = jnp.arange(capacity, dtype=jnp.int32)
    hot = slots[:, None, :] == slot_ids[None, :, None]
    hot_b = hot.astype(jnp.bfloat16)

    def take_rows(rows):
        return (
            jnp.einsum("bst,btd->bsd", hot_b, rows, preferred_element_type=jnp.float32)
            .astype(jnp.bfloat16)
            .reshape(block_count * capacity, model_width)
        )

    def put_rows(rows):
        stacked = rows.reshape(block_count, capacity, model_width)
        return (
            jnp.einsum("bst,bsd->btd", hot_b, stacked, preferred_element_type=jnp.float32)
            .astype(jnp.bfloat16)
            .reshape(block_count * local_len, model_width)
        )

    wide_input = input_rows.astype(jnp.float32)
    normed_one, factor_one, first_hidden_state = rms_forward(wide_input, gain_one)
    query_matrix = jnp.dot(
        first_hidden_state, query_full, preferred_element_type=jnp.float32
    ).reshape(local_len, local_heads, HEAD_SIZE)
    key_value_rows = jnp.dot(
        first_hidden_state, key_value_weight, preferred_element_type=jnp.float32
    ).reshape(local_len, local_kv, 2, HEAD_SIZE)
    place_rows = positions[0]
    cosine_lookup, sine_lookup = rope_tables(place_rows, HEAD_SIZE)
    rotated_query = (
        apply_rotary(query_matrix, cosine_lookup, sine_lookup, 1.0)
        .astype(jnp.bfloat16)
        .reshape(local_len, local_kv, query_group_count, HEAD_SIZE)
    )
    k_rot = apply_rotary(key_value_rows[:, :, 0], cosine_lookup, sine_lookup, 1.0).astype(
        jnp.bfloat16
    )
    v_rows = key_value_rows[:, :, 1].astype(jnp.bfloat16)
    local_ids = jnp.arange(local_len, dtype=jnp.int32)
    query_ids = ctx_rank * local_len + local_ids
    query_starts = query_ids - place_rows
    kv_pack = jnp.concatenate([k_rot, v_rows], axis=-1)
    kv_blocks = [kv_pack]
    key_ids = [query_ids]
    for step in range(1, ctx_count):
        kv_blocks.append(shifted(kv_blocks[-1], "ctx", 1))
        key_ids.append((ctx_rank - step) * local_len + local_ids)
    row_total = jnp.zeros((local_kv, query_group_count, local_len), jnp.float32)
    weighted = jnp.zeros((local_kv, query_group_count, local_len, HEAD_SIZE), jnp.float32)
    masks = []
    for block_index in range(ctx_count):
        allowed = attend_mask(query_ids, query_starts, key_ids[block_index])
        masks.append(allowed)
        key_rows = kv_blocks[block_index][..., :HEAD_SIZE]
        value_rows = kv_blocks[block_index][..., HEAD_SIZE:]
        scores = (
            jnp.einsum(
                "tkgd,skd->kgts", rotated_query, key_rows, preferred_element_type=jnp.float32
            )
            * factor
        )
        exp_scores = jnp.where(allowed[None, None], jnp.exp(scores), 0.0)
        row_total = row_total + jnp.sum(exp_scores, axis=-1)
        weighted = weighted + jnp.einsum(
            "kgts,skd->kgtd",
            exp_scores.astype(jnp.bfloat16),
            value_rows,
            preferred_element_type=jnp.float32,
        )
    head_out = (weighted / row_total[..., None]).astype(jnp.bfloat16)
    flat_heads = head_out.transpose(2, 0, 1, 3).reshape(local_len, local_heads * HEAD_SIZE)
    attn_part = jnp.dot(flat_heads, out_full, preferred_element_type=jnp.float32)

    residual = own_rows(input_rows).astype(jnp.float32) + sum_over_tp(attn_part)
    normed_two, factor_two, hidden_two = rms_forward(residual, gain_two)
    hidden_all = lax.all_gather(hidden_two, everywhere, axis=0, tiled=True)
    own_chosen = jnp.any(route_rows[:, :, None] == expert_ids[None, None, :], axis=1)

    def gate_table(hidden, chosen):
        logits = jnp.dot(hidden, router_full, preferred_element_type=jnp.float32)
        exp_sel = jnp.where(chosen, jnp.exp(logits), 0.0)
        return exp_sel / jnp.sum(exp_sel, axis=-1, keepdims=True)

    own_gates = gate_table(hidden_two, own_chosen)
    gates_all = gate_table(hidden_all, chosen_all)
    expert_gate = jnp.sum(
        jnp.where(expert_ids[None, :] == own_expert, gates_all, 0.0), axis=1
    ).reshape(block_count, local_len)
    scaled = jnp.sum(jnp.where(hot, expert_gate[:, None, :], 0.0), axis=2).reshape(-1)

    picked = take_rows(hidden_all.reshape(block_count, local_len, model_width))
    gate_pre = jnp.dot(picked, gate_weight, preferred_element_type=jnp.float32)
    up_pre = jnp.dot(picked, up_weight, preferred_element_type=jnp.float32)
    activation = (jax.nn.silu(gate_pre) * up_pre).astype(jnp.bfloat16)
    result = jnp.einsum("cf,df->cd", activation, down_weight, preferred_element_type=jnp.float32)
    mixture_part = put_rows((result * scaled[:, None]).astype(jnp.bfloat16))

    grad_rows = take_rows(grad_all)
    grad_wide_rows = grad_rows.astype(jnp.float32)
    slot_grad = jnp.sum(grad_wide_rows * result, axis=1).reshape(block_count, capacity)
    gate_grad_part = jnp.sum(jnp.where(hot, slot_grad[:, :, None], 0.0), axis=1)
    out_grad = (grad_wide_rows * scaled[:, None]).astype(jnp.bfloat16)
    act_grad = jnp.dot(out_grad, down_weight, preferred_element_type=jnp.float32)
    sigmoid_gate = jax.nn.sigmoid(gate_pre)
    gate_pre_grad = (
        act_grad * up_pre * sigmoid_gate * (1.0 + gate_pre * (1.0 - sigmoid_gate))
    ).astype(jnp.bfloat16)
    up_pre_grad = (act_grad * gate_pre * sigmoid_gate).astype(jnp.bfloat16)
    picked_grad = jnp.einsum(
        "cf,df->cd", gate_pre_grad, gate_weight, preferred_element_type=jnp.float32
    ) + jnp.einsum("cf,df->cd", up_pre_grad, up_weight, preferred_element_type=jnp.float32)
    hidden_grad_part = put_rows(picked_grad.astype(jnp.bfloat16))
    hidden_grad_sum = lax.psum_scatter(
        hidden_grad_part, everywhere, scatter_dimension=0, tiled=True
    ).astype(jnp.float32)
    gate_grad = lax.all_to_all(
        gate_grad_part.reshape(block_count * tp_count, own_len), everywhere, 0, 0, tiled=True
    )
    gate_grad = (
        gate_grad.reshape(block_count, tp_count, own_len)
        .transpose(2, 1, 0)
        .reshape(own_len, expert_total)
    )
    mixture = lax.psum_scatter(mixture_part, everywhere, scatter_dimension=0, tiled=True)
    own_out = (residual + mixture.astype(jnp.float32)).astype(jnp.bfloat16)

    weight_grads = [
        jnp.einsum("cd,cf->df", rows, columns, preferred_element_type=jnp.float32)
        .astype(jnp.bfloat16)
        .reshape(fsdp_count, slice_width, ff_width)
        for rows, columns in (
            (picked, gate_pre_grad),
            (picked, up_pre_grad),
            (out_grad, activation),
        )
    ]
    weight_shape = (fsdp_count, ctx_count, slice_width, ff_width)
    weight_outs = [jnp.zeros(weight_shape, jnp.float32) for _ in range(3)]
    for step in range(fsdp_count):
        target = (fsdp_rank + step) % fsdp_count
        piece = jnp.stack([pick_block(grad, target) for grad in weight_grads])
        if step:
            piece = rotated(piece, "fsdp", step)
        source = (fsdp_rank - step) % fsdp_count
        for hop in range(ctx_count):
            seen = rotated(piece, "ctx", hop) if hop else piece
            seen_ctx = (ctx_rank - hop) % ctx_count
            for kind in range(3):
                weight_outs[kind] = lax.dynamic_update_slice(
                    weight_outs[kind],
                    seen[kind].astype(jnp.float32)[None, None],
                    (source, seen_ctx, 0, 0),
                )
    weight_outs = [
        grad.reshape(fsdp_count * ctx_count, slice_width, ff_width) for grad in weight_outs
    ]

    sel_grad = own_gates * (
        gate_grad - jnp.sum(own_gates * gate_grad, axis=-1, keepdims=True)
    )
    logit_grad = jnp.where(own_chosen, sel_grad, 0.0).astype(jnp.bfloat16)
    grad_router = jnp.einsum(
        "te,td->ed", logit_grad, hidden_two, preferred_element_type=jnp.float32
    )
    hidden_grad = hidden_grad_sum + jnp.einsum(
        "te,de->td", logit_grad, router_full, preferred_element_type=jnp.float32
    )
    back_two, grad_ffn_gain = rms_backward(hidden_grad, normed_two, factor_two, gain_two)
    residual_grad = own_rows(cotangent[0]).astype(jnp.float32) + back_two
    residual_gradient_second = lax.all_gather(
        residual_grad.astype(jnp.bfloat16), "tp", axis=0, tiled=True
    )
    early = lax.psum(jnp.concatenate([grad_router, grad_ffn_gain[None]], axis=0), everywhere)
    early = lax.dynamic_slice_in_dim(early, fsdp_rank * slice_width, slice_width, 1)

    grad_out_proj = jnp.einsum(
        "ti,td->id", flat_heads, residual_gradient_second, preferred_element_type=jnp.float32
    )
    grad_out_proj = grad_out_proj.astype(jnp.bfloat16).reshape(
        head_width, fsdp_count, slice_width
    )
    out_proj_total = sum_over_ctx(scatter_over_fsdp(grad_out_proj.transpose(1, 0, 2)))
    per_head_gradient = jnp.einsum(
        "td,id->ti", residual_gradient_second, out_full, preferred_element_type=jnp.float32
    ).astype(jnp.bfloat16)
    per_head_gradient = per_head_gradient.reshape(
        local_len, local_kv, query_group_count, HEAD_SIZE
    ).transpose(1, 2, 0, 3)
    row_delta = jnp.sum(
        per_head_gradient.astype(jnp.float32) * head_out.astype(jnp.float32), axis=-1
    )
    log_total = jnp.log(row_total)
    query_grad = jnp.zeros((local_len, local_kv, query_group_count, HEAD_SIZE), jnp.float32)
    kv_grads = []
    for block_index in range(ctx_count):
        key_rows = kv_blocks[block_index][..., :HEAD_SIZE]
        value_rows = kv_blocks[block_index][..., HEAD_SIZE:]
        scores = (
            jnp.einsum(
                "tkgd,skd->kgts", rotated_query, key_rows, preferred_element_type=jnp.float32
            )
            * factor
        )
        probability = jnp.where(
            masks[block_index][None, None], jnp.exp(scores - log_total[..., None]), 0.0
        )
        prob_grad = jnp.einsum(
            "kgtd,skd->kgts", per_head_gradient, value_rows, preferred_element_type=jnp.float32
        )
        score_grad = (probability * (prob_grad - row_delta[..., None]) * factor).astype(
            jnp.bfloat16
        )
        query_grad = query_grad + jnp.einsum(
            "kgts,skd->tkgd", score_grad, key_rows, preferred_element_type=jnp.float32
        )
        key_grad = jnp.einsum(
            "kgts,tkgd->skd", score_grad, rotated_query, preferred_element_type=jnp.float32
        )
        value_gradient = jnp.einsum(
            "kgts,kgtd->skd",
            probability.astype(jnp.bfloat16),
            per_head_gradient,
            preferred_element_type=jnp.float32,
        )
        kv_grads.append(jnp.concatenate([key_grad, value_gradient], axis=-1))
    kv_grad_total = kv_grads[0]
    for step in range(1, ctx_count):
        kv_grad_total = kv_grad_total + shifted(
            kv_grads[step].astype(jnp.bfloat16), "ctx", -step
        ).astype(jnp.float32)
    key_backward_rows = apply_rotary(
        kv_grad_total[..., :HEAD_SIZE], cosine_lookup, sine_lookup, -1.0
    )
    key_value_backward = (
        jnp.stack([key_backward_rows, kv_grad_total[..., HEAD_SIZE:]], axis=2)
        .astype(jnp.bfloat16)
        .reshape(local_len, kv_width)
    )
    query_back = (
        apply_rotary(
            query_grad.reshape(local_len, local_heads, HEAD_SIZE), cosine_lookup, sine_lookup, -1.0
        )
        .astype(jnp.bfloat16)
        .reshape(local_len, head_width)
    )
    both_back = jnp.concatenate([query_back, key_value_backward], axis=1)
    both_weight = packed[:, : head_width + kv_width]
    hidden_one_part = jnp.einsum(
        "tf,df->td", both_back, both_weight, preferred_element_type=jnp.float32
    )
    grad_attn_gain = lax.psum(jnp.sum(hidden_one_part * normed_one, axis=0), everywhere)
    grad_attn_gain = lax.dynamic_slice_in_dim(
        grad_attn_gain, fsdp_rank * slice_width, slice_width, 0
    )
    projection_grad = jnp.einsum(
        "td,tf->df", first_hidden_state, both_back, preferred_element_type=jnp.float32
    ).astype(jnp.bfloat16)
    projection_total = sum_over_ctx(
        scatter_over_fsdp(projection_grad.reshape(fsdp_count, slice_width, head_width + kv_width))
    )
    hidden_one_grad = sum_over_tp(hidden_one_part)
    back_one, _ = rms_backward(
        hidden_one_grad, own_rows(normed_one), own_rows(factor_one), gain_one
    )
    input_grad = residual_grad + back_one
    finished = jnp.concatenate([own_out, input_grad.astype(jnp.bfloat16)], axis=1)
    finished = lax.all_gather(finished, "tp", axis=0, tiled=True)
    return (
        finished[:, :model_width][None],
        finished[:, model_width:].astype(jnp.float32)[None],
        grad_attn_gain,
        projection_total[:, :head_width],
        projection_total[:, head_width:].reshape(key_value_projection.shape),
        out_proj_total,
        early[expert_total],
        early[:expert_total].T,
        weight_outs[0],
        weight_outs[1],
        weight_outs[2],
    )


def local_any(*args):
    devices = math.prod(lax.axis_size(name) for name in ("fsdp", "ctx", "tp"))
    return (local_spread if args[9].shape[1] == devices else local)(*args)


def solution(mesh):

    return jax.shard_map(
        local_any,
        mesh=mesh,
        in_specs=(
            P("fsdp", "ctx", None),
            P("fsdp", "ctx", None),
            P("fsdp", "ctx"),
            P("fsdp", "ctx", None),
            P("fsdp"),
            P("fsdp", "tp"),
            P("fsdp", "tp", None, None),
            P("tp", "fsdp"),
            P("fsdp"),
            P("fsdp", None),
            P("tp", "fsdp", None),
            P("tp", "fsdp", None),
            P("tp", "fsdp", None),
        ),
        out_specs=(
            P("fsdp", "ctx", None),
            P("fsdp", "ctx", None),
            P("fsdp"),
            P("fsdp", "tp"),
            P("fsdp", "tp", None, None),
            P("tp", "fsdp"),
            P("fsdp"),
            P("fsdp", None),
            P("tp", "fsdp", None),
            P("tp", "fsdp", None),
            P("tp", "fsdp", None),
        ),
        check_vma=False,
    )
```

```python
import math

import jax
import jax.numpy as jnp
from jax import lax
from jax.experimental.layout import Layout, with_layout_constraint
from jax.sharding import PartitionSpec as P

CF_DF_TO_CD = "cf,df->cd"
CTX = "ctx"
ECD_ECF_TO_EDF = "ecd,ecf->edf"
ECD_EDF_TO_ECF = "ecd,edf->ecf"
ECF_EDF_TO_ECD = "ecf,edf->ecd"
FSDP = "fsdp"
KGTD_SKD_TO_KGTS = "kgtd,skd->kgts"
KGTS_KGTD_TO_SKD = "kgts,kgtd->skd"
KGTS_SKD_TO_KGTD = "kgts,skd->kgtd"
KGTS_SKD_TO_TKGD = "kgts,skd->tkgd"
KGTS_TKGD_TO_SKD = "kgts,tkgd->skd"
TD_ID_TO_TI = "td,id->ti"
TD_TE_TO_DE = "td,te->de"
TD_TF_TO_DF = "td,tf->df"
TE_DE_TO_TD = "te,de->td"
TF_DF_TO_TD = "tf,df->td"
TKGD_SKD_TO_KGTS = "tkgd,skd->kgts"
TP = "tp"


QUERY_HEADS = 16
KEY_VALUE_HEADS = 8
HEAD_SIZE = 64


EPS = 1e-06
THETA = 10000.0


def shifted(block, axis, distance):
    devices = range(lax.axis_size(axis))
    route = [(i - distance, i) for i in devices if i - distance in devices]
    return lax.ppermute(block, axis, route)


def rope_tables(place_rows, head_width):
    half_width = head_width // 2
    inverse = THETA ** (-2.0 * jnp.arange(half_width, dtype=jnp.float32) / head_width)
    angle = place_rows.astype(jnp.float32)[:, None] * inverse[None, :]
    return (jnp.cos(angle)[:, None, :], jnp.sin(angle)[:, None, :])


def apply_rotary(vector, cosine_lookup, sine_lookup, direction):
    half_width = vector.shape[-1] // 2
    first_half = vector[..., :half_width]
    second_half = vector[..., half_width:]
    return jnp.concatenate(
        [
            first_half * cosine_lookup - direction * second_half * sine_lookup,
            direction * first_half * sine_lookup + second_half * cosine_lookup,
        ],
        axis=-1,
    )


def rms_forward(wide_rows, gain_vector):
    factor = lax.rsqrt(jnp.mean(wide_rows * wide_rows, axis=-1, keepdims=True) + EPS)
    normed = wide_rows * factor
    return (normed, factor, (normed * gain_vector.astype(jnp.float32)).astype(jnp.bfloat16))


def rms_backward(gradient, normed, factor, gain_vector):
    gain_grad = jnp.sum(gradient * normed, axis=0)
    inner_term = gradient * gain_vector.astype(jnp.float32)
    back_term = factor * (
        inner_term - normed * jnp.mean(inner_term * normed, axis=-1, keepdims=True)
    )
    return (back_term, gain_grad)


def attend_mask(query_ids, query_starts, key_ids):
    return (key_ids[None, :] <= query_ids[:, None]) & (key_ids[None, :] >= query_starts[:, None])


def router_gates(logits, picks):
    selected = jnp.sum(jnp.where(picks, logits[:, None, :], 0.0), axis=-1)
    exp_sel = jnp.exp(selected)
    return exp_sel / jnp.sum(exp_sel, axis=-1, keepdims=True)


def slot_tables(route_rows, gate_weights, first_expert, expert_count, capacity):
    token_count = route_rows.shape[0]
    owners = first_expert + jnp.arange(expert_count, dtype=jnp.int32)
    hit_mask = route_rows[:, :, None] == owners[None, None, :]
    member = jnp.sum(hit_mask.astype(jnp.int32), axis=1)
    weight_rows = jnp.sum(jnp.where(hit_mask, gate_weights[:, :, None], 0.0), axis=1)
    places = jnp.cumsum(member, axis=0) - 1
    expert_ids = jnp.arange(expert_count, dtype=jnp.int32)
    slot_ids = jnp.where(
        member > 0, expert_ids[None, :] * capacity + places, expert_count * capacity
    )
    flat_slots = slot_ids.reshape(-1)
    token_ids = jnp.broadcast_to(
        jnp.arange(token_count, dtype=jnp.int32)[:, None], (token_count, expert_count)
    ).reshape(-1)
    source = jnp.zeros((expert_count * capacity + 1,), jnp.int32).at[flat_slots].set(token_ids)[:-1]
    scaled = (
        jnp.zeros((expert_count * capacity + 1,), jnp.float32)
        .at[flat_slots]
        .set(weight_rows.reshape(-1))[:-1]
    )
    return (hit_mask, slot_ids, source, scaled)


def expert_forward(hidden, source, w_gate, w_up, w_down, expert_count, capacity):
    picked = hidden[source].reshape(expert_count, capacity, hidden.shape[1])
    gate_pre = jnp.einsum(ECD_EDF_TO_ECF, picked, w_gate, preferred_element_type=jnp.float32)
    up_pre = jnp.einsum(ECD_EDF_TO_ECF, picked, w_up, preferred_element_type=jnp.float32)
    activation = (jax.nn.silu(gate_pre) * up_pre).astype(jnp.bfloat16)
    result = jnp.einsum(ECF_EDF_TO_ECD, activation, w_down, preferred_element_type=jnp.float32)
    return (picked, gate_pre, up_pre, activation, result)


def combine(result, source, scaled, token_count):
    model_width = result.shape[-1]
    flat_result = result.reshape(-1, model_width)
    return (
        jnp.zeros((token_count, model_width), jnp.float32)
        .at[source]
        .add(flat_result * scaled[:, None])
    )


def expert_backward(
    grad_rows,
    hit_mask,
    slot_ids,
    source,
    scaled,
    saved,
    w_gate,
    w_up,
    w_down,
    expert_count,
    capacity,
    token_count,
):
    picked, gate_pre, up_pre, activation, result = saved
    model_width = grad_rows.shape[1]
    slot_grad = jnp.sum(grad_rows * result.reshape(expert_count * capacity, model_width), axis=1)
    padded = jnp.concatenate([slot_grad, jnp.zeros((1,), jnp.float32)])
    per_expert = padded[slot_ids]
    gate_grad = jnp.sum(jnp.where(hit_mask, per_expert[:, None, :], 0.0), axis=2)
    out_grad = (
        (grad_rows * scaled[:, None])
        .astype(jnp.bfloat16)
        .reshape(expert_count, capacity, model_width)
    )
    grad_down = jnp.einsum(ECD_ECF_TO_EDF, out_grad, activation, preferred_element_type=jnp.float32)
    act_grad = jnp.einsum(ECD_EDF_TO_ECF, out_grad, w_down, preferred_element_type=jnp.float32)
    sigmoid_gate = jax.nn.sigmoid(gate_pre)
    gate_pre_grad = (
        act_grad * up_pre * sigmoid_gate * (1.0 + gate_pre * (1.0 - sigmoid_gate))
    ).astype(jnp.bfloat16)
    up_pre_grad = (act_grad * gate_pre * sigmoid_gate).astype(jnp.bfloat16)
    grad_gate = jnp.einsum(
        ECD_ECF_TO_EDF, picked, gate_pre_grad, preferred_element_type=jnp.float32
    )
    grad_up = jnp.einsum(ECD_ECF_TO_EDF, picked, up_pre_grad, preferred_element_type=jnp.float32)
    picked_grad = jnp.einsum(
        ECF_EDF_TO_ECD, gate_pre_grad, w_gate, preferred_element_type=jnp.float32
    ) + jnp.einsum(ECF_EDF_TO_ECD, up_pre_grad, w_up, preferred_element_type=jnp.float32)
    hidden_grad = (
        jnp.zeros((token_count, model_width), jnp.float32)
        .at[source]
        .add(picked_grad.reshape(-1, model_width))
    )
    return (gate_grad, hidden_grad, grad_gate, grad_up, grad_down)


def local(
    tokens,
    cotangent,
    positions,
    routes,
    attn_gain,
    w_query,
    key_value_projection,
    output_projection_weight,
    ffn_gain,
    w_router,
    w_gate,
    w_up,
    w_down,
):
    gain_one, gain_two, query_full, keyval_full, out_full, router_full = (
        lax.all_gather(attn_gain, FSDP, axis=0, tiled=True),
        lax.all_gather(ffn_gain, FSDP, axis=0, tiled=True),
        lax.all_gather(w_query, FSDP, axis=0, tiled=True),
        lax.all_gather(key_value_projection, FSDP, axis=0, tiled=True),
        lax.all_gather(output_projection_weight, FSDP, axis=1, tiled=True),
        lax.all_gather(w_router, FSDP, axis=0, tiled=True),
    )
    expert_full = (
        lax.all_gather(w_gate, FSDP, axis=1, tiled=True),
        lax.all_gather(w_up, FSDP, axis=1, tiled=True),
        lax.all_gather(w_down, FSDP, axis=1, tiled=True),
    )
    input_rows = tokens[0]
    local_len = input_rows.shape[0]
    model_width = input_rows.shape[1]
    query_group_count = QUERY_HEADS // KEY_VALUE_HEADS
    local_heads = w_query.shape[1] // HEAD_SIZE
    local_kv = local_heads // query_group_count
    expert_count = w_gate.shape[0]
    capacity = local_len // 2
    ctx_count = lax.axis_size(CTX)
    ctx_rank = lax.axis_index(CTX)
    factor = 1.0 / math.sqrt(HEAD_SIZE)
    key_value_weight = keyval_full.reshape(model_width, local_kv * 2 * HEAD_SIZE)
    wide_input = input_rows.astype(jnp.float32)
    normed_one, factor_one, first_hidden_state = rms_forward(wide_input, gain_one)
    query_matrix = jnp.dot(
        first_hidden_state, query_full, preferred_element_type=jnp.float32
    ).reshape(local_len, local_heads, HEAD_SIZE)
    key_value_rows = jnp.dot(
        first_hidden_state, key_value_weight, preferred_element_type=jnp.float32
    ).reshape(local_len, local_kv, 2, HEAD_SIZE)
    place_rows = positions[0]
    cosine_lookup, sine_lookup = rope_tables(place_rows, HEAD_SIZE)
    rotated_query = (
        apply_rotary(query_matrix, cosine_lookup, sine_lookup, 1.0)
        .astype(jnp.bfloat16)
        .reshape(local_len, local_kv, query_group_count, HEAD_SIZE)
    )
    k_rot = apply_rotary(key_value_rows[:, :, 0], cosine_lookup, sine_lookup, 1.0).astype(
        jnp.bfloat16
    )
    v_rows = key_value_rows[:, :, 1].astype(jnp.bfloat16)
    local_ids = jnp.arange(local_len, dtype=jnp.int32)
    query_ids = ctx_rank * local_len + local_ids
    query_starts = query_ids - place_rows
    kv_pack = jnp.concatenate([k_rot, v_rows], axis=-1)
    kv_blocks = [kv_pack]
    key_ids = [query_ids]
    travelling = kv_pack
    cycle_step = 1
    travelling = shifted(travelling, CTX, 1)
    kv_blocks.append(travelling)
    key_ids.append((ctx_rank - cycle_step) * local_len + local_ids)
    row_total = jnp.zeros((local_kv, query_group_count, local_len), jnp.float32)
    weighted = jnp.zeros((local_kv, query_group_count, local_len, HEAD_SIZE), jnp.float32)
    masks = []
    for block_index in range(ctx_count):
        allowed = attend_mask(query_ids, query_starts, key_ids[block_index])
        masks.append(allowed)
        key_rows = kv_blocks[block_index][..., :HEAD_SIZE]
        value_rows = kv_blocks[block_index][..., HEAD_SIZE:]
        scores = (
            jnp.einsum(
                TKGD_SKD_TO_KGTS, rotated_query, key_rows, preferred_element_type=jnp.float32
            )
            * factor
        )
        exp_scores = jnp.where(allowed[None, None], jnp.exp(scores), 0.0)
        row_total = row_total + jnp.sum(exp_scores, axis=-1)
        weighted = weighted + jnp.einsum(
            KGTS_SKD_TO_KGTD,
            exp_scores.astype(jnp.bfloat16),
            value_rows,
            preferred_element_type=jnp.float32,
        )
    head_out = (weighted / row_total[..., None]).astype(jnp.bfloat16)
    flat_heads = head_out.transpose(2, 0, 1, 3).reshape(local_len, local_heads * HEAD_SIZE)
    attn_part = jnp.dot(flat_heads, out_full, preferred_element_type=jnp.float32)
    residual = wide_input + lax.psum(attn_part, TP)
    normed_two, factor_two, hidden_two = rms_forward(residual, gain_two)
    logits = jnp.dot(hidden_two, router_full, preferred_element_type=jnp.float32)
    route_rows = routes[0]
    picks = (
        route_rows[:, :, None] == jnp.arange(router_full.shape[1], dtype=jnp.int32)[None, None, :]
    )
    gate_weights = router_gates(logits, picks)
    first_expert = lax.axis_index(TP) * expert_count
    hit_mask, slot_ids, source, scaled = slot_tables(
        route_rows, gate_weights, first_expert, expert_count, capacity
    )
    saved = expert_forward(
        hidden_two, source, expert_full[0], expert_full[1], expert_full[2], expert_count, capacity
    )
    mixture_part = combine(saved[4], source, scaled, local_len)
    mixture = lax.psum(mixture_part.astype(jnp.bfloat16), TP).astype(jnp.float32)
    out_rows = (residual + mixture).astype(jnp.bfloat16)
    grad_wide = cotangent[0].astype(jnp.float32)
    back_weights = (
        lax.all_gather(w_gate, FSDP, axis=1, tiled=True),
        lax.all_gather(w_up, FSDP, axis=1, tiled=True),
        lax.all_gather(w_down, FSDP, axis=1, tiled=True),
    )
    grad_rows = grad_wide[source]
    gate_grad_part, hidden_grad_part, grad_gate, grad_up, grad_down = expert_backward(
        grad_rows,
        hit_mask,
        slot_ids,
        source,
        scaled,
        saved,
        back_weights[0],
        back_weights[1],
        back_weights[2],
        expert_count,
        capacity,
        local_len,
    )
    hidden_grad_sum, gate_grad = lax.psum((hidden_grad_part, gate_grad_part), TP)
    sel_grad = gate_weights * (
        gate_grad - jnp.sum(gate_weights * gate_grad, axis=-1, keepdims=True)
    )
    logit_grad = jnp.sum(jnp.where(picks, sel_grad[:, :, None], 0.0), axis=1).astype(jnp.bfloat16)
    grad_router = jnp.einsum(
        TD_TE_TO_DE, hidden_two, logit_grad, preferred_element_type=jnp.float32
    )
    hidden_grad = hidden_grad_sum + jnp.einsum(
        TE_DE_TO_TD, logit_grad, router_full, preferred_element_type=jnp.float32
    )
    back_two, grad_ffn_gain = rms_backward(hidden_grad, normed_two, factor_two, gain_two)
    residual_grad = grad_wide + back_two
    residual_gradient_second = residual_grad.astype(jnp.bfloat16)
    grad_out_proj = jnp.einsum(
        "ti,td->id", flat_heads, residual_gradient_second, preferred_element_type=jnp.float32
    )
    per_head_gradient = jnp.einsum(
        TD_ID_TO_TI, residual_gradient_second, out_full, preferred_element_type=jnp.float32
    ).astype(jnp.bfloat16)
    per_head_gradient = per_head_gradient.reshape(
        local_len, local_kv, query_group_count, HEAD_SIZE
    ).transpose(1, 2, 0, 3)
    row_delta = jnp.sum(
        per_head_gradient.astype(jnp.float32) * head_out.astype(jnp.float32), axis=-1
    )
    log_total = jnp.log(row_total)
    query_grad = jnp.zeros((local_len, local_kv, query_group_count, HEAD_SIZE), jnp.float32)
    kv_grads = []
    for block_index in range(ctx_count):
        key_rows = kv_blocks[block_index][..., :HEAD_SIZE]
        value_rows = kv_blocks[block_index][..., HEAD_SIZE:]
        scores = (
            jnp.einsum(
                TKGD_SKD_TO_KGTS, rotated_query, key_rows, preferred_element_type=jnp.float32
            )
            * factor
        )
        probability = jnp.where(
            masks[block_index][None, None], jnp.exp(scores - log_total[..., None]), 0.0
        )
        prob_grad = jnp.einsum(
            KGTD_SKD_TO_KGTS, per_head_gradient, value_rows, preferred_element_type=jnp.float32
        )
        score_grad = (probability * (prob_grad - row_delta[..., None]) * factor).astype(
            jnp.bfloat16
        )
        query_grad = query_grad + jnp.einsum(
            KGTS_SKD_TO_TKGD, score_grad, key_rows, preferred_element_type=jnp.float32
        )
        key_grad = jnp.einsum(
            KGTS_TKGD_TO_SKD, score_grad, rotated_query, preferred_element_type=jnp.float32
        )
        value_gradient = jnp.einsum(
            KGTS_KGTD_TO_SKD,
            probability.astype(jnp.bfloat16),
            per_head_gradient,
            preferred_element_type=jnp.float32,
        )
        kv_grads.append(jnp.concatenate([key_grad, value_gradient], axis=-1))
    cycle_step = 1
    returning = shifted(kv_grads[cycle_step].astype(jnp.bfloat16), CTX, -1).astype(jnp.float32)
    kv_grad_total = kv_grads[0] + returning
    key_backward_rows = apply_rotary(
        kv_grad_total[..., :HEAD_SIZE], cosine_lookup, sine_lookup, -1.0
    )
    key_value_backward = (
        jnp.stack([key_backward_rows, kv_grad_total[..., HEAD_SIZE:]], axis=2)
        .astype(jnp.bfloat16)
        .reshape(local_len, local_kv * 2 * HEAD_SIZE)
    )
    query_back = (
        apply_rotary(
            query_grad.reshape(local_len, local_heads, HEAD_SIZE), cosine_lookup, sine_lookup, -1.0
        )
        .astype(jnp.bfloat16)
        .reshape(local_len, local_heads * HEAD_SIZE)
    )
    grad_query = jnp.einsum(
        TD_TF_TO_DF, first_hidden_state, query_back, preferred_element_type=jnp.float32
    )
    key_value_gradient = jnp.einsum(
        TD_TF_TO_DF, first_hidden_state, key_value_backward, preferred_element_type=jnp.float32
    ).reshape(model_width, local_kv, 2, HEAD_SIZE)
    hidden_one_part = jnp.einsum(
        TF_DF_TO_TD, query_back, query_full, preferred_element_type=jnp.float32
    ) + jnp.einsum(
        TF_DF_TO_TD, key_value_backward, key_value_weight, preferred_element_type=jnp.float32
    )
    hidden_one_grad = lax.psum(hidden_one_part.astype(jnp.bfloat16), TP).astype(jnp.float32)
    back_one, grad_attn_gain = rms_backward(hidden_one_grad, normed_one, factor_one, gain_one)
    input_grad = residual_grad + back_one
    shards = (
        lax.psum_scatter(
            grad_attn_gain.astype(jnp.bfloat16), FSDP, scatter_dimension=0, tiled=True
        ).astype(jnp.float32),
        lax.psum_scatter(
            grad_ffn_gain.astype(jnp.bfloat16), FSDP, scatter_dimension=0, tiled=True
        ).astype(jnp.float32),
        lax.psum_scatter(
            grad_query.astype(jnp.bfloat16), FSDP, scatter_dimension=0, tiled=True
        ).astype(jnp.float32),
        lax.psum_scatter(
            key_value_gradient.astype(jnp.bfloat16), FSDP, scatter_dimension=0, tiled=True
        ).astype(jnp.float32),
        lax.psum_scatter(
            grad_out_proj.astype(jnp.bfloat16), FSDP, scatter_dimension=1, tiled=True
        ).astype(jnp.float32),
        lax.psum_scatter(
            grad_router.astype(jnp.bfloat16), FSDP, scatter_dimension=0, tiled=True
        ).astype(jnp.float32),
    )
    piece_gate, piece_up, piece_down = (
        lax.psum_scatter(
            grad_gate.astype(jnp.bfloat16), (FSDP, CTX), scatter_dimension=1, tiled=True
        ).astype(jnp.float32),
        lax.psum_scatter(
            grad_up.astype(jnp.bfloat16), (FSDP, CTX), scatter_dimension=1, tiled=True
        ).astype(jnp.float32),
        lax.psum_scatter(
            grad_down.astype(jnp.bfloat16), (FSDP, CTX), scatter_dimension=1, tiled=True
        ).astype(jnp.float32),
    )
    expert_totals = (
        lax.all_gather(piece_gate.astype(jnp.bfloat16), CTX, axis=1, tiled=True).astype(
            piece_gate.dtype
        ),
        lax.all_gather(piece_up.astype(jnp.bfloat16), CTX, axis=1, tiled=True).astype(
            piece_up.dtype
        ),
        lax.all_gather(piece_down.astype(jnp.bfloat16), CTX, axis=1, tiled=True).astype(
            piece_down.dtype
        ),
    )
    small_totals = (
        lax.psum(shards[0].astype(jnp.bfloat16), CTX).astype(jnp.float32),
        lax.psum(shards[1].astype(jnp.bfloat16), CTX).astype(jnp.float32),
        lax.psum(shards[2].astype(jnp.bfloat16), CTX).astype(jnp.float32),
        lax.psum(shards[3].astype(jnp.bfloat16), CTX).astype(jnp.float32),
        lax.psum(shards[4].astype(jnp.bfloat16), CTX).astype(jnp.float32),
        lax.psum(shards[5].astype(jnp.bfloat16), CTX).astype(jnp.float32),
    )
    return (
        out_rows[None],
        input_grad[None],
        small_totals[0],
        small_totals[2],
        small_totals[3],
        small_totals[4],
        small_totals[1],
        small_totals[5],
        expert_totals[0],
        expert_totals[1],
        expert_totals[2],
    )


def rotated(block, axis, distance):
    count = lax.axis_size(axis)
    return lax.ppermute(block, axis, [(i, (i + distance) % count) for i in range(count)])


def pick_block(stacked, index):
    return lax.dynamic_index_in_dim(stacked, index, 0, keepdims=False)


def sum_over_tp(part, shared=None):
    count = lax.axis_size(TP)
    pieces = part.astype(jnp.bfloat16).reshape(count, part.shape[0] // count, part.shape[1])
    if shared is not None:
        shared = jnp.pad(shared.astype(jnp.bfloat16)[None, None], ((0, 0), (0, 15), (0, 0)))
        shared = jnp.broadcast_to(shared, (count,) + shared.shape[1:])
        pieces = jnp.concatenate([pieces, shared], axis=1)
    pieces = lax.all_to_all(pieces, TP, 0, 0, tiled=True)
    return jnp.sum(pieces.astype(jnp.float32), axis=0)


def row_major(rows):
    return with_layout_constraint(rows, Layout(major_to_minor=tuple(range(rows.ndim))))


def after(value, earlier):
    return lax.optimization_barrier((value, earlier))[0]


def in_order(pieces, axis, place=0):
    count = lax.axis_size(axis)
    rank = lax.axis_index(axis)
    shape = pieces[0].shape
    whole = jnp.zeros(shape[:place] + (count,) + shape[place:], pieces[0].dtype)
    for step in range(count):
        whole = lax.dynamic_update_index_in_dim(
            whole, pieces[step], (rank - step) % count, place
        )
    return whole


def all_steps(block, axis):
    return [block] + [rotated(block, axis, step) for step in range(1, lax.axis_size(axis))]


def tp_partner(block, distance):
    count = lax.axis_size(TP)
    return lax.ppermute(block, TP, [(i, i ^ distance) for i in range(count)])


def tp_stages():
    distances = []
    distance = lax.axis_size(TP) // 2
    while distance:
        distances.append(distance)
        distance //= 2
    return distances


def spread(pieces):
    far, *near = tp_stages()
    result = []
    for flip, block in enumerate(halves(in_order(pieces, FSDP))):
        done = [FSDP]
        for stage in ([far, CTX] if flip else [CTX, far]) + near:
            place = sum(1 for other in done if rank_of(other) < rank_of(stage))
            if isinstance(stage, str):
                pieces = all_steps(block, stage)
            else:
                pieces = [block, tp_partner(block, stage)]
            if isinstance(stage, str):
                block = in_order(pieces, stage, place)
            else:
                bit = (lax.axis_index(TP) // stage) % 2
                shape = block.shape
                whole = jnp.zeros(shape[:place] + (2,) + shape[place:], block.dtype)
                whole = lax.dynamic_update_index_in_dim(whole, pieces[0], bit, place)
                block = lax.dynamic_update_index_in_dim(whole, pieces[1], 1 - bit, place)
            done.append(stage)
        result.append(block)
    return result


def rank_of(stage):
    return {FSDP: 0, CTX: 1}[stage] if isinstance(stage, str) else 2 + 1.0 / stage


def collect(parts):
    far, *near = tp_stages()
    summed = []
    for flip, stacked in enumerate(parts):
        stages = list(reversed(near)) + ([CTX, far] if flip else [far, CTX])
        left = sorted(stages + [FSDP], key=rank_of)
        for stage in stages:
            place = left.index(stage)
            left.remove(stage)
            if isinstance(stage, str):
                count = lax.axis_size(stage)
                rank = lax.axis_index(stage)
                pieces = [lax.dynamic_index_in_dim(stacked, rank, place, keepdims=False)]
                for step in range(1, count):
                    leaving = lax.dynamic_index_in_dim(
                        stacked, (rank + step) % count, place, keepdims=False
                    )
                    pieces.append(rotated(leaving, stage, step))
            else:
                bit = (lax.axis_index(TP) // stage) % 2
                leaving = lax.dynamic_index_in_dim(stacked, 1 - bit, place, keepdims=False)
                pieces = [
                    lax.dynamic_index_in_dim(stacked, bit, place, keepdims=False),
                    tp_partner(leaving, stage),
                ]
            total = sum(piece.astype(jnp.float32) for piece in pieces)
            stacked = total.astype(jnp.bfloat16)
        summed.append(stacked)
    pieces = scatter_start(jnp.concatenate(summed, axis=-1))
    return sum(piece.astype(jnp.float32) for piece in pieces)


def halves(rows):
    width = rows.shape[-1] // 2
    return rows[..., :width], rows[..., width:]


def scatter_start(stacked):
    count = lax.axis_size(FSDP)
    rank = lax.axis_index(FSDP)
    pieces = [pick_block(stacked, rank)]
    for step in range(1, count):
        pieces.append(rotated(pick_block(stacked, (rank + step) % count), FSDP, step))
    return pieces


def scatter_finish(pieces):
    total = sum(piece.astype(jnp.float32) for piece in pieces)
    sent = total.astype(jnp.bfloat16)
    for step in range(1, lax.axis_size(CTX)):
        total = total + rotated(sent, CTX, step).astype(jnp.float32)
    return total


def local_spread(
    tokens,
    cotangent,
    positions,
    routes,
    attn_gain,
    w_query,
    key_value_projection,
    output_projection_weight,
    ffn_gain,
    w_router,
    w_gate,
    w_up,
    w_down,
):
    everywhere = (FSDP, CTX, TP)
    fsdp_count, ctx_count, tp_count = (lax.axis_size(name) for name in everywhere)
    fsdp_rank, ctx_rank, tp_rank = (lax.axis_index(name) for name in everywhere)
    input_rows = tokens[0]
    local_len, model_width = input_rows.shape
    slice_width = w_query.shape[0]
    own_len = local_len // tp_count
    block_count = fsdp_count * ctx_count
    expert_total = w_router.shape[1]
    ff_width = w_gate.shape[2]
    query_group_count = QUERY_HEADS // KEY_VALUE_HEADS
    head_width = w_query.shape[1]
    local_heads = head_width // HEAD_SIZE
    local_kv = local_heads // query_group_count
    capacity = local_len // 2
    factor = 1.0 / math.sqrt(HEAD_SIZE)
    own_start = tp_rank * own_len

    def own_rows(rows):
        return lax.dynamic_slice_in_dim(rows, own_start, own_len, 0)

    route_rows = own_rows(routes[0])
    kv_width = key_value_projection.shape[1] * 2 * HEAD_SIZE
    side = jnp.concatenate([w_router, attn_gain[:, None], ffn_gain[:, None]], axis=1)
    side = jnp.pad(side, ((0, 0), (0, -side.shape[1] % 128)))
    packed = jnp.concatenate(
        [w_query, key_value_projection.reshape(slice_width, kv_width), side], axis=1
    )
    packed_parts = all_steps(row_major(packed), FSDP)
    both_width = head_width + kv_width
    both_weight = in_order([p[:, :both_width] for p in packed_parts], FSDP).reshape(
        model_width, both_width
    )
    both_weight = row_major(both_weight)
    side_full = in_order([p[:, both_width:] for p in packed_parts], FSDP).reshape(
        model_width, side.shape[1]
    )
    out_parts = all_steps(after(output_projection_weight, packed_parts), FSDP)
    out_full = (
        in_order(out_parts, FSDP).transpose(1, 0, 2).reshape(head_width, model_width)
    )
    query_full = both_weight[:, :head_width]
    key_value_weight = both_weight[:, head_width:]
    router_full = side_full[:, :expert_total]
    gain_one = side_full[:, expert_total]
    gain_two = side_full[:, expert_total + 1]

    route_tail = jnp.pad(
        route_rows.astype(jnp.bfloat16), ((0, 0), (0, -route_rows.shape[1] % 256))
    )
    carried = jnp.concatenate([own_rows(cotangent[0]), route_tail], axis=1)
    grad_pieces = all_steps(after(carried, out_parts), FSDP)

    def weight_packet(weights, earlier):
        packets = []
        for step in range(fsdp_count):
            index = ((fsdp_rank + step) % fsdp_count) * ctx_count + ctx_rank
            packet = jnp.stack([pick_block(weight, index) for weight in weights])
            if step:
                packet = after(packet, earlier)
                packet = rotated(packet, FSDP, step)
            packets.append(packet)
        return packets

    def whole_weights(packets):
        return [
            in_order([packet[kind] for packet in packets], FSDP).reshape(
                fsdp_count * slice_width, ff_width
            )
            for kind in range(packets[0].shape[0])
        ]

    wide_input = input_rows.astype(jnp.float32)
    normed_one, factor_one, first_hidden_state = rms_forward(wide_input, gain_one)
    query_matrix = jnp.dot(
        first_hidden_state, query_full, preferred_element_type=jnp.float32
    ).reshape(local_len, local_heads, HEAD_SIZE)
    key_value_rows = jnp.dot(
        first_hidden_state, key_value_weight, preferred_element_type=jnp.float32
    ).reshape(local_len, local_kv, 2, HEAD_SIZE)
    place_rows = positions[0]
    cosine_lookup, sine_lookup = rope_tables(place_rows, HEAD_SIZE)
    rotated_query = (
        apply_rotary(query_matrix, cosine_lookup, sine_lookup, 1.0)
        .astype(jnp.bfloat16)
        .reshape(local_len, local_kv, query_group_count, HEAD_SIZE)
    )
    k_rot = apply_rotary(key_value_rows[:, :, 0], cosine_lookup, sine_lookup, 1.0).astype(
        jnp.bfloat16
    )
    v_rows = key_value_rows[:, :, 1].astype(jnp.bfloat16)
    local_ids = jnp.arange(local_len, dtype=jnp.int32)
    query_ids = ctx_rank * local_len + local_ids
    query_starts = query_ids - place_rows
    kv_pack = jnp.concatenate([k_rot, v_rows], axis=-1)
    kv_blocks = [kv_pack]
    key_ids = [query_ids]
    for step in range(1, ctx_count):
        kv_blocks.append(shifted(kv_blocks[-1], CTX, 1))
        key_ids.append((ctx_rank - step) * local_len + local_ids)
    row_total = jnp.zeros((local_kv, query_group_count, local_len), jnp.float32)
    weighted = jnp.zeros((local_kv, query_group_count, local_len, HEAD_SIZE), jnp.float32)
    masks = []
    for block_index in range(ctx_count):
        allowed = attend_mask(query_ids, query_starts, key_ids[block_index])
        masks.append(allowed)
        key_rows = kv_blocks[block_index][..., :HEAD_SIZE]
        value_rows = kv_blocks[block_index][..., HEAD_SIZE:]
        scores = (
            jnp.einsum(
                TKGD_SKD_TO_KGTS, rotated_query, key_rows, preferred_element_type=jnp.float32
            )
            * factor
        )
        exp_scores = jnp.where(allowed[None, None], jnp.exp(scores), 0.0)
        row_total = row_total + jnp.sum(exp_scores, axis=-1)
        weighted = weighted + jnp.einsum(
            KGTS_SKD_TO_KGTD,
            exp_scores.astype(jnp.bfloat16),
            value_rows,
            preferred_element_type=jnp.float32,
        )
    head_out = (weighted / row_total[..., None]).astype(jnp.bfloat16)
    flat_heads = head_out.transpose(2, 0, 1, 3).reshape(local_len, local_heads * HEAD_SIZE)
    attn_part = jnp.dot(flat_heads, out_full, preferred_element_type=jnp.float32)

    attn_total = sum_over_tp(attn_part)
    residual = own_rows(input_rows).astype(jnp.float32) + attn_total
    normed_two, factor_two, hidden_two = rms_forward(residual, gain_two)
    hidden_pieces = all_steps(hidden_two, FSDP)
    grad_halves = [
        half.reshape(block_count, local_len, half.shape[-1])
        for half in spread(after(grad_pieces, hidden_two))
    ]
    hidden_halves = [
        half.reshape(block_count, local_len, half.shape[-1])
        for half in spread(hidden_pieces)
    ]
    tail_start = grad_halves[1].shape[-1] - route_tail.shape[1]
    routes_all = grad_halves[1][:, :, tail_start : tail_start + route_rows.shape[1]]
    routes_all = routes_all.astype(jnp.int32).reshape(-1, route_rows.shape[1])
    expert_ids = jnp.arange(expert_total, dtype=jnp.int32)
    chosen_all = jnp.any(routes_all[:, :, None] == expert_ids[None, None, :], axis=1)
    own_expert = tp_rank * block_count + fsdp_rank * ctx_count + ctx_rank
    member = jnp.any(routes_all == own_expert, axis=1).reshape(block_count, local_len)
    places = jnp.cumsum(member.astype(jnp.int32), axis=1) - 1
    slots = jnp.where(member, places, capacity)
    slot_ids = jnp.arange(capacity, dtype=jnp.int32)
    hot = slots[:, None, :] == slot_ids[None, :, None]
    hot_b = hot.astype(jnp.bfloat16)

    def take_rows(rows):
        return (
            jnp.einsum("bst,btd->bsd", hot_b, rows, preferred_element_type=jnp.float32)
            .astype(jnp.bfloat16)
            .reshape(block_count * capacity, rows.shape[2])
        )

    slot_chosen = take_rows(
        chosen_all.astype(jnp.bfloat16).reshape(block_count, local_len, expert_total)
    ).astype(jnp.float32)

    def put_rows(rows):
        stacked = rows.reshape(block_count, capacity, rows.shape[1])
        return (
            jnp.einsum("bst,bsd->btd", hot_b, stacked, preferred_element_type=jnp.float32)
            .astype(jnp.bfloat16)
            .reshape(
                (fsdp_count, ctx_count)
                + (2,) * len(tp_stages())
                + (own_len, rows.shape[1])
            )
        )

    first_packets = weight_packet((w_gate, w_up), hidden_pieces)
    down_packets = weight_packet((w_down,), hidden_pieces)
    hidden_halves, first_packets, down_packets = lax.optimization_barrier(
        (hidden_halves, first_packets, down_packets)
    )
    gate_weight, up_weight = whole_weights(first_packets)
    (down_weight,) = whole_weights(down_packets)
    own_chosen = jnp.any(route_rows[:, :, None] == expert_ids[None, None, :], axis=1)

    def exp_logits(hidden, chosen):
        logits = jnp.dot(hidden, router_full, preferred_element_type=jnp.float32)
        return jnp.where(chosen, jnp.exp(logits), 0.0)

    own_exp = exp_logits(hidden_two, own_chosen)
    own_gates = own_exp / jnp.sum(own_exp, axis=-1, keepdims=True)

    picked = jnp.concatenate([take_rows(half) for half in hidden_halves], axis=1)
    slot_exp = exp_logits(picked, slot_chosen > 0)
    slot_live = jnp.sum(slot_chosen, axis=1) > 0
    slot_total = jnp.where(slot_live, jnp.sum(slot_exp, axis=1), 1.0)
    slot_own = jnp.sum(jnp.where(expert_ids[None, :] == own_expert, slot_exp, 0.0), axis=1)
    scaled = jnp.where(slot_live, slot_own / slot_total, 0.0)
    gate_pre = jnp.dot(picked, gate_weight, preferred_element_type=jnp.float32)
    up_pre = jnp.dot(picked, up_weight, preferred_element_type=jnp.float32)
    activation = (jax.nn.silu(gate_pre) * up_pre).astype(jnp.bfloat16)
    result = jnp.einsum(CF_DF_TO_CD, activation, down_weight, preferred_element_type=jnp.float32)

    mixture_rows = (result * scaled[:, None]).astype(jnp.bfloat16)

    grad_rows = jnp.concatenate([take_rows(half) for half in grad_halves], axis=1)
    grad_rows = grad_rows[:, :model_width]
    grad_wide_rows = grad_rows.astype(jnp.float32)
    slot_grad = jnp.sum(grad_wide_rows * result, axis=1).reshape(block_count, capacity)
    out_grad = row_major((grad_wide_rows * scaled[:, None]).astype(jnp.bfloat16))
    act_grad = jnp.dot(out_grad, down_weight, preferred_element_type=jnp.float32)
    sigmoid_gate = jax.nn.sigmoid(gate_pre)
    gate_pre_grad = (
        act_grad * up_pre * sigmoid_gate * (1.0 + gate_pre * (1.0 - sigmoid_gate))
    ).astype(jnp.bfloat16)
    up_pre_grad = (act_grad * gate_pre * sigmoid_gate).astype(jnp.bfloat16)
    picked_grad = jnp.einsum(
        CF_DF_TO_CD, gate_pre_grad, gate_weight, preferred_element_type=jnp.float32
    ) + jnp.einsum(CF_DF_TO_CD, up_pre_grad, up_weight, preferred_element_type=jnp.float32)
    gate_grad_part = jnp.sum(jnp.where(hot, slot_grad[:, :, None], 0.0), axis=1)
    gate_grad = lax.all_to_all(
        gate_grad_part.reshape(block_count * tp_count, own_len), everywhere, 0, 0, tiled=True
    )
    gate_grad = (
        gate_grad.reshape(block_count, tp_count, own_len)
        .transpose(2, 1, 0)
        .reshape(own_len, expert_total)
    )
    back_parts = [put_rows(half) for half in halves(picked_grad.astype(jnp.bfloat16))]
    (back_parts, picked, gate_pre_grad, up_pre_grad, out_grad, activation, mixture_rows) = (
        lax.optimization_barrier(
            (
                back_parts,
                picked,
                gate_pre_grad,
                up_pre_grad,
                out_grad,
                activation,
                mixture_rows,
            )
        )
    )
    hidden_grad_sum = collect(back_parts)
    mixture = collect([put_rows(half) for half in halves(mixture_rows)])
    own_out = (residual + mixture).astype(jnp.bfloat16)

    def weight_grad(rows, columns):
        return (
            jnp.einsum("cd,cf->df", rows, columns, preferred_element_type=jnp.float32)
            .astype(jnp.bfloat16)
            .reshape(fsdp_count, slice_width, ff_width)
        )

    early_grads = [weight_grad(picked, rows) for rows in (gate_pre_grad, up_pre_grad)]
    late_grads = [weight_grad(out_grad, activation)]
    grad_packets = []
    for kinds in (early_grads, late_grads):
        packets = []
        for step in range(fsdp_count):
            target = (fsdp_rank + step) % fsdp_count
            packet = jnp.stack([pick_block(grad, target) for grad in kinds])
            if step:
                if len(grad_packets):
                    packet = after(packet, hidden_grad_sum)
                packet = rotated(packet, FSDP, step)
            packets.append(packet)
        grad_packets.append(packets)

    sel_grad = own_gates * (
        gate_grad - jnp.sum(own_gates * gate_grad, axis=-1, keepdims=True)
    )
    logit_grad = jnp.where(own_chosen, sel_grad, 0.0).astype(jnp.bfloat16)
    hidden_grad = hidden_grad_sum + jnp.einsum(
        TE_DE_TO_TD, logit_grad, router_full, preferred_element_type=jnp.float32
    )
    back_two, grad_ffn_gain = rms_backward(hidden_grad, normed_two, factor_two, gain_two)
    residual_grad = own_rows(cotangent[0]).astype(jnp.float32) + back_two
    row_pad = 16
    sent = jnp.concatenate(
        [
            residual_grad.astype(jnp.bfloat16),
            jnp.pad(grad_ffn_gain.astype(jnp.bfloat16)[None], ((0, row_pad - 1), (0, 0))),
        ],
        axis=0,
    )
    logit_tail = jnp.pad(logit_grad, ((0, row_pad), (0, -expert_total % 128)))
    sent = lax.all_gather(jnp.concatenate([sent, logit_tail], axis=1), TP, axis=0)
    residual_gradient_second = sent[:, :own_len, :model_width].reshape(local_len, model_width)
    logit_grad = sent[:, :own_len, model_width : model_width + expert_total].reshape(
        local_len, expert_total
    )
    grad_ffn_gain = jnp.sum(sent[:, own_len, :model_width].astype(jnp.float32), axis=0)
    own_block = fsdp_rank * ctx_count + ctx_rank
    block_hidden = jnp.concatenate(
        [pick_block(half, own_block) for half in hidden_halves], axis=1
    )
    grad_router = jnp.einsum(
        TD_TE_TO_DE, block_hidden, logit_grad, preferred_element_type=jnp.float32
    )

    grad_out_proj = jnp.einsum(
        "td,ti->di", residual_gradient_second, flat_heads, preferred_element_type=jnp.float32
    )
    early = jnp.concatenate([grad_out_proj, grad_router, grad_ffn_gain[:, None]], axis=1)
    early = jnp.pad(early, ((0, 0), (0, -early.shape[1] % 128))).astype(jnp.bfloat16)
    early = early.reshape(fsdp_count, slice_width, early.shape[1])
    early_parts = scatter_start(early)
    per_head_gradient = jnp.einsum(
        TD_ID_TO_TI, residual_gradient_second, out_full, preferred_element_type=jnp.float32
    ).astype(jnp.bfloat16)
    per_head_gradient = per_head_gradient.reshape(
        local_len, local_kv, query_group_count, HEAD_SIZE
    ).transpose(1, 2, 0, 3)
    row_delta = jnp.sum(
        per_head_gradient.astype(jnp.float32) * head_out.astype(jnp.float32), axis=-1
    )
    log_total = jnp.log(row_total)
    query_grad = jnp.zeros((local_len, local_kv, query_group_count, HEAD_SIZE), jnp.float32)
    kv_grads = []
    for block_index in range(ctx_count):
        key_rows = kv_blocks[block_index][..., :HEAD_SIZE]
        value_rows = kv_blocks[block_index][..., HEAD_SIZE:]
        scores = (
            jnp.einsum(
                TKGD_SKD_TO_KGTS, rotated_query, key_rows, preferred_element_type=jnp.float32
            )
            * factor
        )
        probability = jnp.where(
            masks[block_index][None, None], jnp.exp(scores - log_total[..., None]), 0.0
        )
        prob_grad = jnp.einsum(
            KGTD_SKD_TO_KGTS, per_head_gradient, value_rows, preferred_element_type=jnp.float32
        )
        score_grad = (probability * (prob_grad - row_delta[..., None]) * factor).astype(
            jnp.bfloat16
        )
        query_grad = query_grad + jnp.einsum(
            KGTS_SKD_TO_TKGD, score_grad, key_rows, preferred_element_type=jnp.float32
        )
        key_grad = jnp.einsum(
            KGTS_TKGD_TO_SKD, score_grad, rotated_query, preferred_element_type=jnp.float32
        )
        value_gradient = jnp.einsum(
            KGTS_KGTD_TO_SKD,
            probability.astype(jnp.bfloat16),
            per_head_gradient,
            preferred_element_type=jnp.float32,
        )
        kv_grads.append(jnp.concatenate([key_grad, value_gradient], axis=-1))
    weight_shape = (fsdp_count, ctx_count, slice_width, ff_width)
    weight_outs = [jnp.zeros(weight_shape, jnp.float32) for _ in range(3)]
    weight_hops = []
    for step in range(fsdp_count):
        early_hops = all_steps(grad_packets[0][step], CTX)
        late_hops = all_steps(grad_packets[1][step], CTX)
        weight_hops.append((early_hops, late_hops))
    kv_grad_total = kv_grads[0]
    for step in range(1, ctx_count):
        returning = shifted(kv_grads[step].astype(jnp.bfloat16), CTX, -step)
        kv_grad_total = kv_grad_total + returning.astype(jnp.float32)
    key_backward_rows = apply_rotary(
        kv_grad_total[..., :HEAD_SIZE], cosine_lookup, sine_lookup, -1.0
    )
    key_value_backward = (
        jnp.stack([key_backward_rows, kv_grad_total[..., HEAD_SIZE:]], axis=2)
        .astype(jnp.bfloat16)
        .reshape(local_len, kv_width)
    )
    query_back = (
        apply_rotary(
            query_grad.reshape(local_len, local_heads, HEAD_SIZE), cosine_lookup, sine_lookup, -1.0
        )
        .astype(jnp.bfloat16)
        .reshape(local_len, head_width)
    )
    both_back = jnp.concatenate([query_back, key_value_backward], axis=1)
    hidden_one_part = jnp.einsum(
        TF_DF_TO_TD, both_back, both_weight, preferred_element_type=jnp.float32
    )
    grad_attn_gain = jnp.sum(hidden_one_part * normed_one, axis=0)
    projection_grad = jnp.einsum(
        TD_TF_TO_DF, first_hidden_state, both_back, preferred_element_type=jnp.float32
    )
    projection_grad = projection_grad.astype(jnp.bfloat16).reshape(
        fsdp_count, slice_width, both_width
    )
    projection_parts = scatter_start(projection_grad)
    summed = sum_over_tp(hidden_one_part, grad_attn_gain)
    hidden_one_grad = summed[:own_len]
    grad_attn_gain = summed[own_len].astype(jnp.bfloat16).reshape(fsdp_count, 1, slice_width)
    gain_parts = scatter_start(grad_attn_gain)
    grad_attn_gain = scatter_finish(gain_parts)[0]
    early_total = scatter_finish(after(early_parts, hidden_one_grad))
    out_rows = lax.all_gather(own_out, TP, axis=0, tiled=True)
    projection_total = scatter_finish(after(projection_parts, (hidden_one_grad, out_rows)))
    for step in range(fsdp_count):
        for hops, kinds in zip(weight_hops[step], ((0, 1), (2,))):
            for hop, seen in enumerate(hops):
                seen = after(seen, hidden_one_part)
                place = ((fsdp_rank - step) % fsdp_count, (ctx_rank - hop) % ctx_count, 0, 0)
                for number, kind in enumerate(kinds):
                    weight_outs[kind] = lax.dynamic_update_slice(
                        weight_outs[kind], seen[number].astype(jnp.float32)[None, None], place
                    )
    weight_outs = [
        grad.reshape(fsdp_count * ctx_count, slice_width, ff_width) for grad in weight_outs
    ]
    back_one, _ = rms_backward(
        hidden_one_grad, own_rows(normed_one), own_rows(factor_one), gain_one
    )
    input_grad = residual_grad + back_one
    input_grad = lax.all_gather(
        after(input_grad.astype(jnp.bfloat16), gain_parts), TP, axis=0, tiled=True
    )
    return (
        out_rows[None],
        input_grad.astype(jnp.float32)[None],
        grad_attn_gain,
        projection_total[:, :head_width],
        projection_total[:, head_width:].reshape(key_value_projection.shape),
        early_total[:, :head_width].T,
        early_total[:, head_width + expert_total],
        early_total[:, head_width : head_width + expert_total],
        weight_outs[0],
        weight_outs[1],
        weight_outs[2],
    )


def local_any(*args):
    devices = math.prod(lax.axis_size(name) for name in (FSDP, CTX, TP))
    if args[9].shape[1] != devices:
        return local(*args)
    return local_spread(*args)


def solution(mesh):

    return jax.shard_map(
        local_any,
        mesh=mesh,
        in_specs=(
            P(FSDP, CTX, None),
            P(FSDP, CTX, None),
            P(FSDP, CTX),
            P(FSDP, CTX, None),
            P(FSDP),
            P(FSDP, TP),
            P(FSDP, TP, None, None),
            P(TP, FSDP),
            P(FSDP),
            P(FSDP, None),
            P(TP, FSDP, None),
            P(TP, FSDP, None),
            P(TP, FSDP, None),
        ),
        out_specs=(
            P(FSDP, CTX, None),
            P(FSDP, CTX, None),
            P(FSDP),
            P(FSDP, TP),
            P(FSDP, TP, None, None),
            P(TP, FSDP),
            P(FSDP),
            P(FSDP, None),
            P(TP, FSDP, None),
            P(TP, FSDP, None),
            P(TP, FSDP, None),
        ),
        check_vma=False,
    )
```

```python
import math

import jax
import jax.numpy as jnp
from jax import lax
from jax.experimental import pallas as pl
from jax.experimental.pallas import tpu as pltpu
from jax.experimental.layout import Layout, with_layout_constraint
from jax.sharding import PartitionSpec as P

CF_DF_TO_CD = "cf,df->cd"
CTX = "ctx"
ECD_ECF_TO_EDF = "ecd,ecf->edf"
ECD_EDF_TO_ECF = "ecd,edf->ecf"
ECF_EDF_TO_ECD = "ecf,edf->ecd"
FSDP = "fsdp"
KGTD_SKD_TO_KGTS = "kgtd,skd->kgts"
KGTS_KGTD_TO_SKD = "kgts,kgtd->skd"
KGTS_SKD_TO_KGTD = "kgts,skd->kgtd"
KGTS_SKD_TO_TKGD = "kgts,skd->tkgd"
KGTS_TKGD_TO_SKD = "kgts,tkgd->skd"
TD_ID_TO_TI = "td,id->ti"
TD_TE_TO_DE = "td,te->de"
TD_TF_TO_DF = "td,tf->df"
TE_DE_TO_TD = "te,de->td"
TF_DF_TO_TD = "tf,df->td"
TKGD_SKD_TO_KGTS = "tkgd,skd->kgts"
TP = "tp"


QUERY_HEADS = 16
KEY_VALUE_HEADS = 8
HEAD_SIZE = 64


EPS = 1e-06
THETA = 10000.0


def shifted(block, axis, distance):
    devices = range(lax.axis_size(axis))
    route = [(i - distance, i) for i in devices if i - distance in devices]
    return lax.ppermute(block, axis, route)


def rope_tables(place_rows, head_width):
    half_width = head_width // 2
    inverse = THETA ** (-2.0 * jnp.arange(half_width, dtype=jnp.float32) / head_width)
    angle = place_rows.astype(jnp.float32)[:, None] * inverse[None, :]
    return (jnp.cos(angle)[:, None, :], jnp.sin(angle)[:, None, :])


def apply_rotary(vector, cosine_lookup, sine_lookup, direction):
    half_width = vector.shape[-1] // 2
    first_half = vector[..., :half_width]
    second_half = vector[..., half_width:]
    return jnp.concatenate(
        [
            first_half * cosine_lookup - direction * second_half * sine_lookup,
            direction * first_half * sine_lookup + second_half * cosine_lookup,
        ],
        axis=-1,
    )


def rms_forward(wide_rows, gain_vector):
    factor = lax.rsqrt(jnp.mean(wide_rows * wide_rows, axis=-1, keepdims=True) + EPS)
    normed = wide_rows * factor
    return (normed, factor, (normed * gain_vector.astype(jnp.float32)).astype(jnp.bfloat16))


def rms_backward(gradient, normed, factor, gain_vector):
    gain_grad = jnp.sum(gradient * normed, axis=0)
    inner_term = gradient * gain_vector.astype(jnp.float32)
    back_term = factor * (
        inner_term - normed * jnp.mean(inner_term * normed, axis=-1, keepdims=True)
    )
    return (back_term, gain_grad)


def attend_mask(query_ids, query_starts, key_ids):
    return (key_ids[None, :] <= query_ids[:, None]) & (key_ids[None, :] >= query_starts[:, None])


def router_gates(logits, picks):
    selected = jnp.sum(jnp.where(picks, logits[:, None, :], 0.0), axis=-1)
    exp_sel = jnp.exp(selected)
    return exp_sel / jnp.sum(exp_sel, axis=-1, keepdims=True)


def slot_tables(route_rows, gate_weights, first_expert, expert_count, capacity):
    token_count = route_rows.shape[0]
    owners = first_expert + jnp.arange(expert_count, dtype=jnp.int32)
    hit_mask = route_rows[:, :, None] == owners[None, None, :]
    member = jnp.sum(hit_mask.astype(jnp.int32), axis=1)
    weight_rows = jnp.sum(jnp.where(hit_mask, gate_weights[:, :, None], 0.0), axis=1)
    places = jnp.cumsum(member, axis=0) - 1
    expert_ids = jnp.arange(expert_count, dtype=jnp.int32)
    slot_ids = jnp.where(
        member > 0, expert_ids[None, :] * capacity + places, expert_count * capacity
    )
    flat_slots = slot_ids.reshape(-1)
    token_ids = jnp.broadcast_to(
        jnp.arange(token_count, dtype=jnp.int32)[:, None], (token_count, expert_count)
    ).reshape(-1)
    source = jnp.zeros((expert_count * capacity + 1,), jnp.int32).at[flat_slots].set(token_ids)[:-1]
    scaled = (
        jnp.zeros((expert_count * capacity + 1,), jnp.float32)
        .at[flat_slots]
        .set(weight_rows.reshape(-1))[:-1]
    )
    return (hit_mask, slot_ids, source, scaled)


def expert_forward(hidden, source, w_gate, w_up, w_down, expert_count, capacity):
    picked = hidden[source].reshape(expert_count, capacity, hidden.shape[1])
    gate_pre = jnp.einsum(ECD_EDF_TO_ECF, picked, w_gate, preferred_element_type=jnp.float32)
    up_pre = jnp.einsum(ECD_EDF_TO_ECF, picked, w_up, preferred_element_type=jnp.float32)
    activation = (jax.nn.silu(gate_pre) * up_pre).astype(jnp.bfloat16)
    result = jnp.einsum(ECF_EDF_TO_ECD, activation, w_down, preferred_element_type=jnp.float32)
    return (picked, gate_pre, up_pre, activation, result)


def combine(result, source, scaled, token_count):
    model_width = result.shape[-1]
    flat_result = result.reshape(-1, model_width)
    return (
        jnp.zeros((token_count, model_width), jnp.float32)
        .at[source]
        .add(flat_result * scaled[:, None])
    )


def expert_backward(
    grad_rows,
    hit_mask,
    slot_ids,
    source,
    scaled,
    saved,
    w_gate,
    w_up,
    w_down,
    expert_count,
    capacity,
    token_count,
):
    picked, gate_pre, up_pre, activation, result = saved
    model_width = grad_rows.shape[1]
    slot_grad = jnp.sum(grad_rows * result.reshape(expert_count * capacity, model_width), axis=1)
    padded = jnp.concatenate([slot_grad, jnp.zeros((1,), jnp.float32)])
    per_expert = padded[slot_ids]
    gate_grad = jnp.sum(jnp.where(hit_mask, per_expert[:, None, :], 0.0), axis=2)
    out_grad = (
        (grad_rows * scaled[:, None])
        .astype(jnp.bfloat16)
        .reshape(expert_count, capacity, model_width)
    )
    grad_down = jnp.einsum(ECD_ECF_TO_EDF, out_grad, activation, preferred_element_type=jnp.float32)
    act_grad = jnp.einsum(ECD_EDF_TO_ECF, out_grad, w_down, preferred_element_type=jnp.float32)
    sigmoid_gate = jax.nn.sigmoid(gate_pre)
    gate_pre_grad = (
        act_grad * up_pre * sigmoid_gate * (1.0 + gate_pre * (1.0 - sigmoid_gate))
    ).astype(jnp.bfloat16)
    up_pre_grad = (act_grad * gate_pre * sigmoid_gate).astype(jnp.bfloat16)
    grad_gate = jnp.einsum(
        ECD_ECF_TO_EDF, picked, gate_pre_grad, preferred_element_type=jnp.float32
    )
    grad_up = jnp.einsum(ECD_ECF_TO_EDF, picked, up_pre_grad, preferred_element_type=jnp.float32)
    picked_grad = jnp.einsum(
        ECF_EDF_TO_ECD, gate_pre_grad, w_gate, preferred_element_type=jnp.float32
    ) + jnp.einsum(ECF_EDF_TO_ECD, up_pre_grad, w_up, preferred_element_type=jnp.float32)
    hidden_grad = (
        jnp.zeros((token_count, model_width), jnp.float32)
        .at[source]
        .add(picked_grad.reshape(-1, model_width))
    )
    return (gate_grad, hidden_grad, grad_gate, grad_up, grad_down)


def local(
    tokens,
    cotangent,
    positions,
    routes,
    attn_gain,
    w_query,
    key_value_projection,
    output_projection_weight,
    ffn_gain,
    w_router,
    w_gate,
    w_up,
    w_down,
):
    gain_one, gain_two, query_full, keyval_full, out_full, router_full = (
        lax.all_gather(attn_gain, FSDP, axis=0, tiled=True),
        lax.all_gather(ffn_gain, FSDP, axis=0, tiled=True),
        lax.all_gather(w_query, FSDP, axis=0, tiled=True),
        lax.all_gather(key_value_projection, FSDP, axis=0, tiled=True),
        lax.all_gather(output_projection_weight, FSDP, axis=1, tiled=True),
        lax.all_gather(w_router, FSDP, axis=0, tiled=True),
    )
    expert_full = (
        lax.all_gather(w_gate, FSDP, axis=1, tiled=True),
        lax.all_gather(w_up, FSDP, axis=1, tiled=True),
        lax.all_gather(w_down, FSDP, axis=1, tiled=True),
    )
    input_rows = tokens[0]
    local_len = input_rows.shape[0]
    model_width = input_rows.shape[1]
    query_group_count = QUERY_HEADS // KEY_VALUE_HEADS
    local_heads = w_query.shape[1] // HEAD_SIZE
    local_kv = local_heads // query_group_count
    expert_count = w_gate.shape[0]
    capacity = local_len // 2
    ctx_count = lax.axis_size(CTX)
    ctx_rank = lax.axis_index(CTX)
    factor = 1.0 / math.sqrt(HEAD_SIZE)
    key_value_weight = keyval_full.reshape(model_width, local_kv * 2 * HEAD_SIZE)
    wide_input = input_rows.astype(jnp.float32)
    normed_one, factor_one, first_hidden_state = rms_forward(wide_input, gain_one)
    query_matrix = jnp.dot(
        first_hidden_state, query_full, preferred_element_type=jnp.float32
    ).reshape(local_len, local_heads, HEAD_SIZE)
    key_value_rows = jnp.dot(
        first_hidden_state, key_value_weight, preferred_element_type=jnp.float32
    ).reshape(local_len, local_kv, 2, HEAD_SIZE)
    place_rows = positions[0]
    cosine_lookup, sine_lookup = rope_tables(place_rows, HEAD_SIZE)
    rotated_query = (
        apply_rotary(query_matrix, cosine_lookup, sine_lookup, 1.0)
        .astype(jnp.bfloat16)
        .reshape(local_len, local_kv, query_group_count, HEAD_SIZE)
    )
    k_rot = apply_rotary(key_value_rows[:, :, 0], cosine_lookup, sine_lookup, 1.0).astype(
        jnp.bfloat16
    )
    v_rows = key_value_rows[:, :, 1].astype(jnp.bfloat16)
    local_ids = jnp.arange(local_len, dtype=jnp.int32)
    query_ids = ctx_rank * local_len + local_ids
    query_starts = query_ids - place_rows
    kv_pack = jnp.concatenate([k_rot, v_rows], axis=-1)
    kv_blocks = [kv_pack]
    key_ids = [query_ids]
    travelling = kv_pack
    cycle_step = 1
    travelling = shifted(travelling, CTX, 1)
    kv_blocks.append(travelling)
    key_ids.append((ctx_rank - cycle_step) * local_len + local_ids)
    row_total = jnp.zeros((local_kv, query_group_count, local_len), jnp.float32)
    weighted = jnp.zeros((local_kv, query_group_count, local_len, HEAD_SIZE), jnp.float32)
    masks = []
    for block_index in range(ctx_count):
        allowed = attend_mask(query_ids, query_starts, key_ids[block_index])
        masks.append(allowed)
        key_rows = kv_blocks[block_index][..., :HEAD_SIZE]
        value_rows = kv_blocks[block_index][..., HEAD_SIZE:]
        scores = (
            jnp.einsum(
                TKGD_SKD_TO_KGTS, rotated_query, key_rows, preferred_element_type=jnp.float32
            )
            * factor
        )
        exp_scores = jnp.where(allowed[None, None], jnp.exp(scores), 0.0)
        row_total = row_total + jnp.sum(exp_scores, axis=-1)
        weighted = weighted + jnp.einsum(
            KGTS_SKD_TO_KGTD,
            exp_scores.astype(jnp.bfloat16),
            value_rows,
            preferred_element_type=jnp.float32,
        )
    head_out = (weighted / row_total[..., None]).astype(jnp.bfloat16)
    flat_heads = head_out.transpose(2, 0, 1, 3).reshape(local_len, local_heads * HEAD_SIZE)
    attn_part = jnp.dot(flat_heads, out_full, preferred_element_type=jnp.float32)
    residual = wide_input + lax.psum(attn_part, TP)
    normed_two, factor_two, hidden_two = rms_forward(residual, gain_two)
    logits = jnp.dot(hidden_two, router_full, preferred_element_type=jnp.float32)
    route_rows = routes[0]
    picks = (
        route_rows[:, :, None] == jnp.arange(router_full.shape[1], dtype=jnp.int32)[None, None, :]
    )
    gate_weights = router_gates(logits, picks)
    first_expert = lax.axis_index(TP) * expert_count
    hit_mask, slot_ids, source, scaled = slot_tables(
        route_rows, gate_weights, first_expert, expert_count, capacity
    )
    saved = expert_forward(
        hidden_two, source, expert_full[0], expert_full[1], expert_full[2], expert_count, capacity
    )
    mixture_part = combine(saved[4], source, scaled, local_len)
    mixture = lax.psum(mixture_part.astype(jnp.bfloat16), TP).astype(jnp.float32)
    out_rows = (residual + mixture).astype(jnp.bfloat16)
    grad_wide = cotangent[0].astype(jnp.float32)
    back_weights = (
        lax.all_gather(w_gate, FSDP, axis=1, tiled=True),
        lax.all_gather(w_up, FSDP, axis=1, tiled=True),
        lax.all_gather(w_down, FSDP, axis=1, tiled=True),
    )
    grad_rows = grad_wide[source]
    gate_grad_part, hidden_grad_part, grad_gate, grad_up, grad_down = expert_backward(
        grad_rows,
        hit_mask,
        slot_ids,
        source,
        scaled,
        saved,
        back_weights[0],
        back_weights[1],
        back_weights[2],
        expert_count,
        capacity,
        local_len,
    )
    hidden_grad_sum, gate_grad = lax.psum((hidden_grad_part, gate_grad_part), TP)
    sel_grad = gate_weights * (
        gate_grad - jnp.sum(gate_weights * gate_grad, axis=-1, keepdims=True)
    )
    logit_grad = jnp.sum(jnp.where(picks, sel_grad[:, :, None], 0.0), axis=1).astype(jnp.bfloat16)
    grad_router = jnp.einsum(
        TD_TE_TO_DE, hidden_two, logit_grad, preferred_element_type=jnp.float32
    )
    hidden_grad = hidden_grad_sum + jnp.einsum(
        TE_DE_TO_TD, logit_grad, router_full, preferred_element_type=jnp.float32
    )
    back_two, grad_ffn_gain = rms_backward(hidden_grad, normed_two, factor_two, gain_two)
    residual_grad = grad_wide + back_two
    residual_gradient_second = residual_grad.astype(jnp.bfloat16)
    grad_out_proj = jnp.einsum(
        "ti,td->id", flat_heads, residual_gradient_second, preferred_element_type=jnp.float32
    )
    per_head_gradient = jnp.einsum(
        TD_ID_TO_TI, residual_gradient_second, out_full, preferred_element_type=jnp.float32
    ).astype(jnp.bfloat16)
    per_head_gradient = per_head_gradient.reshape(
        local_len, local_kv, query_group_count, HEAD_SIZE
    ).transpose(1, 2, 0, 3)
    row_delta = jnp.sum(
        per_head_gradient.astype(jnp.float32) * head_out.astype(jnp.float32), axis=-1
    )
    log_total = jnp.log(row_total)
    query_grad = jnp.zeros((local_len, local_kv, query_group_count, HEAD_SIZE), jnp.float32)
    kv_grads = []
    for block_index in range(ctx_count):
        key_rows = kv_blocks[block_index][..., :HEAD_SIZE]
        value_rows = kv_blocks[block_index][..., HEAD_SIZE:]
        scores = (
            jnp.einsum(
                TKGD_SKD_TO_KGTS, rotated_query, key_rows, preferred_element_type=jnp.float32
            )
            * factor
        )
        probability = jnp.where(
            masks[block_index][None, None], jnp.exp(scores - log_total[..., None]), 0.0
        )
        prob_grad = jnp.einsum(
            KGTD_SKD_TO_KGTS, per_head_gradient, value_rows, preferred_element_type=jnp.float32
        )
        score_grad = (probability * (prob_grad - row_delta[..., None]) * factor).astype(
            jnp.bfloat16
        )
        query_grad = query_grad + jnp.einsum(
            KGTS_SKD_TO_TKGD, score_grad, key_rows, preferred_element_type=jnp.float32
        )
        key_grad = jnp.einsum(
            KGTS_TKGD_TO_SKD, score_grad, rotated_query, preferred_element_type=jnp.float32
        )
        value_gradient = jnp.einsum(
            KGTS_KGTD_TO_SKD,
            probability.astype(jnp.bfloat16),
            per_head_gradient,
            preferred_element_type=jnp.float32,
        )
        kv_grads.append(jnp.concatenate([key_grad, value_gradient], axis=-1))
    cycle_step = 1
    returning = shifted(kv_grads[cycle_step].astype(jnp.bfloat16), CTX, -1).astype(jnp.float32)
    kv_grad_total = kv_grads[0] + returning
    key_backward_rows = apply_rotary(
        kv_grad_total[..., :HEAD_SIZE], cosine_lookup, sine_lookup, -1.0
    )
    key_value_backward = (
        jnp.stack([key_backward_rows, kv_grad_total[..., HEAD_SIZE:]], axis=2)
        .astype(jnp.bfloat16)
        .reshape(local_len, local_kv * 2 * HEAD_SIZE)
    )
    query_back = (
        apply_rotary(
            query_grad.reshape(local_len, local_heads, HEAD_SIZE), cosine_lookup, sine_lookup, -1.0
        )
        .astype(jnp.bfloat16)
        .reshape(local_len, local_heads * HEAD_SIZE)
    )
    grad_query = jnp.einsum(
        TD_TF_TO_DF, first_hidden_state, query_back, preferred_element_type=jnp.float32
    )
    key_value_gradient = jnp.einsum(
        TD_TF_TO_DF, first_hidden_state, key_value_backward, preferred_element_type=jnp.float32
    ).reshape(model_width, local_kv, 2, HEAD_SIZE)
    hidden_one_part = jnp.einsum(
        TF_DF_TO_TD, query_back, query_full, preferred_element_type=jnp.float32
    ) + jnp.einsum(
        TF_DF_TO_TD, key_value_backward, key_value_weight, preferred_element_type=jnp.float32
    )
    hidden_one_grad = lax.psum(hidden_one_part.astype(jnp.bfloat16), TP).astype(jnp.float32)
    back_one, grad_attn_gain = rms_backward(hidden_one_grad, normed_one, factor_one, gain_one)
    input_grad = residual_grad + back_one
    shards = (
        lax.psum_scatter(
            grad_attn_gain.astype(jnp.bfloat16), FSDP, scatter_dimension=0, tiled=True
        ).astype(jnp.float32),
        lax.psum_scatter(
            grad_ffn_gain.astype(jnp.bfloat16), FSDP, scatter_dimension=0, tiled=True
        ).astype(jnp.float32),
        lax.psum_scatter(
            grad_query.astype(jnp.bfloat16), FSDP, scatter_dimension=0, tiled=True
        ).astype(jnp.float32),
        lax.psum_scatter(
            key_value_gradient.astype(jnp.bfloat16), FSDP, scatter_dimension=0, tiled=True
        ).astype(jnp.float32),
        lax.psum_scatter(
            grad_out_proj.astype(jnp.bfloat16), FSDP, scatter_dimension=1, tiled=True
        ).astype(jnp.float32),
        lax.psum_scatter(
            grad_router.astype(jnp.bfloat16), FSDP, scatter_dimension=0, tiled=True
        ).astype(jnp.float32),
    )
    piece_gate, piece_up, piece_down = (
        lax.psum_scatter(
            grad_gate.astype(jnp.bfloat16), (FSDP, CTX), scatter_dimension=1, tiled=True
        ).astype(jnp.float32),
        lax.psum_scatter(
            grad_up.astype(jnp.bfloat16), (FSDP, CTX), scatter_dimension=1, tiled=True
        ).astype(jnp.float32),
        lax.psum_scatter(
            grad_down.astype(jnp.bfloat16), (FSDP, CTX), scatter_dimension=1, tiled=True
        ).astype(jnp.float32),
    )
    expert_totals = (
        lax.all_gather(piece_gate.astype(jnp.bfloat16), CTX, axis=1, tiled=True).astype(
            piece_gate.dtype
        ),
        lax.all_gather(piece_up.astype(jnp.bfloat16), CTX, axis=1, tiled=True).astype(
            piece_up.dtype
        ),
        lax.all_gather(piece_down.astype(jnp.bfloat16), CTX, axis=1, tiled=True).astype(
            piece_down.dtype
        ),
    )
    small_totals = (
        lax.psum(shards[0].astype(jnp.bfloat16), CTX).astype(jnp.float32),
        lax.psum(shards[1].astype(jnp.bfloat16), CTX).astype(jnp.float32),
        lax.psum(shards[2].astype(jnp.bfloat16), CTX).astype(jnp.float32),
        lax.psum(shards[3].astype(jnp.bfloat16), CTX).astype(jnp.float32),
        lax.psum(shards[4].astype(jnp.bfloat16), CTX).astype(jnp.float32),
        lax.psum(shards[5].astype(jnp.bfloat16), CTX).astype(jnp.float32),
    )
    return (
        out_rows[None],
        input_grad[None],
        small_totals[0],
        small_totals[2],
        small_totals[3],
        small_totals[4],
        small_totals[1],
        small_totals[5],
        expert_totals[0],
        expert_totals[1],
        expert_totals[2],
    )


def rotated(block, axis, distance):
    count = lax.axis_size(axis)
    return lax.ppermute(block, axis, [(i, (i + distance) % count) for i in range(count)])


def pick_block(stacked, index):
    return lax.dynamic_index_in_dim(stacked, index, 0, keepdims=False)


def sum_over_tp(part, shared=None):
    count = lax.axis_size(TP)
    pieces = part.astype(jnp.bfloat16).reshape(count, part.shape[0] // count, part.shape[1])
    if shared is not None:
        shared = jnp.pad(shared.astype(jnp.bfloat16)[None, None], ((0, 0), (0, 15), (0, 0)))
        shared = jnp.broadcast_to(shared, (count,) + shared.shape[1:])
        pieces = jnp.concatenate([pieces, shared], axis=1)
    pieces = lax.all_to_all(pieces, TP, 0, 0, tiled=True)
    return jnp.sum(pieces.astype(jnp.float32), axis=0)


def row_major(rows):
    return with_layout_constraint(rows, Layout(major_to_minor=tuple(range(rows.ndim))))


def after(value, earlier):
    return lax.optimization_barrier((value, earlier))[0]


def in_order(pieces, axis, place=0):
    count = lax.axis_size(axis)
    rank = lax.axis_index(axis)
    shape = pieces[0].shape
    whole = jnp.zeros(shape[:place] + (count,) + shape[place:], pieces[0].dtype)
    for step in range(count):
        whole = lax.dynamic_update_index_in_dim(
            whole, pieces[step], (rank - step) % count, place
        )
    return whole


def all_steps(block, axis):
    return [block] + [rotated(block, axis, step) for step in range(1, lax.axis_size(axis))]


def tp_partner(block, distance):
    count = lax.axis_size(TP)
    return lax.ppermute(block, TP, [(i, i ^ distance) for i in range(count)])


def tp_stages():
    distances = []
    distance = lax.axis_size(TP) // 2
    while distance:
        distances.append(distance)
        distance //= 2
    return distances


def spread(pieces):
    far, *near = tp_stages()
    result = []
    for flip, block in enumerate(halves(in_order(pieces, FSDP))):
        done = [FSDP]
        for stage in ([far, CTX] if flip else [CTX, far]) + near:
            place = sum(1 for other in done if rank_of(other) < rank_of(stage))
            if isinstance(stage, str):
                pieces = all_steps(block, stage)
            else:
                pieces = [block, tp_partner(block, stage)]
            if isinstance(stage, str):
                block = in_order(pieces, stage, place)
            else:
                bit = (lax.axis_index(TP) // stage) % 2
                shape = block.shape
                whole = jnp.zeros(shape[:place] + (2,) + shape[place:], block.dtype)
                whole = lax.dynamic_update_index_in_dim(whole, pieces[0], bit, place)
                block = lax.dynamic_update_index_in_dim(whole, pieces[1], 1 - bit, place)
            done.append(stage)
        result.append(block)
    return result


def rank_of(stage):
    return {FSDP: 0, CTX: 1}[stage] if isinstance(stage, str) else 2 + 1.0 / stage


def collect(parts, ready=None):
    far, *near = tp_stages()
    summed = []
    for flip, stacked in enumerate(parts):
        stages = list(reversed(near)) + ([CTX, far] if flip else [far, CTX])
        left = sorted(stages + [FSDP], key=rank_of)
        for stage in stages:
            place = left.index(stage)
            left.remove(stage)
            if isinstance(stage, str):
                count = lax.axis_size(stage)
                rank = lax.axis_index(stage)
                pieces = [lax.dynamic_index_in_dim(stacked, rank, place, keepdims=False)]
                for step in range(1, count):
                    leaving = lax.dynamic_index_in_dim(
                        stacked, (rank + step) % count, place, keepdims=False
                    )
                    pieces.append(rotated(leaving, stage, step))
            else:
                bit = (lax.axis_index(TP) // stage) % 2
                leaving = lax.dynamic_index_in_dim(stacked, 1 - bit, place, keepdims=False)
                pieces = [
                    lax.dynamic_index_in_dim(stacked, bit, place, keepdims=False),
                    tp_partner(leaving, stage),
                ]
            total = sum(piece.astype(jnp.float32) for piece in pieces)
            stacked = total.astype(jnp.bfloat16)
        summed.append(stacked)
    pieces = scatter_start(jnp.concatenate(summed, axis=-1))
    if ready is not None:
        pieces = after(pieces, ready)
    return sum(piece.astype(jnp.float32) for piece in pieces)


def assemble(pieces, places):
    kinds, rows, columns = pieces[0].shape
    count = len(pieces)

    def kernel(places_ref, *refs):
        for number in range(count):

            @pl.when(pl.program_id(0) == number)
            def _():
                for kind in range(kinds):
                    refs[count + kind][0] = refs[number][kind].astype(jnp.float32)

    size = kinds * count * rows * columns
    return pl.pallas_call(
        kernel,
        out_shape=[jax.ShapeDtypeStruct((count, rows, columns), jnp.float32)] * kinds,
        grid_spec=pltpu.PrefetchScalarGridSpec(
            num_scalar_prefetch=1,
            grid=(count,),
            in_specs=[pl.BlockSpec((kinds, rows, columns), lambda i, p: (0, 0, 0))] * count,
            out_specs=[pl.BlockSpec((1, rows, columns), lambda i, p: (p[i], 0, 0))] * kinds,
        ),
        cost_estimate=pl.CostEstimate(flops=size, bytes_accessed=6 * size, transcendentals=0),
    )(places, *pieces)


def halves(rows):
    width = rows.shape[-1] // 2
    return rows[..., :width], rows[..., width:]


def scatter_start(stacked):
    count = lax.axis_size(FSDP)
    rank = lax.axis_index(FSDP)
    pieces = [pick_block(stacked, rank)]
    for step in range(1, count):
        pieces.append(rotated(pick_block(stacked, (rank + step) % count), FSDP, step))
    return pieces


def scatter_finish(pieces):
    total = sum(piece.astype(jnp.float32) for piece in pieces)
    sent = total.astype(jnp.bfloat16)
    for step in range(1, lax.axis_size(CTX)):
        total = total + rotated(sent, CTX, step).astype(jnp.float32)
    return total


def local_spread(
    tokens,
    cotangent,
    positions,
    routes,
    attn_gain,
    w_query,
    key_value_projection,
    output_projection_weight,
    ffn_gain,
    w_router,
    w_gate,
    w_up,
    w_down,
):
    everywhere = (FSDP, CTX, TP)
    fsdp_count, ctx_count, tp_count = (lax.axis_size(name) for name in everywhere)
    fsdp_rank, ctx_rank, tp_rank = (lax.axis_index(name) for name in everywhere)
    input_rows = tokens[0]
    local_len, model_width = input_rows.shape
    slice_width = w_query.shape[0]
    own_len = local_len // tp_count
    block_count = fsdp_count * ctx_count
    expert_total = w_router.shape[1]
    ff_width = w_gate.shape[2]
    query_group_count = QUERY_HEADS // KEY_VALUE_HEADS
    head_width = w_query.shape[1]
    local_heads = head_width // HEAD_SIZE
    local_kv = local_heads // query_group_count
    capacity = local_len // 2
    factor = 1.0 / math.sqrt(HEAD_SIZE)
    own_start = tp_rank * own_len

    def own_rows(rows):
        return lax.dynamic_slice_in_dim(rows, own_start, own_len, 0)

    route_rows = own_rows(routes[0])
    kv_width = key_value_projection.shape[1] * 2 * HEAD_SIZE
    gains = jnp.pad(jnp.stack([attn_gain, ffn_gain]), ((0, 14), (0, 0)))
    gains = in_order(all_steps(gains, FSDP), FSDP)
    gain_one, gain_two = (gains[:, row].reshape(model_width) for row in range(2))
    packed = jnp.concatenate(
        [w_query, key_value_projection.reshape(slice_width, kv_width)], axis=1
    )
    packed_parts = all_steps(row_major(packed), FSDP)
    both_width = head_width + kv_width
    both_weight = row_major(in_order(packed_parts, FSDP).reshape(model_width, both_width))
    query_full = both_weight[:, :head_width]
    key_value_weight = both_weight[:, head_width:]
    router = jnp.pad(w_router, ((0, 0), (0, -expert_total % 128)))
    out_parts = jnp.concatenate([output_projection_weight, router], axis=1)
    out_parts = all_steps(after(out_parts, packed_parts), FSDP)
    out_full = (
        in_order([part[:, :slice_width] for part in out_parts], FSDP)
        .transpose(1, 0, 2)
        .reshape(head_width, model_width)
    )
    router_full = in_order([part[:, slice_width:] for part in out_parts], FSDP)
    router_full = router_full.reshape(model_width, router.shape[1])[:, :expert_total]

    route_tail = jnp.pad(
        route_rows.astype(jnp.bfloat16), ((0, 0), (0, -route_rows.shape[1] % 256))
    )
    carried = jnp.concatenate([own_rows(cotangent[0]), route_tail], axis=1)
    grad_pieces = all_steps(after(carried, out_parts), FSDP)

    def weight_packet(weights, earlier):
        packets = []
        for step in range(fsdp_count):
            index = ((fsdp_rank + step) % fsdp_count) * ctx_count + ctx_rank
            packet = jnp.stack([pick_block(weight, index) for weight in weights])
            if step:
                packet = after(packet, earlier)
                packet = rotated(packet, FSDP, step)
            packets.append(packet)
        return packets

    def whole_weights(packets):
        return [
            in_order([packet[kind] for packet in packets], FSDP).reshape(
                fsdp_count * slice_width, ff_width
            )
            for kind in range(packets[0].shape[0])
        ]

    wide_input = input_rows.astype(jnp.float32)
    normed_one, factor_one, first_hidden_state = rms_forward(wide_input, gain_one)
    query_matrix = jnp.dot(
        first_hidden_state, query_full, preferred_element_type=jnp.float32
    ).reshape(local_len, local_heads, HEAD_SIZE)
    key_value_rows = jnp.dot(
        first_hidden_state, key_value_weight, preferred_element_type=jnp.float32
    ).reshape(local_len, local_kv, 2, HEAD_SIZE)
    place_rows = positions[0]
    cosine_lookup, sine_lookup = rope_tables(place_rows, HEAD_SIZE)
    rotated_query = (
        apply_rotary(query_matrix, cosine_lookup, sine_lookup, 1.0)
        .astype(jnp.bfloat16)
        .reshape(local_len, local_kv, query_group_count, HEAD_SIZE)
    )
    k_rot = apply_rotary(key_value_rows[:, :, 0], cosine_lookup, sine_lookup, 1.0).astype(
        jnp.bfloat16
    )
    v_rows = key_value_rows[:, :, 1].astype(jnp.bfloat16)
    local_ids = jnp.arange(local_len, dtype=jnp.int32)
    query_ids = ctx_rank * local_len + local_ids
    query_starts = query_ids - place_rows
    kv_pack = jnp.concatenate([k_rot, v_rows], axis=-1)
    kv_blocks = [kv_pack]
    key_ids = [query_ids]
    for step in range(1, ctx_count):
        kv_blocks.append(shifted(kv_blocks[-1], CTX, 1))
        key_ids.append((ctx_rank - step) * local_len + local_ids)
    row_total = jnp.zeros((local_kv, query_group_count, local_len), jnp.float32)
    weighted = jnp.zeros((local_kv, query_group_count, local_len, HEAD_SIZE), jnp.float32)
    masks = []
    for block_index in range(ctx_count):
        allowed = attend_mask(query_ids, query_starts, key_ids[block_index])
        masks.append(allowed)
        key_rows = kv_blocks[block_index][..., :HEAD_SIZE]
        value_rows = kv_blocks[block_index][..., HEAD_SIZE:]
        scores = (
            jnp.einsum(
                TKGD_SKD_TO_KGTS, rotated_query, key_rows, preferred_element_type=jnp.float32
            )
            * factor
        )
        exp_scores = jnp.where(allowed[None, None], jnp.exp(scores), 0.0)
        row_total = row_total + jnp.sum(exp_scores, axis=-1)
        weighted = weighted + jnp.einsum(
            KGTS_SKD_TO_KGTD,
            exp_scores.astype(jnp.bfloat16),
            value_rows,
            preferred_element_type=jnp.float32,
        )
    head_out = (weighted / row_total[..., None]).astype(jnp.bfloat16)
    flat_heads = head_out.transpose(2, 0, 1, 3).reshape(local_len, local_heads * HEAD_SIZE)
    attn_part = jnp.dot(flat_heads, out_full, preferred_element_type=jnp.float32)

    attn_total = sum_over_tp(attn_part)
    residual = own_rows(input_rows).astype(jnp.float32) + attn_total
    normed_two, factor_two, hidden_two = rms_forward(residual, gain_two)
    hidden_pieces = all_steps(hidden_two, FSDP)
    grad_halves = [
        half.reshape(block_count, local_len, half.shape[-1])
        for half in spread(grad_pieces)
    ]
    hidden_halves = [
        half.reshape(block_count, local_len, half.shape[-1])
        for half in spread(hidden_pieces)
    ]
    tail_start = grad_halves[1].shape[-1] - route_tail.shape[1]
    routes_all = grad_halves[1][:, :, tail_start : tail_start + route_rows.shape[1]]
    routes_all = routes_all.astype(jnp.int32).reshape(-1, route_rows.shape[1])
    expert_ids = jnp.arange(expert_total, dtype=jnp.int32)
    chosen_all = jnp.any(routes_all[:, :, None] == expert_ids[None, None, :], axis=1)
    own_expert = tp_rank * block_count + fsdp_rank * ctx_count + ctx_rank
    member = jnp.any(routes_all == own_expert, axis=1).reshape(block_count, local_len)
    places = jnp.cumsum(member.astype(jnp.int32), axis=1) - 1
    slots = jnp.where(member, places, capacity)
    slot_ids = jnp.arange(capacity, dtype=jnp.int32)
    hot = slots[:, None, :] == slot_ids[None, :, None]
    hot_b = hot.astype(jnp.bfloat16)

    def take_rows(rows):
        return (
            jnp.einsum("bst,btd->bsd", hot_b, rows, preferred_element_type=jnp.float32)
            .astype(jnp.bfloat16)
            .reshape(block_count * capacity, rows.shape[2])
        )

    slot_chosen = take_rows(
        chosen_all.astype(jnp.bfloat16).reshape(block_count, local_len, expert_total)
    ).astype(jnp.float32)

    def put_rows(rows):
        stacked = rows.reshape(block_count, capacity, rows.shape[1])
        return (
            jnp.einsum("bst,bsd->btd", hot_b, stacked, preferred_element_type=jnp.float32)
            .astype(jnp.bfloat16)
            .reshape(
                (fsdp_count, ctx_count)
                + (2,) * len(tp_stages())
                + (own_len, rows.shape[1])
            )
        )

    first_packets = weight_packet((w_gate, w_up), hidden_pieces)
    down_packets = weight_packet((w_down,), hidden_pieces)
    hidden_halves, first_packets, down_packets = lax.optimization_barrier(
        (hidden_halves, first_packets, down_packets)
    )
    gate_weight, up_weight = whole_weights(first_packets)
    (down_weight,) = whole_weights(down_packets)
    own_chosen = jnp.any(route_rows[:, :, None] == expert_ids[None, None, :], axis=1)

    def exp_logits(hidden, chosen):
        logits = jnp.dot(hidden, router_full, preferred_element_type=jnp.float32)
        return jnp.where(chosen, jnp.exp(logits), 0.0)

    own_exp = exp_logits(hidden_two, own_chosen)
    own_gates = own_exp / jnp.sum(own_exp, axis=-1, keepdims=True)

    picked = jnp.concatenate([take_rows(half) for half in hidden_halves], axis=1)
    slot_exp = exp_logits(picked, slot_chosen > 0)
    slot_live = jnp.sum(slot_chosen, axis=1) > 0
    slot_total = jnp.where(slot_live, jnp.sum(slot_exp, axis=1), 1.0)
    slot_own = jnp.sum(jnp.where(expert_ids[None, :] == own_expert, slot_exp, 0.0), axis=1)
    scaled = jnp.where(slot_live, slot_own / slot_total, 0.0)
    gate_pre = jnp.dot(picked, gate_weight, preferred_element_type=jnp.float32)
    up_pre = jnp.dot(picked, up_weight, preferred_element_type=jnp.float32)
    activation = (jax.nn.silu(gate_pre) * up_pre).astype(jnp.bfloat16)
    result = jnp.einsum(CF_DF_TO_CD, activation, down_weight, preferred_element_type=jnp.float32)

    mixture_rows = (result * scaled[:, None]).astype(jnp.bfloat16)

    grad_rows = jnp.concatenate([take_rows(half) for half in grad_halves], axis=1)
    grad_rows = grad_rows[:, :model_width]
    grad_wide_rows = grad_rows.astype(jnp.float32)
    slot_grad = jnp.sum(grad_wide_rows * result, axis=1).reshape(block_count, capacity)
    out_grad = row_major((grad_wide_rows * scaled[:, None]).astype(jnp.bfloat16))
    act_grad = jnp.dot(out_grad, down_weight, preferred_element_type=jnp.float32)
    sigmoid_gate = jax.nn.sigmoid(gate_pre)
    gate_pre_grad = (
        act_grad * up_pre * sigmoid_gate * (1.0 + gate_pre * (1.0 - sigmoid_gate))
    ).astype(jnp.bfloat16)
    up_pre_grad = (act_grad * gate_pre * sigmoid_gate).astype(jnp.bfloat16)
    picked_grad = jnp.einsum(
        CF_DF_TO_CD, gate_pre_grad, gate_weight, preferred_element_type=jnp.float32
    ) + jnp.einsum(CF_DF_TO_CD, up_pre_grad, up_weight, preferred_element_type=jnp.float32)
    gate_grad_part = jnp.sum(jnp.where(hot, slot_grad[:, :, None], 0.0), axis=1)
    gate_grad = lax.all_to_all(
        gate_grad_part.reshape(block_count * tp_count, own_len), everywhere, 0, 0, tiled=True
    )
    gate_grad = (
        gate_grad.reshape(block_count, tp_count, own_len)
        .transpose(2, 1, 0)
        .reshape(own_len, expert_total)
    )
    back_parts = [put_rows(half) for half in halves(picked_grad.astype(jnp.bfloat16))]
    back_parts, picked, gate_pre_grad, up_pre_grad, out_grad, activation = (
        lax.optimization_barrier(
            (back_parts, picked, gate_pre_grad, up_pre_grad, out_grad, activation)
        )
    )
    mixture = collect([put_rows(half) for half in halves(mixture_rows)])
    own_out = (residual + mixture).astype(jnp.bfloat16)
    hidden_grad_sum = collect(back_parts)

    def weight_grad(rows, columns):
        return (
            jnp.einsum("cd,cf->df", rows, columns, preferred_element_type=jnp.float32)
            .astype(jnp.bfloat16)
            .reshape(fsdp_count, slice_width, ff_width)
        )

    early_grads = [weight_grad(picked, rows) for rows in (gate_pre_grad, up_pre_grad)]
    late_grads = [weight_grad(out_grad, activation)]
    grad_packets = []
    for kinds in (early_grads, late_grads):
        packets = []
        for step in range(fsdp_count):
            target = (fsdp_rank + step) % fsdp_count
            packet = jnp.stack([pick_block(grad, target) for grad in kinds])
            if step:
                if len(grad_packets):
                    packet = after(packet, hidden_grad_sum)
                packet = rotated(packet, FSDP, step)
            packets.append(packet)
        grad_packets.append(packets)

    sel_grad = own_gates * (
        gate_grad - jnp.sum(own_gates * gate_grad, axis=-1, keepdims=True)
    )
    logit_grad = jnp.where(own_chosen, sel_grad, 0.0).astype(jnp.bfloat16)
    hidden_grad = hidden_grad_sum + jnp.einsum(
        TE_DE_TO_TD, logit_grad, router_full, preferred_element_type=jnp.float32
    )
    back_two, grad_ffn_gain = rms_backward(hidden_grad, normed_two, factor_two, gain_two)
    residual_grad = own_rows(cotangent[0]).astype(jnp.float32) + back_two
    row_pad = 16
    sent = jnp.concatenate(
        [
            residual_grad.astype(jnp.bfloat16),
            jnp.pad(grad_ffn_gain.astype(jnp.bfloat16)[None], ((0, row_pad - 1), (0, 0))),
        ],
        axis=0,
    )
    logit_tail = jnp.pad(logit_grad, ((0, row_pad), (0, -expert_total % 128)))
    sent = lax.all_gather(jnp.concatenate([sent, logit_tail], axis=1), TP, axis=0)
    residual_gradient_second = sent[:, :own_len, :model_width].reshape(local_len, model_width)
    logit_grad = sent[:, :own_len, model_width : model_width + expert_total].reshape(
        local_len, expert_total
    )
    grad_ffn_gain = jnp.sum(sent[:, own_len, :model_width].astype(jnp.float32), axis=0)
    own_block = fsdp_rank * ctx_count + ctx_rank
    block_hidden = jnp.concatenate(
        [pick_block(half, own_block) for half in hidden_halves], axis=1
    )
    grad_router = jnp.einsum(
        TD_TE_TO_DE, block_hidden, logit_grad, preferred_element_type=jnp.float32
    )

    grad_out_proj = jnp.einsum(
        "td,ti->di", residual_gradient_second, flat_heads, preferred_element_type=jnp.float32
    )
    early = jnp.concatenate([grad_out_proj, grad_router, grad_ffn_gain[:, None]], axis=1)
    early = jnp.pad(early, ((0, 0), (0, -early.shape[1] % 128))).astype(jnp.bfloat16)
    early = early.reshape(fsdp_count, slice_width, early.shape[1])
    early_parts = scatter_start(early)
    per_head_gradient = jnp.einsum(
        TD_ID_TO_TI, residual_gradient_second, out_full, preferred_element_type=jnp.float32
    ).astype(jnp.bfloat16)
    per_head_gradient = per_head_gradient.reshape(
        local_len, local_kv, query_group_count, HEAD_SIZE
    ).transpose(1, 2, 0, 3)
    row_delta = jnp.sum(
        per_head_gradient.astype(jnp.float32) * head_out.astype(jnp.float32), axis=-1
    )
    log_total = jnp.log(row_total)
    query_grad = jnp.zeros((local_len, local_kv, query_group_count, HEAD_SIZE), jnp.float32)
    kv_grads = []
    for block_index in range(ctx_count):
        key_rows = kv_blocks[block_index][..., :HEAD_SIZE]
        value_rows = kv_blocks[block_index][..., HEAD_SIZE:]
        scores = (
            jnp.einsum(
                TKGD_SKD_TO_KGTS, rotated_query, key_rows, preferred_element_type=jnp.float32
            )
            * factor
        )
        probability = jnp.where(
            masks[block_index][None, None], jnp.exp(scores - log_total[..., None]), 0.0
        )
        prob_grad = jnp.einsum(
            KGTD_SKD_TO_KGTS, per_head_gradient, value_rows, preferred_element_type=jnp.float32
        )
        score_grad = (probability * (prob_grad - row_delta[..., None]) * factor).astype(
            jnp.bfloat16
        )
        query_grad = query_grad + jnp.einsum(
            KGTS_SKD_TO_TKGD, score_grad, key_rows, preferred_element_type=jnp.float32
        )
        key_grad = jnp.einsum(
            KGTS_TKGD_TO_SKD, score_grad, rotated_query, preferred_element_type=jnp.float32
        )
        value_gradient = jnp.einsum(
            KGTS_KGTD_TO_SKD,
            probability.astype(jnp.bfloat16),
            per_head_gradient,
            preferred_element_type=jnp.float32,
        )
        kv_grads.append(jnp.concatenate([key_grad, value_gradient], axis=-1))
    weight_hops = []
    for step in range(fsdp_count):
        early_hops = all_steps(grad_packets[0][step], CTX)
        late_hops = all_steps(grad_packets[1][step], CTX)
        weight_hops.append((early_hops, late_hops))
    kv_grad_total = kv_grads[0]
    for step in range(1, ctx_count):
        returning = shifted(kv_grads[step].astype(jnp.bfloat16), CTX, -step)
        kv_grad_total = kv_grad_total + returning.astype(jnp.float32)
    key_backward_rows = apply_rotary(
        kv_grad_total[..., :HEAD_SIZE], cosine_lookup, sine_lookup, -1.0
    )
    key_value_backward = (
        jnp.stack([key_backward_rows, kv_grad_total[..., HEAD_SIZE:]], axis=2)
        .astype(jnp.bfloat16)
        .reshape(local_len, kv_width)
    )
    query_back = (
        apply_rotary(
            query_grad.reshape(local_len, local_heads, HEAD_SIZE), cosine_lookup, sine_lookup, -1.0
        )
        .astype(jnp.bfloat16)
        .reshape(local_len, head_width)
    )
    both_back = jnp.concatenate([query_back, key_value_backward], axis=1)
    hidden_one_part = jnp.einsum(
        TF_DF_TO_TD, both_back, both_weight, preferred_element_type=jnp.float32
    )
    grad_attn_gain = jnp.sum(hidden_one_part * normed_one, axis=0)
    projection_grad = jnp.einsum(
        TD_TF_TO_DF, first_hidden_state, both_back, preferred_element_type=jnp.float32
    )
    projection_grad = projection_grad.astype(jnp.bfloat16).reshape(
        fsdp_count, slice_width, both_width
    )
    projection_parts = scatter_start(projection_grad)
    summed = sum_over_tp(hidden_one_part, grad_attn_gain)
    hidden_one_grad = summed[:own_len]
    grad_attn_gain = summed[own_len].astype(jnp.bfloat16).reshape(fsdp_count, 1, slice_width)
    gain_parts = scatter_start(grad_attn_gain)
    back_one, _ = rms_backward(
        hidden_one_grad, own_rows(normed_one), own_rows(factor_one), gain_one
    )
    input_grad = (residual_grad + back_one).astype(jnp.bfloat16)
    input_grad = lax.all_gather(input_grad, TP, axis=0, tiled=True)
    out_rows = lax.all_gather(after(own_out, input_grad), TP, axis=0, tiled=True)
    grad_attn_gain = scatter_finish(after(gain_parts, out_rows))[0]
    early_total = scatter_finish(after(early_parts, out_rows))
    projection_total = scatter_finish(after(projection_parts, out_rows))
    hop_places = jnp.stack(
        [
            (fsdp_rank - step) % fsdp_count * ctx_count + (ctx_rank - hop) % ctx_count
            for step in range(fsdp_count)
            for hop in range(ctx_count)
        ]
    ).astype(jnp.int32)
    weight_outs = assemble(
        after([seen for hops, _ in weight_hops for seen in hops], out_rows), hop_places
    ) + assemble(
        after([seen for _, hops in weight_hops for seen in hops], out_rows), hop_places
    )
    return (
        out_rows[None],
        input_grad.astype(jnp.float32)[None],
        grad_attn_gain,
        projection_total[:, :head_width],
        projection_total[:, head_width:].reshape(key_value_projection.shape),
        early_total[:, :head_width].T,
        early_total[:, head_width + expert_total],
        early_total[:, head_width : head_width + expert_total],
        weight_outs[0],
        weight_outs[1],
        weight_outs[2],
    )


def local_any(*args):
    devices = math.prod(lax.axis_size(name) for name in (FSDP, CTX, TP))
    if args[9].shape[1] != devices:
        return local(*args)
    return local_spread(*args)


def solution(mesh):

    return jax.shard_map(
        local_any,
        mesh=mesh,
        in_specs=(
            P(FSDP, CTX, None),
            P(FSDP, CTX, None),
            P(FSDP, CTX),
            P(FSDP, CTX, None),
            P(FSDP),
            P(FSDP, TP),
            P(FSDP, TP, None, None),
            P(TP, FSDP),
            P(FSDP),
            P(FSDP, None),
            P(TP, FSDP, None),
            P(TP, FSDP, None),
            P(TP, FSDP, None),
        ),
        out_specs=(
            P(FSDP, CTX, None),
            P(FSDP, CTX, None),
            P(FSDP),
            P(FSDP, TP),
            P(FSDP, TP, None, None),
            P(TP, FSDP),
            P(FSDP),
            P(FSDP, None),
            P(TP, FSDP, None),
            P(TP, FSDP, None),
            P(TP, FSDP, None),
        ),
        check_vma=False,
    )
```

```python
import math

import jax
import jax.numpy as jnp
from jax import lax
from jax.experimental import pallas as pl
from jax.experimental.pallas import tpu as pltpu
from jax.experimental.layout import Layout, with_layout_constraint
from jax.sharding import PartitionSpec as P

CF_DF_TO_CD = "cf,df->cd"
CTX = "ctx"
ECD_ECF_TO_EDF = "ecd,ecf->edf"
ECD_EDF_TO_ECF = "ecd,edf->ecf"
ECF_EDF_TO_ECD = "ecf,edf->ecd"
FSDP = "fsdp"
KGTD_SKD_TO_KGTS = "kgtd,skd->kgts"
KGTS_KGTD_TO_SKD = "kgts,kgtd->skd"
KGTS_SKD_TO_KGTD = "kgts,skd->kgtd"
KGTS_SKD_TO_TKGD = "kgts,skd->tkgd"
KGTS_TKGD_TO_SKD = "kgts,tkgd->skd"
TD_ID_TO_TI = "td,id->ti"
TD_TE_TO_DE = "td,te->de"
TD_TF_TO_DF = "td,tf->df"
TE_DE_TO_TD = "te,de->td"
TF_DF_TO_TD = "tf,df->td"
TKGD_SKD_TO_KGTS = "tkgd,skd->kgts"
TP = "tp"


QUERY_HEADS = 16
KEY_VALUE_HEADS = 8
HEAD_SIZE = 64


EPS = 1e-06
THETA = 10000.0


def shifted(block, axis, distance):
    devices = range(lax.axis_size(axis))
    route = [(i - distance, i) for i in devices if i - distance in devices]
    return lax.ppermute(block, axis, route)


def rope_tables(place_rows, head_width):
    half_width = head_width // 2
    inverse = THETA ** (-2.0 * jnp.arange(half_width, dtype=jnp.float32) / head_width)
    angle = place_rows.astype(jnp.float32)[:, None] * inverse[None, :]
    return (jnp.cos(angle)[:, None, :], jnp.sin(angle)[:, None, :])


def apply_rotary(vector, cosine_lookup, sine_lookup, direction):
    half_width = vector.shape[-1] // 2
    first_half = vector[..., :half_width]
    second_half = vector[..., half_width:]
    return jnp.concatenate(
        [
            first_half * cosine_lookup - direction * second_half * sine_lookup,
            direction * first_half * sine_lookup + second_half * cosine_lookup,
        ],
        axis=-1,
    )


def rms_forward(wide_rows, gain_vector):
    factor = lax.rsqrt(jnp.mean(wide_rows * wide_rows, axis=-1, keepdims=True) + EPS)
    normed = wide_rows * factor
    return (normed, factor, (normed * gain_vector.astype(jnp.float32)).astype(jnp.bfloat16))


def rms_backward(gradient, normed, factor, gain_vector):
    gain_grad = jnp.sum(gradient * normed, axis=0)
    inner_term = gradient * gain_vector.astype(jnp.float32)
    back_term = factor * (
        inner_term - normed * jnp.mean(inner_term * normed, axis=-1, keepdims=True)
    )
    return (back_term, gain_grad)


def attend_mask(query_ids, query_starts, key_ids):
    return (key_ids[None, :] <= query_ids[:, None]) & (key_ids[None, :] >= query_starts[:, None])


def router_gates(logits, picks):
    selected = jnp.sum(jnp.where(picks, logits[:, None, :], 0.0), axis=-1)
    exp_sel = jnp.exp(selected)
    return exp_sel / jnp.sum(exp_sel, axis=-1, keepdims=True)


def slot_tables(route_rows, gate_weights, first_expert, expert_count, capacity):
    token_count = route_rows.shape[0]
    owners = first_expert + jnp.arange(expert_count, dtype=jnp.int32)
    hit_mask = route_rows[:, :, None] == owners[None, None, :]
    member = jnp.sum(hit_mask.astype(jnp.int32), axis=1)
    weight_rows = jnp.sum(jnp.where(hit_mask, gate_weights[:, :, None], 0.0), axis=1)
    places = jnp.cumsum(member, axis=0) - 1
    expert_ids = jnp.arange(expert_count, dtype=jnp.int32)
    slot_ids = jnp.where(
        member > 0, expert_ids[None, :] * capacity + places, expert_count * capacity
    )
    flat_slots = slot_ids.reshape(-1)
    token_ids = jnp.broadcast_to(
        jnp.arange(token_count, dtype=jnp.int32)[:, None], (token_count, expert_count)
    ).reshape(-1)
    source = jnp.zeros((expert_count * capacity + 1,), jnp.int32).at[flat_slots].set(token_ids)[:-1]
    scaled = (
        jnp.zeros((expert_count * capacity + 1,), jnp.float32)
        .at[flat_slots]
        .set(weight_rows.reshape(-1))[:-1]
    )
    return (hit_mask, slot_ids, source, scaled)


def expert_forward(hidden, source, w_gate, w_up, w_down, expert_count, capacity):
    picked = hidden[source].reshape(expert_count, capacity, hidden.shape[1])
    gate_pre = jnp.einsum(ECD_EDF_TO_ECF, picked, w_gate, preferred_element_type=jnp.float32)
    up_pre = jnp.einsum(ECD_EDF_TO_ECF, picked, w_up, preferred_element_type=jnp.float32)
    activation = (jax.nn.silu(gate_pre) * up_pre).astype(jnp.bfloat16)
    result = jnp.einsum(ECF_EDF_TO_ECD, activation, w_down, preferred_element_type=jnp.float32)
    return (picked, gate_pre, up_pre, activation, result)


def combine(result, source, scaled, token_count):
    model_width = result.shape[-1]
    flat_result = result.reshape(-1, model_width)
    return (
        jnp.zeros((token_count, model_width), jnp.float32)
        .at[source]
        .add(flat_result * scaled[:, None])
    )


def expert_backward(
    grad_rows,
    hit_mask,
    slot_ids,
    source,
    scaled,
    saved,
    w_gate,
    w_up,
    w_down,
    expert_count,
    capacity,
    token_count,
):
    picked, gate_pre, up_pre, activation, result = saved
    model_width = grad_rows.shape[1]
    slot_grad = jnp.sum(grad_rows * result.reshape(expert_count * capacity, model_width), axis=1)
    padded = jnp.concatenate([slot_grad, jnp.zeros((1,), jnp.float32)])
    per_expert = padded[slot_ids]
    gate_grad = jnp.sum(jnp.where(hit_mask, per_expert[:, None, :], 0.0), axis=2)
    out_grad = (
        (grad_rows * scaled[:, None])
        .astype(jnp.bfloat16)
        .reshape(expert_count, capacity, model_width)
    )
    grad_down = jnp.einsum(ECD_ECF_TO_EDF, out_grad, activation, preferred_element_type=jnp.float32)
    act_grad = jnp.einsum(ECD_EDF_TO_ECF, out_grad, w_down, preferred_element_type=jnp.float32)
    sigmoid_gate = jax.nn.sigmoid(gate_pre)
    gate_pre_grad = (
        act_grad * up_pre * sigmoid_gate * (1.0 + gate_pre * (1.0 - sigmoid_gate))
    ).astype(jnp.bfloat16)
    up_pre_grad = (act_grad * gate_pre * sigmoid_gate).astype(jnp.bfloat16)
    grad_gate = jnp.einsum(
        ECD_ECF_TO_EDF, picked, gate_pre_grad, preferred_element_type=jnp.float32
    )
    grad_up = jnp.einsum(ECD_ECF_TO_EDF, picked, up_pre_grad, preferred_element_type=jnp.float32)
    picked_grad = jnp.einsum(
        ECF_EDF_TO_ECD, gate_pre_grad, w_gate, preferred_element_type=jnp.float32
    ) + jnp.einsum(ECF_EDF_TO_ECD, up_pre_grad, w_up, preferred_element_type=jnp.float32)
    hidden_grad = (
        jnp.zeros((token_count, model_width), jnp.float32)
        .at[source]
        .add(picked_grad.reshape(-1, model_width))
    )
    return (gate_grad, hidden_grad, grad_gate, grad_up, grad_down)


def local(
    tokens,
    cotangent,
    positions,
    routes,
    attn_gain,
    w_query,
    key_value_projection,
    output_projection_weight,
    ffn_gain,
    w_router,
    w_gate,
    w_up,
    w_down,
):
    gain_one, gain_two, query_full, keyval_full, out_full, router_full = (
        lax.all_gather(attn_gain, FSDP, axis=0, tiled=True),
        lax.all_gather(ffn_gain, FSDP, axis=0, tiled=True),
        lax.all_gather(w_query, FSDP, axis=0, tiled=True),
        lax.all_gather(key_value_projection, FSDP, axis=0, tiled=True),
        lax.all_gather(output_projection_weight, FSDP, axis=1, tiled=True),
        lax.all_gather(w_router, FSDP, axis=0, tiled=True),
    )
    expert_full = (
        lax.all_gather(w_gate, FSDP, axis=1, tiled=True),
        lax.all_gather(w_up, FSDP, axis=1, tiled=True),
        lax.all_gather(w_down, FSDP, axis=1, tiled=True),
    )
    input_rows = tokens[0]
    local_len = input_rows.shape[0]
    model_width = input_rows.shape[1]
    query_group_count = QUERY_HEADS // KEY_VALUE_HEADS
    local_heads = w_query.shape[1] // HEAD_SIZE
    local_kv = local_heads // query_group_count
    expert_count = w_gate.shape[0]
    capacity = local_len // 2
    ctx_count = lax.axis_size(CTX)
    ctx_rank = lax.axis_index(CTX)
    factor = 1.0 / math.sqrt(HEAD_SIZE)
    key_value_weight = keyval_full.reshape(model_width, local_kv * 2 * HEAD_SIZE)
    wide_input = input_rows.astype(jnp.float32)
    normed_one, factor_one, first_hidden_state = rms_forward(wide_input, gain_one)
    query_matrix = jnp.dot(
        first_hidden_state, query_full, preferred_element_type=jnp.float32
    ).reshape(local_len, local_heads, HEAD_SIZE)
    key_value_rows = jnp.dot(
        first_hidden_state, key_value_weight, preferred_element_type=jnp.float32
    ).reshape(local_len, local_kv, 2, HEAD_SIZE)
    place_rows = positions[0]
    cosine_lookup, sine_lookup = rope_tables(place_rows, HEAD_SIZE)
    rotated_query = (
        apply_rotary(query_matrix, cosine_lookup, sine_lookup, 1.0)
        .astype(jnp.bfloat16)
        .reshape(local_len, local_kv, query_group_count, HEAD_SIZE)
    )
    k_rot = apply_rotary(key_value_rows[:, :, 0], cosine_lookup, sine_lookup, 1.0).astype(
        jnp.bfloat16
    )
    v_rows = key_value_rows[:, :, 1].astype(jnp.bfloat16)
    local_ids = jnp.arange(local_len, dtype=jnp.int32)
    query_ids = ctx_rank * local_len + local_ids
    query_starts = query_ids - place_rows
    kv_pack = jnp.concatenate([k_rot, v_rows], axis=-1)
    kv_blocks = [kv_pack]
    key_ids = [query_ids]
    travelling = kv_pack
    cycle_step = 1
    travelling = shifted(travelling, CTX, 1)
    kv_blocks.append(travelling)
    key_ids.append((ctx_rank - cycle_step) * local_len + local_ids)
    row_total = jnp.zeros((local_kv, query_group_count, local_len), jnp.float32)
    weighted = jnp.zeros((local_kv, query_group_count, local_len, HEAD_SIZE), jnp.float32)
    masks = []
    for block_index in range(ctx_count):
        allowed = attend_mask(query_ids, query_starts, key_ids[block_index])
        masks.append(allowed)
        key_rows = kv_blocks[block_index][..., :HEAD_SIZE]
        value_rows = kv_blocks[block_index][..., HEAD_SIZE:]
        scores = (
            jnp.einsum(
                TKGD_SKD_TO_KGTS, rotated_query, key_rows, preferred_element_type=jnp.float32
            )
            * factor
        )
        exp_scores = jnp.where(allowed[None, None], jnp.exp(scores), 0.0)
        row_total = row_total + jnp.sum(exp_scores, axis=-1)
        weighted = weighted + jnp.einsum(
            KGTS_SKD_TO_KGTD,
            exp_scores.astype(jnp.bfloat16),
            value_rows,
            preferred_element_type=jnp.float32,
        )
    head_out = (weighted / row_total[..., None]).astype(jnp.bfloat16)
    flat_heads = head_out.transpose(2, 0, 1, 3).reshape(local_len, local_heads * HEAD_SIZE)
    attn_part = jnp.dot(flat_heads, out_full, preferred_element_type=jnp.float32)
    residual = wide_input + lax.psum(attn_part, TP)
    normed_two, factor_two, hidden_two = rms_forward(residual, gain_two)
    logits = jnp.dot(hidden_two, router_full, preferred_element_type=jnp.float32)
    route_rows = routes[0]
    picks = (
        route_rows[:, :, None] == jnp.arange(router_full.shape[1], dtype=jnp.int32)[None, None, :]
    )
    gate_weights = router_gates(logits, picks)
    first_expert = lax.axis_index(TP) * expert_count
    hit_mask, slot_ids, source, scaled = slot_tables(
        route_rows, gate_weights, first_expert, expert_count, capacity
    )
    saved = expert_forward(
        hidden_two, source, expert_full[0], expert_full[1], expert_full[2], expert_count, capacity
    )
    mixture_part = combine(saved[4], source, scaled, local_len)
    mixture = lax.psum(mixture_part.astype(jnp.bfloat16), TP).astype(jnp.float32)
    out_rows = (residual + mixture).astype(jnp.bfloat16)
    grad_wide = cotangent[0].astype(jnp.float32)
    back_weights = (
        lax.all_gather(w_gate, FSDP, axis=1, tiled=True),
        lax.all_gather(w_up, FSDP, axis=1, tiled=True),
        lax.all_gather(w_down, FSDP, axis=1, tiled=True),
    )
    grad_rows = grad_wide[source]
    gate_grad_part, hidden_grad_part, grad_gate, grad_up, grad_down = expert_backward(
        grad_rows,
        hit_mask,
        slot_ids,
        source,
        scaled,
        saved,
        back_weights[0],
        back_weights[1],
        back_weights[2],
        expert_count,
        capacity,
        local_len,
    )
    hidden_grad_sum, gate_grad = lax.psum((hidden_grad_part, gate_grad_part), TP)
    sel_grad = gate_weights * (
        gate_grad - jnp.sum(gate_weights * gate_grad, axis=-1, keepdims=True)
    )
    logit_grad = jnp.sum(jnp.where(picks, sel_grad[:, :, None], 0.0), axis=1).astype(jnp.bfloat16)
    grad_router = jnp.einsum(
        TD_TE_TO_DE, hidden_two, logit_grad, preferred_element_type=jnp.float32
    )
    hidden_grad = hidden_grad_sum + jnp.einsum(
        TE_DE_TO_TD, logit_grad, router_full, preferred_element_type=jnp.float32
    )
    back_two, grad_ffn_gain = rms_backward(hidden_grad, normed_two, factor_two, gain_two)
    residual_grad = grad_wide + back_two
    residual_gradient_second = residual_grad.astype(jnp.bfloat16)
    grad_out_proj = jnp.einsum(
        "ti,td->id", flat_heads, residual_gradient_second, preferred_element_type=jnp.float32
    )
    per_head_gradient = jnp.einsum(
        TD_ID_TO_TI, residual_gradient_second, out_full, preferred_element_type=jnp.float32
    ).astype(jnp.bfloat16)
    per_head_gradient = per_head_gradient.reshape(
        local_len, local_kv, query_group_count, HEAD_SIZE
    ).transpose(1, 2, 0, 3)
    row_delta = jnp.sum(
        per_head_gradient.astype(jnp.float32) * head_out.astype(jnp.float32), axis=-1
    )
    log_total = jnp.log(row_total)
    query_grad = jnp.zeros((local_len, local_kv, query_group_count, HEAD_SIZE), jnp.float32)
    kv_grads = []
    for block_index in range(ctx_count):
        key_rows = kv_blocks[block_index][..., :HEAD_SIZE]
        value_rows = kv_blocks[block_index][..., HEAD_SIZE:]
        scores = (
            jnp.einsum(
                TKGD_SKD_TO_KGTS, rotated_query, key_rows, preferred_element_type=jnp.float32
            )
            * factor
        )
        probability = jnp.where(
            masks[block_index][None, None], jnp.exp(scores - log_total[..., None]), 0.0
        )
        prob_grad = jnp.einsum(
            KGTD_SKD_TO_KGTS, per_head_gradient, value_rows, preferred_element_type=jnp.float32
        )
        score_grad = (probability * (prob_grad - row_delta[..., None]) * factor).astype(
            jnp.bfloat16
        )
        query_grad = query_grad + jnp.einsum(
            KGTS_SKD_TO_TKGD, score_grad, key_rows, preferred_element_type=jnp.float32
        )
        key_grad = jnp.einsum(
            KGTS_TKGD_TO_SKD, score_grad, rotated_query, preferred_element_type=jnp.float32
        )
        value_gradient = jnp.einsum(
            KGTS_KGTD_TO_SKD,
            probability.astype(jnp.bfloat16),
            per_head_gradient,
            preferred_element_type=jnp.float32,
        )
        kv_grads.append(jnp.concatenate([key_grad, value_gradient], axis=-1))
    cycle_step = 1
    returning = shifted(kv_grads[cycle_step].astype(jnp.bfloat16), CTX, -1).astype(jnp.float32)
    kv_grad_total = kv_grads[0] + returning
    key_backward_rows = apply_rotary(
        kv_grad_total[..., :HEAD_SIZE], cosine_lookup, sine_lookup, -1.0
    )
    key_value_backward = (
        jnp.stack([key_backward_rows, kv_grad_total[..., HEAD_SIZE:]], axis=2)
        .astype(jnp.bfloat16)
        .reshape(local_len, local_kv * 2 * HEAD_SIZE)
    )
    query_back = (
        apply_rotary(
            query_grad.reshape(local_len, local_heads, HEAD_SIZE), cosine_lookup, sine_lookup, -1.0
        )
        .astype(jnp.bfloat16)
        .reshape(local_len, local_heads * HEAD_SIZE)
    )
    grad_query = jnp.einsum(
        TD_TF_TO_DF, first_hidden_state, query_back, preferred_element_type=jnp.float32
    )
    key_value_gradient = jnp.einsum(
        TD_TF_TO_DF, first_hidden_state, key_value_backward, preferred_element_type=jnp.float32
    ).reshape(model_width, local_kv, 2, HEAD_SIZE)
    hidden_one_part = jnp.einsum(
        TF_DF_TO_TD, query_back, query_full, preferred_element_type=jnp.float32
    ) + jnp.einsum(
        TF_DF_TO_TD, key_value_backward, key_value_weight, preferred_element_type=jnp.float32
    )
    hidden_one_grad = lax.psum(hidden_one_part.astype(jnp.bfloat16), TP).astype(jnp.float32)
    back_one, grad_attn_gain = rms_backward(hidden_one_grad, normed_one, factor_one, gain_one)
    input_grad = residual_grad + back_one
    shards = (
        lax.psum_scatter(
            grad_attn_gain.astype(jnp.bfloat16), FSDP, scatter_dimension=0, tiled=True
        ).astype(jnp.float32),
        lax.psum_scatter(
            grad_ffn_gain.astype(jnp.bfloat16), FSDP, scatter_dimension=0, tiled=True
        ).astype(jnp.float32),
        lax.psum_scatter(
            grad_query.astype(jnp.bfloat16), FSDP, scatter_dimension=0, tiled=True
        ).astype(jnp.float32),
        lax.psum_scatter(
            key_value_gradient.astype(jnp.bfloat16), FSDP, scatter_dimension=0, tiled=True
        ).astype(jnp.float32),
        lax.psum_scatter(
            grad_out_proj.astype(jnp.bfloat16), FSDP, scatter_dimension=1, tiled=True
        ).astype(jnp.float32),
        lax.psum_scatter(
            grad_router.astype(jnp.bfloat16), FSDP, scatter_dimension=0, tiled=True
        ).astype(jnp.float32),
    )
    piece_gate, piece_up, piece_down = (
        lax.psum_scatter(
            grad_gate.astype(jnp.bfloat16), (FSDP, CTX), scatter_dimension=1, tiled=True
        ).astype(jnp.float32),
        lax.psum_scatter(
            grad_up.astype(jnp.bfloat16), (FSDP, CTX), scatter_dimension=1, tiled=True
        ).astype(jnp.float32),
        lax.psum_scatter(
            grad_down.astype(jnp.bfloat16), (FSDP, CTX), scatter_dimension=1, tiled=True
        ).astype(jnp.float32),
    )
    expert_totals = (
        lax.all_gather(piece_gate.astype(jnp.bfloat16), CTX, axis=1, tiled=True).astype(
            piece_gate.dtype
        ),
        lax.all_gather(piece_up.astype(jnp.bfloat16), CTX, axis=1, tiled=True).astype(
            piece_up.dtype
        ),
        lax.all_gather(piece_down.astype(jnp.bfloat16), CTX, axis=1, tiled=True).astype(
            piece_down.dtype
        ),
    )
    small_totals = (
        lax.psum(shards[0].astype(jnp.bfloat16), CTX).astype(jnp.float32),
        lax.psum(shards[1].astype(jnp.bfloat16), CTX).astype(jnp.float32),
        lax.psum(shards[2].astype(jnp.bfloat16), CTX).astype(jnp.float32),
        lax.psum(shards[3].astype(jnp.bfloat16), CTX).astype(jnp.float32),
        lax.psum(shards[4].astype(jnp.bfloat16), CTX).astype(jnp.float32),
        lax.psum(shards[5].astype(jnp.bfloat16), CTX).astype(jnp.float32),
    )
    return (
        out_rows[None],
        input_grad[None],
        small_totals[0],
        small_totals[2],
        small_totals[3],
        small_totals[4],
        small_totals[1],
        small_totals[5],
        expert_totals[0],
        expert_totals[1],
        expert_totals[2],
    )


def rotated(block, axis, distance):
    count = lax.axis_size(axis)
    return lax.ppermute(block, axis, [(i, (i + distance) % count) for i in range(count)])


def pick_block(stacked, index):
    return lax.dynamic_index_in_dim(stacked, index, 0, keepdims=False)


def sum_over_tp(part, shared=None):
    count = lax.axis_size(TP)
    pieces = part.astype(jnp.bfloat16).reshape(count, part.shape[0] // count, part.shape[1])
    if shared is not None:
        shared = jnp.pad(shared.astype(jnp.bfloat16)[None, None], ((0, 0), (0, 15), (0, 0)))
        shared = jnp.broadcast_to(shared, (count,) + shared.shape[1:])
        pieces = jnp.concatenate([pieces, shared], axis=1)
    pieces = lax.all_to_all(pieces, TP, 0, 0, tiled=True)
    return jnp.sum(pieces.astype(jnp.float32), axis=0)


def row_major(rows):
    return with_layout_constraint(rows, Layout(major_to_minor=tuple(range(rows.ndim))))


def after(value, earlier):
    return lax.optimization_barrier((value, earlier))[0]


def in_order(pieces, axis, place=0):
    count = lax.axis_size(axis)
    rank = lax.axis_index(axis)
    shape = pieces[0].shape
    whole = jnp.zeros(shape[:place] + (count,) + shape[place:], pieces[0].dtype)
    for step in range(count):
        whole = lax.dynamic_update_index_in_dim(
            whole, pieces[step], (rank - step) % count, place
        )
    return whole


def all_steps(block, axis):
    return [block] + [rotated(block, axis, step) for step in range(1, lax.axis_size(axis))]


def tp_partner(block, distance):
    count = lax.axis_size(TP)
    return lax.ppermute(block, TP, [(i, i ^ distance) for i in range(count)])


def tp_stages():
    distances = []
    distance = lax.axis_size(TP) // 2
    while distance:
        distances.append(distance)
        distance //= 2
    return distances


def spread(pieces):
    far, *near = tp_stages()
    result = []
    for flip, block in enumerate(halves(in_order(pieces, FSDP))):
        done = [FSDP]
        for stage in ([far, CTX] if flip else [CTX, far]) + near:
            place = sum(1 for other in done if rank_of(other) < rank_of(stage))
            if isinstance(stage, str):
                pieces = all_steps(block, stage)
            else:
                pieces = [block, tp_partner(block, stage)]
            if isinstance(stage, str):
                block = in_order(pieces, stage, place)
            else:
                bit = (lax.axis_index(TP) // stage) % 2
                shape = block.shape
                whole = jnp.zeros(shape[:place] + (2,) + shape[place:], block.dtype)
                whole = lax.dynamic_update_index_in_dim(whole, pieces[0], bit, place)
                block = lax.dynamic_update_index_in_dim(whole, pieces[1], 1 - bit, place)
            done.append(stage)
        result.append(block)
    return result


def rank_of(stage):
    return {FSDP: 0, CTX: 1}[stage] if isinstance(stage, str) else 2 + 1.0 / stage


def collect(parts, ready=None):
    far, *near = tp_stages()
    summed = []
    for flip, stacked in enumerate(parts):
        stages = list(reversed(near)) + ([CTX, far] if flip else [far, CTX])
        left = sorted(stages + [FSDP], key=rank_of)
        for stage in stages:
            place = left.index(stage)
            left.remove(stage)
            if isinstance(stage, str):
                count = lax.axis_size(stage)
                rank = lax.axis_index(stage)
                pieces = [lax.dynamic_index_in_dim(stacked, rank, place, keepdims=False)]
                for step in range(1, count):
                    leaving = lax.dynamic_index_in_dim(
                        stacked, (rank + step) % count, place, keepdims=False
                    )
                    pieces.append(rotated(leaving, stage, step))
            else:
                bit = (lax.axis_index(TP) // stage) % 2
                leaving = lax.dynamic_index_in_dim(stacked, 1 - bit, place, keepdims=False)
                pieces = [
                    lax.dynamic_index_in_dim(stacked, bit, place, keepdims=False),
                    tp_partner(leaving, stage),
                ]
            total = sum(piece.astype(jnp.float32) for piece in pieces)
            stacked = total.astype(jnp.bfloat16)
        summed.append(stacked)
    pieces = scatter_start(jnp.concatenate(summed, axis=-1))
    if ready is not None:
        pieces = after(pieces, ready)
    return sum(piece.astype(jnp.float32) for piece in pieces)


def assemble(pieces, places):
    kinds, rows, columns = pieces[0].shape
    count = len(pieces)

    def kernel(places_ref, *refs):
        for number in range(count):

            @pl.when(pl.program_id(0) == number)
            def _():
                for kind in range(kinds):
                    refs[count + kind][0] = refs[number][kind].astype(jnp.float32)

    size = kinds * count * rows * columns
    return pl.pallas_call(
        kernel,
        out_shape=[jax.ShapeDtypeStruct((count, rows, columns), jnp.float32)] * kinds,
        grid_spec=pltpu.PrefetchScalarGridSpec(
            num_scalar_prefetch=1,
            grid=(count,),
            in_specs=[pl.BlockSpec((kinds, rows, columns), lambda i, p: (0, 0, 0))] * count,
            out_specs=[pl.BlockSpec((1, rows, columns), lambda i, p: (p[i], 0, 0))] * kinds,
        ),
        cost_estimate=pl.CostEstimate(flops=size, bytes_accessed=6 * size, transcendentals=0),
    )(places, *pieces)


def halves(rows):
    width = rows.shape[-1] // 2
    return rows[..., :width], rows[..., width:]


def scatter_start(stacked):
    count = lax.axis_size(FSDP)
    rank = lax.axis_index(FSDP)
    pieces = [pick_block(stacked, rank)]
    for step in range(1, count):
        pieces.append(rotated(pick_block(stacked, (rank + step) % count), FSDP, step))
    return pieces


def scatter_finish(pieces):
    total = sum(piece.astype(jnp.float32) for piece in pieces)
    sent = total.astype(jnp.bfloat16)
    for step in range(1, lax.axis_size(CTX)):
        total = total + rotated(sent, CTX, step).astype(jnp.float32)
    return total


def local_spread(
    tokens,
    cotangent,
    positions,
    routes,
    attn_gain,
    w_query,
    key_value_projection,
    output_projection_weight,
    ffn_gain,
    w_router,
    w_gate,
    w_up,
    w_down,
):
    everywhere = (FSDP, CTX, TP)
    fsdp_count, ctx_count, tp_count = (lax.axis_size(name) for name in everywhere)
    fsdp_rank, ctx_rank, tp_rank = (lax.axis_index(name) for name in everywhere)
    input_rows = tokens[0]
    local_len, model_width = input_rows.shape
    slice_width = w_query.shape[0]
    own_len = local_len // tp_count
    block_count = fsdp_count * ctx_count
    expert_total = w_router.shape[1]
    ff_width = w_gate.shape[2]
    query_group_count = QUERY_HEADS // KEY_VALUE_HEADS
    head_width = w_query.shape[1]
    local_heads = head_width // HEAD_SIZE
    local_kv = local_heads // query_group_count
    capacity = local_len // 2
    factor = 1.0 / math.sqrt(HEAD_SIZE)
    own_start = tp_rank * own_len

    def own_rows(rows):
        return lax.dynamic_slice_in_dim(rows, own_start, own_len, 0)

    route_rows = own_rows(routes[0])
    kv_width = key_value_projection.shape[1] * 2 * HEAD_SIZE
    gains = jnp.pad(jnp.stack([attn_gain, ffn_gain]), ((0, 14), (0, 0)))
    gains = in_order(all_steps(gains, FSDP), FSDP)
    gain_one, gain_two = (gains[:, row].reshape(model_width) for row in range(2))
    packed = jnp.concatenate(
        [w_query, key_value_projection.reshape(slice_width, kv_width)], axis=1
    )
    packed_parts = all_steps(row_major(packed), FSDP)
    both_width = head_width + kv_width
    both_weight = row_major(in_order(packed_parts, FSDP).reshape(model_width, both_width))
    query_full = both_weight[:, :head_width]
    key_value_weight = both_weight[:, head_width:]
    router = jnp.pad(w_router, ((0, 0), (0, -expert_total % 128)))
    out_parts = jnp.concatenate([output_projection_weight, router], axis=1)
    out_parts = all_steps(after(out_parts, packed_parts), FSDP)
    out_full = (
        in_order([part[:, :slice_width] for part in out_parts], FSDP)
        .transpose(1, 0, 2)
        .reshape(head_width, model_width)
    )
    router_full = in_order([part[:, slice_width:] for part in out_parts], FSDP)
    router_full = router_full.reshape(model_width, router.shape[1])[:, :expert_total]

    expert_ids = jnp.arange(expert_total, dtype=jnp.int32)
    own_chosen = jnp.any(route_rows[:, :, None] == expert_ids[None, None, :], axis=1)
    route_tail = jnp.pad(own_chosen.astype(jnp.bfloat16), ((0, 0), (0, -expert_total % 256)))
    carried = jnp.concatenate([own_rows(cotangent[0]), route_tail], axis=1)
    grad_pieces = all_steps(after(carried, out_parts), FSDP)

    def weight_packet(weights, earlier):
        packets = []
        for step in range(fsdp_count):
            index = ((fsdp_rank + step) % fsdp_count) * ctx_count + ctx_rank
            packet = jnp.stack([pick_block(weight, index) for weight in weights])
            if step:
                packet = after(packet, earlier)
                packet = rotated(packet, FSDP, step)
            packets.append(packet)
        return packets

    def whole_weights(packets):
        return [
            in_order([packet[kind] for packet in packets], FSDP).reshape(
                fsdp_count * slice_width, ff_width
            )
            for kind in range(packets[0].shape[0])
        ]

    wide_input = input_rows.astype(jnp.float32)
    normed_one, factor_one, first_hidden_state = rms_forward(wide_input, gain_one)
    query_matrix = jnp.dot(
        first_hidden_state, query_full, preferred_element_type=jnp.float32
    ).reshape(local_len, local_heads, HEAD_SIZE)
    key_value_rows = jnp.dot(
        first_hidden_state, key_value_weight, preferred_element_type=jnp.float32
    ).reshape(local_len, local_kv, 2, HEAD_SIZE)
    place_rows = positions[0]
    cosine_lookup, sine_lookup = rope_tables(place_rows, HEAD_SIZE)
    rotated_query = (
        apply_rotary(query_matrix, cosine_lookup, sine_lookup, 1.0)
        .astype(jnp.bfloat16)
        .reshape(local_len, local_kv, query_group_count, HEAD_SIZE)
    )
    k_rot = apply_rotary(key_value_rows[:, :, 0], cosine_lookup, sine_lookup, 1.0).astype(
        jnp.bfloat16
    )
    v_rows = key_value_rows[:, :, 1].astype(jnp.bfloat16)
    local_ids = jnp.arange(local_len, dtype=jnp.int32)
    query_ids = ctx_rank * local_len + local_ids
    query_starts = query_ids - place_rows
    kv_pack = jnp.concatenate([k_rot, v_rows], axis=-1)
    kv_blocks = [kv_pack]
    key_ids = [query_ids]
    for step in range(1, ctx_count):
        kv_blocks.append(shifted(kv_blocks[-1], CTX, 1))
        key_ids.append((ctx_rank - step) * local_len + local_ids)
    row_total = jnp.zeros((local_kv, query_group_count, local_len), jnp.float32)
    weighted = jnp.zeros((local_kv, query_group_count, local_len, HEAD_SIZE), jnp.float32)
    masks = []
    for block_index in range(ctx_count):
        allowed = attend_mask(query_ids, query_starts, key_ids[block_index])
        masks.append(allowed)
        key_rows = kv_blocks[block_index][..., :HEAD_SIZE]
        value_rows = kv_blocks[block_index][..., HEAD_SIZE:]
        scores = (
            jnp.einsum(
                TKGD_SKD_TO_KGTS, rotated_query, key_rows, preferred_element_type=jnp.float32
            )
            * factor
        )
        exp_scores = jnp.where(allowed[None, None], jnp.exp(scores), 0.0)
        row_total = row_total + jnp.sum(exp_scores, axis=-1)
        weighted = weighted + jnp.einsum(
            KGTS_SKD_TO_KGTD,
            exp_scores.astype(jnp.bfloat16),
            value_rows,
            preferred_element_type=jnp.float32,
        )
    head_out = (weighted / row_total[..., None]).astype(jnp.bfloat16)
    flat_heads = head_out.transpose(2, 0, 1, 3).reshape(local_len, local_heads * HEAD_SIZE)
    attn_part = jnp.dot(flat_heads, out_full, preferred_element_type=jnp.float32)

    attn_total = sum_over_tp(attn_part)
    residual = own_rows(input_rows).astype(jnp.float32) + attn_total
    normed_two, factor_two, hidden_two = rms_forward(residual, gain_two)
    hidden_pieces = all_steps(hidden_two, FSDP)
    grad_halves = [
        half.reshape(block_count, local_len, half.shape[-1])
        for half in spread(grad_pieces)
    ]
    hidden_halves = [
        half.reshape(block_count, local_len, half.shape[-1])
        for half in spread(hidden_pieces)
    ]
    tail_start = grad_halves[1].shape[-1] - route_tail.shape[1]
    chosen_all = grad_halves[1][:, :, tail_start : tail_start + expert_total]
    own_expert = tp_rank * block_count + fsdp_rank * ctx_count + ctx_rank
    member = jnp.any((expert_ids == own_expert) & (chosen_all > 0), axis=2)
    places = jnp.cumsum(member.astype(jnp.int32), axis=1) - 1
    slots = jnp.where(member, places, capacity)
    slot_ids = jnp.arange(capacity, dtype=jnp.int32)
    hot = slots[:, None, :] == slot_ids[None, :, None]
    hot_b = hot.astype(jnp.bfloat16)

    def take_rows(rows):
        return (
            jnp.einsum("bst,btd->bsd", hot_b, rows, preferred_element_type=jnp.float32)
            .astype(jnp.bfloat16)
            .reshape(block_count * capacity, rows.shape[2])
        )

    grad_rows = jnp.concatenate([take_rows(half) for half in grad_halves], axis=1)
    slot_chosen = grad_rows[:, model_width : model_width + expert_total].astype(jnp.float32)

    def put_rows(rows):
        stacked = rows.reshape(block_count, capacity, rows.shape[1])
        return (
            jnp.einsum("bst,bsd->btd", hot_b, stacked, preferred_element_type=jnp.float32)
            .astype(jnp.bfloat16)
            .reshape(
                (fsdp_count, ctx_count)
                + (2,) * len(tp_stages())
                + (own_len, rows.shape[1])
            )
        )

    first_packets = weight_packet((w_gate, w_up), hidden_pieces)
    down_packets = weight_packet((w_down,), hidden_pieces)
    hidden_halves, first_packets, down_packets = lax.optimization_barrier(
        (hidden_halves, first_packets, down_packets)
    )
    gate_weight, up_weight = whole_weights(first_packets)
    (down_weight,) = whole_weights(down_packets)

    def exp_logits(hidden, chosen):
        logits = jnp.dot(hidden, router_full, preferred_element_type=jnp.float32)
        return jnp.where(chosen, jnp.exp(logits), 0.0)

    own_exp = exp_logits(hidden_two, own_chosen)
    own_gates = own_exp / jnp.sum(own_exp, axis=-1, keepdims=True)

    picked = jnp.concatenate([take_rows(half) for half in hidden_halves], axis=1)
    slot_exp = exp_logits(picked, slot_chosen > 0)
    slot_live = jnp.sum(slot_chosen, axis=1) > 0
    slot_total = jnp.where(slot_live, jnp.sum(slot_exp, axis=1), 1.0)
    slot_own = jnp.sum(jnp.where(expert_ids[None, :] == own_expert, slot_exp, 0.0), axis=1)
    scaled = jnp.where(slot_live, slot_own / slot_total, 0.0)
    gate_pre = jnp.dot(picked, gate_weight, preferred_element_type=jnp.float32)
    up_pre = jnp.dot(picked, up_weight, preferred_element_type=jnp.float32)
    activation = (jax.nn.silu(gate_pre) * up_pre).astype(jnp.bfloat16)
    result = jnp.einsum(CF_DF_TO_CD, activation, down_weight, preferred_element_type=jnp.float32)

    mixture_rows = (result * scaled[:, None]).astype(jnp.bfloat16)

    grad_rows = grad_rows[:, :model_width]
    grad_wide_rows = grad_rows.astype(jnp.float32)
    slot_grad = jnp.sum(grad_wide_rows * result, axis=1).reshape(block_count, capacity)
    out_grad = row_major((grad_wide_rows * scaled[:, None]).astype(jnp.bfloat16))
    act_grad = jnp.dot(out_grad, down_weight, preferred_element_type=jnp.float32)
    sigmoid_gate = jax.nn.sigmoid(gate_pre)
    gate_pre_grad = (
        act_grad * up_pre * sigmoid_gate * (1.0 + gate_pre * (1.0 - sigmoid_gate))
    ).astype(jnp.bfloat16)
    up_pre_grad = (act_grad * gate_pre * sigmoid_gate).astype(jnp.bfloat16)
    picked_grad = jnp.einsum(
        CF_DF_TO_CD, gate_pre_grad, gate_weight, preferred_element_type=jnp.float32
    ) + jnp.einsum(CF_DF_TO_CD, up_pre_grad, up_weight, preferred_element_type=jnp.float32)
    gate_grad_part = jnp.sum(jnp.where(hot, slot_grad[:, :, None], 0.0), axis=1)
    gate_grad = lax.all_to_all(
        gate_grad_part.reshape(block_count * tp_count, own_len), everywhere, 0, 0, tiled=True
    )
    gate_grad = (
        gate_grad.reshape(block_count, tp_count, own_len)
        .transpose(2, 1, 0)
        .reshape(own_len, expert_total)
    )
    back_parts = [put_rows(half) for half in halves(picked_grad.astype(jnp.bfloat16))]
    back_parts, picked, gate_pre_grad, up_pre_grad, out_grad, activation = (
        lax.optimization_barrier(
            (back_parts, picked, gate_pre_grad, up_pre_grad, out_grad, activation)
        )
    )
    mixture = collect([put_rows(half) for half in halves(mixture_rows)])
    own_out = (residual + mixture).astype(jnp.bfloat16)
    hidden_grad_sum = collect(back_parts)

    def weight_grad(rows, columns):
        return (
            jnp.einsum("cd,cf->df", rows, columns, preferred_element_type=jnp.float32)
            .astype(jnp.bfloat16)
            .reshape(fsdp_count, slice_width, ff_width)
        )

    early_grads = [weight_grad(picked, rows) for rows in (gate_pre_grad, up_pre_grad)]
    late_grads = [weight_grad(out_grad, activation)]
    grad_packets = []
    for kinds in (early_grads, late_grads):
        packets = []
        for step in range(fsdp_count):
            target = (fsdp_rank + step) % fsdp_count
            packet = jnp.stack([pick_block(grad, target) for grad in kinds])
            if step:
                if len(grad_packets):
                    packet = after(packet, hidden_grad_sum)
                packet = rotated(packet, FSDP, step)
            packets.append(packet)
        grad_packets.append(packets)

    sel_grad = own_gates * (
        gate_grad - jnp.sum(own_gates * gate_grad, axis=-1, keepdims=True)
    )
    logit_grad = jnp.where(own_chosen, sel_grad, 0.0).astype(jnp.bfloat16)
    hidden_grad = hidden_grad_sum + jnp.einsum(
        TE_DE_TO_TD, logit_grad, router_full, preferred_element_type=jnp.float32
    )
    back_two, grad_ffn_gain = rms_backward(hidden_grad, normed_two, factor_two, gain_two)
    residual_grad = own_rows(cotangent[0]).astype(jnp.float32) + back_two
    row_pad = 16
    sent = jnp.concatenate(
        [
            residual_grad.astype(jnp.bfloat16),
            jnp.pad(grad_ffn_gain.astype(jnp.bfloat16)[None], ((0, row_pad - 1), (0, 0))),
        ],
        axis=0,
    )
    logit_tail = jnp.pad(logit_grad, ((0, row_pad), (0, -expert_total % 128)))
    sent = lax.all_gather(jnp.concatenate([sent, logit_tail], axis=1), TP, axis=0)
    residual_gradient_second = sent[:, :own_len, :model_width].reshape(local_len, model_width)
    logit_grad = sent[:, :own_len, model_width : model_width + expert_total].reshape(
        local_len, expert_total
    )
    grad_ffn_gain = jnp.sum(sent[:, own_len, :model_width].astype(jnp.float32), axis=0)
    own_block = fsdp_rank * ctx_count + ctx_rank
    block_hidden = jnp.concatenate(
        [pick_block(half, own_block) for half in hidden_halves], axis=1
    )
    grad_router = jnp.einsum(
        TD_TE_TO_DE, block_hidden, logit_grad, preferred_element_type=jnp.float32
    )

    grad_out_proj = jnp.einsum(
        "td,ti->di", residual_gradient_second, flat_heads, preferred_element_type=jnp.float32
    )
    early = jnp.concatenate([grad_out_proj, grad_router, grad_ffn_gain[:, None]], axis=1)
    early = jnp.pad(early, ((0, 0), (0, -early.shape[1] % 128))).astype(jnp.bfloat16)
    early = early.reshape(fsdp_count, slice_width, early.shape[1])
    early_parts = scatter_start(early)
    per_head_gradient = jnp.einsum(
        TD_ID_TO_TI, residual_gradient_second, out_full, preferred_element_type=jnp.float32
    ).astype(jnp.bfloat16)
    per_head_gradient = per_head_gradient.reshape(
        local_len, local_kv, query_group_count, HEAD_SIZE
    ).transpose(1, 2, 0, 3)
    row_delta = jnp.sum(
        per_head_gradient.astype(jnp.float32) * head_out.astype(jnp.float32), axis=-1
    )
    log_total = jnp.log(row_total)
    query_grad = jnp.zeros((local_len, local_kv, query_group_count, HEAD_SIZE), jnp.float32)
    kv_grads = []
    for block_index in range(ctx_count):
        key_rows = kv_blocks[block_index][..., :HEAD_SIZE]
        value_rows = kv_blocks[block_index][..., HEAD_SIZE:]
        scores = (
            jnp.einsum(
                TKGD_SKD_TO_KGTS, rotated_query, key_rows, preferred_element_type=jnp.float32
            )
            * factor
        )
        probability = jnp.where(
            masks[block_index][None, None], jnp.exp(scores - log_total[..., None]), 0.0
        )
        prob_grad = jnp.einsum(
            KGTD_SKD_TO_KGTS, per_head_gradient, value_rows, preferred_element_type=jnp.float32
        )
        score_grad = (probability * (prob_grad - row_delta[..., None]) * factor).astype(
            jnp.bfloat16
        )
        query_grad = query_grad + jnp.einsum(
            KGTS_SKD_TO_TKGD, score_grad, key_rows, preferred_element_type=jnp.float32
        )
        key_grad = jnp.einsum(
            KGTS_TKGD_TO_SKD, score_grad, rotated_query, preferred_element_type=jnp.float32
        )
        value_gradient = jnp.einsum(
            KGTS_KGTD_TO_SKD,
            probability.astype(jnp.bfloat16),
            per_head_gradient,
            preferred_element_type=jnp.float32,
        )
        kv_grads.append(jnp.concatenate([key_grad, value_gradient], axis=-1))
    weight_hops = []
    for step in range(fsdp_count):
        early_hops = all_steps(grad_packets[0][step], CTX)
        late_hops = all_steps(grad_packets[1][step], CTX)
        weight_hops.append((early_hops, late_hops))
    kv_grad_total = kv_grads[0]
    for step in range(1, ctx_count):
        returning = shifted(kv_grads[step].astype(jnp.bfloat16), CTX, -step)
        kv_grad_total = kv_grad_total + returning.astype(jnp.float32)
    key_backward_rows = apply_rotary(
        kv_grad_total[..., :HEAD_SIZE], cosine_lookup, sine_lookup, -1.0
    )
    key_value_backward = (
        jnp.stack([key_backward_rows, kv_grad_total[..., HEAD_SIZE:]], axis=2)
        .astype(jnp.bfloat16)
        .reshape(local_len, kv_width)
    )
    query_back = (
        apply_rotary(
            query_grad.reshape(local_len, local_heads, HEAD_SIZE), cosine_lookup, sine_lookup, -1.0
        )
        .astype(jnp.bfloat16)
        .reshape(local_len, head_width)
    )
    both_back = jnp.concatenate([query_back, key_value_backward], axis=1)
    hidden_one_part = jnp.einsum(
        TF_DF_TO_TD, both_back, both_weight, preferred_element_type=jnp.float32
    )
    grad_attn_gain = jnp.sum(hidden_one_part * normed_one, axis=0)
    projection_grad = jnp.einsum(
        TD_TF_TO_DF, first_hidden_state, both_back, preferred_element_type=jnp.float32
    )
    projection_grad = projection_grad.astype(jnp.bfloat16).reshape(
        fsdp_count, slice_width, both_width
    )
    projection_parts = scatter_start(projection_grad)
    summed = sum_over_tp(hidden_one_part, grad_attn_gain)
    hidden_one_grad = summed[:own_len]
    grad_attn_gain = summed[own_len].astype(jnp.bfloat16).reshape(fsdp_count, 1, slice_width)
    gain_parts = scatter_start(grad_attn_gain)
    back_one, _ = rms_backward(
        hidden_one_grad, own_rows(normed_one), own_rows(factor_one), gain_one
    )
    input_grad = (residual_grad + back_one).astype(jnp.bfloat16)
    input_grad = lax.all_gather(input_grad, TP, axis=0, tiled=True)
    out_rows = lax.all_gather(after(own_out, input_grad), TP, axis=0, tiled=True)
    grad_attn_gain = scatter_finish(after(gain_parts, out_rows))[0]
    early_total = scatter_finish(after(early_parts, out_rows))
    projection_total = scatter_finish(after(projection_parts, out_rows))
    hop_places = jnp.stack(
        [
            (fsdp_rank - step) % fsdp_count * ctx_count + (ctx_rank - hop) % ctx_count
            for step in range(fsdp_count)
            for hop in range(ctx_count)
        ]
    ).astype(jnp.int32)
    weight_outs = assemble(
        after([seen for hops, _ in weight_hops for seen in hops], out_rows), hop_places
    ) + assemble(
        after([seen for _, hops in weight_hops for seen in hops], out_rows), hop_places
    )
    return (
        out_rows[None],
        input_grad.astype(jnp.float32)[None],
        grad_attn_gain,
        projection_total[:, :head_width],
        projection_total[:, head_width:].reshape(key_value_projection.shape),
        early_total[:, :head_width].T,
        early_total[:, head_width + expert_total],
        early_total[:, head_width : head_width + expert_total],
        weight_outs[0],
        weight_outs[1],
        weight_outs[2],
    )


def local_any(*args):
    devices = math.prod(lax.axis_size(name) for name in (FSDP, CTX, TP))
    if args[9].shape[1] != devices:
        return local(*args)
    return local_spread(*args)


def solution(mesh):

    return jax.shard_map(
        local_any,
        mesh=mesh,
        in_specs=(
            P(FSDP, CTX, None),
            P(FSDP, CTX, None),
            P(FSDP, CTX),
            P(FSDP, CTX, None),
            P(FSDP),
            P(FSDP, TP),
            P(FSDP, TP, None, None),
            P(TP, FSDP),
            P(FSDP),
            P(FSDP, None),
            P(TP, FSDP, None),
            P(TP, FSDP, None),
            P(TP, FSDP, None),
        ),
        out_specs=(
            P(FSDP, CTX, None),
            P(FSDP, CTX, None),
            P(FSDP),
            P(FSDP, TP),
            P(FSDP, TP, None, None),
            P(TP, FSDP),
            P(FSDP),
            P(FSDP, None),
            P(TP, FSDP, None),
            P(TP, FSDP, None),
            P(TP, FSDP, None),
        ),
        check_vma=False,
    )
```
